256 devices in a mesh: ax: 64 (over y_lo, z, x), sec: 4 (over y_hi, core).
Axes of the slice: x: 4, y: 4 (y_hi: 2, y_lo: 2; y = y_hi * 2 + y_lo), z: 8, core: 2. Of those that a mesh axis runs over, the one named last changes fastest.
Arguments:
- load: float32 [8192, 6, 1024], P('ax', None, 'sec'), may hold values from -6 to 6
- disp: float32 [8192, 6, 1024], P('ax', None, 'sec'), may hold values from -1.5 to 1.5
- stiff: float32 [8192, 6, 1024], P('ax', None, 'sec'), may hold values from 0.5 to 2
- hole: int32 [8192, 1024], P('ax', 'sec'), may hold values 0 or 1
- section_class: int32 [8192], P('ax'), may hold values from 0 to 3
- class_table: float32 [4, 6], replicated, may hold values from 0.5 to 2
- precond: float32 [6, 6, 1024], replicated, may hold values from -0.5 to 0.5, as said below
Outputs:
- disp_new: float32 [8192, 6, 1024], P('ax', None, 'sec')
- residual_new: float32 [8192, 6, 1024], P('ax', None, 'sec')
- stats: float32 [3], replicated
The draws below stay inside these ranges and needn't reach their ends.
Inputs may be any that keep to these rules, and one draw needn't show every extreme that they name: `precond`: for each harmonic the matrix over the first two dimensions is symmetric and positive definite.
All inputs are finite; a program needn't handle non-finite values. No bound on the sum of `hole` on one device may be relied on, other than what follows from the above.
Results may differ from the reference program's by a relative error of at most 0.0075.
Values sent between devices are 32-bit elements; how exact they have to be, the bound alone decides.
A program may use at most 64 MiB of HBM per device.

```python
import math
import jax
import jax.numpy as jnp
from jax import lax

CH = 3
RAD = 2
NC = 1024
CLASSES = 4
CA = 128
NA = 8192
N_AX = 64


def draw_precond(key, part):
    key_diag = jax.random.fold_in(key, 11)
    key_mix = jax.random.fold_in(key, 23)
    harmonic = jnp.arange(NC).astype(jnp.float32)
    symbol = 5.5 + 4.0 * jnp.sin(math.pi * harmonic / NC) ** 2
    rough = jnp.exp(jax.random.uniform(key_diag, (CH * RAD, NC), jnp.float32, math.log(0.5), math.log(2.0)))
    diagonal = rough / symbol[None, :]
    mixing = jax.random.uniform(key_mix, (CH * RAD, CH * RAD, NC), jnp.float32, -1.0, 1.0)
    mixing = 0.5 * (mixing + jnp.transpose(mixing, (1, 0, 2)))
    bound_pair = jnp.minimum(diagonal[:, None, :], diagonal[None, :, :])
    identity = jnp.eye(CH * RAD, dtype=jnp.float32)[:, :, None]
    return (1.0 - identity) * 0.18 * bound_pair * mixing + identity * diagonal[:, None, :]


def with_ends(values, stream_key, smallest, top_value):
    shape = values.shape
    spot = [jax.random.randint(jax.random.fold_in(stream_key, axis), (), 0, shape[axis]) for axis in range(len(shape))]
    values = values.at[tuple(spot)].set(smallest)
    longest = shape.index(max(shape))
    spot[longest] = (spot[longest] + 1) % shape[longest]
    return values.at[tuple(spot)].set(top_value)


def shard_levels(rng, shape, split, smallest, high):
    def one(dim, shards_of):
        heights = jax.random.uniform(jax.random.fold_in(jax.random.fold_in(rng, 6), dim), (shards_of,), jnp.float32, smallest / len(split), high / len(split))
        return jnp.repeat(jnp.exp(heights), shape[dim] // shards_of).reshape((-1,) + (1,) * (len(shape) - dim - 1))

    level = one(*split[0])
    for cut in split[1:]:
        level = level * one(*cut)
    return level


def gaussian(stream_key, shape, scale, limit, cuts=(), kind=jnp.bfloat16):
    entries = jax.random.normal(stream_key, shape, jnp.float32) * scale
    if len(cuts) > 0:
        entries = shard_levels(stream_key, shape, cuts, -0.22, 0.18) * entries
    return jnp.clip(entries, min=-limit, max=limit).astype(kind)


def setup_inputs(seed: int = 0) -> dict:
    key_list = jax.random.split(jax.random.key(seed), 8)
    load = gaussian(key_list[0], (NA, CH * RAD, NC), 1.0, 6.0, ((0, 64), (2, 4)), jnp.float32)
    disp = gaussian(key_list[1], (NA, CH * RAD, NC), 0.25, 1.5, ((0, 64), (2, 4)), jnp.float32)
    stiff = jnp.clip(jnp.exp(math.log(2.0) - 1.3862944 * jax.random.uniform(key_list[2], (NA, CH * RAD, NC), jnp.float32) ** shard_levels(key_list[2], (NA, CH * RAD, NC), ((0, 64), (2, 4)), -0.2, 0.2)), 0.5, 2.0)
    hole = with_ends((jax.random.randint(key_list[3], (NA, NC), 0, 16) < 1).astype(jnp.int32), jax.random.fold_in(key_list[3], 1), 0, 1)
    section_class = with_ends(jax.random.randint(key_list[4], (NA,), 0, CLASSES), jax.random.fold_in(key_list[4], 1), 0, CLASSES - 1).astype(jnp.int32)
    class_table = jnp.clip(jnp.exp(jax.random.uniform(key_list[5], (CLASSES, CH * RAD), jnp.float32, math.log(0.5), math.log(2.0))), 0.5, 2.0)
    precond = draw_precond(jax.random.fold_in(key_list[7], 71), 0)
    return {"load": load, "disp": disp, "stiff": stiff, "hole": hole, "section_class": section_class, "class_table": class_table, "precond": precond}


def swap_radial(field):
    extent = field.shape
    folded = field.reshape(extent[0], extent[1] // 2, 2, extent[2])
    return jnp.flip(folded, axis=2).reshape(extent)


def operate(field, stiffness):
    padded = jnp.pad(field, ((1, 1), (0, 0), (0, 0)))
    beside = padded[2:] + padded[:-2]
    beside = beside + jnp.roll(field, 1, axis=2) + jnp.roll(field, -1, axis=2)
    return (stiffness + 4.5) * field - beside - 0.5 * swap_radial(field)


def reference(load, disp, stiff, hole, section_class, class_table, precond):
    position = jnp.arange(NA).astype(jnp.float32)
    taper = 1.0 + 2.0 * position / (NA - 1)
    stiffness = stiff * (class_table[section_class] * taper[:, None])[:, :, None]
    solid = (1 - hole).astype(jnp.float32)[:, None, :]
    residual = solid * (load - operate(disp, stiffness))

    def transform(block):
        spectrum = jnp.fft.fft(block, axis=2)
        cos_part = jnp.einsum("qpk,apk->aqk", precond, spectrum.real, precision=lax.Precision.HIGHEST)
        sin_part = jnp.einsum("qpk,apk->aqk", precond, -spectrum.imag, precision=lax.Precision.HIGHEST)
        return jnp.fft.ifft(lax.complex(cos_part, -sin_part), axis=2).real

    blocks = residual.reshape(N_AX, CA, CH * RAD, NC)
    smoothed = lax.map(transform, blocks).reshape(NA, CH * RAD, NC)
    prec = solid * smoothed
    image = solid * operate(prec, stiffness)
    cell_total = NA * CH * RAD * NC
    inner_rz = jnp.sum(residual * prec) / cell_total
    inner_zq = jnp.sum(prec * image) / cell_total
    alpha = inner_rz / inner_zq
    disp_new = disp + alpha * prec
    residual_new = residual - alpha * image
    square_new = jnp.sum(residual_new * residual_new) / cell_total
    return disp_new, residual_new, jnp.stack([inner_rz, inner_zq, square_new])
```

```python
import math

import jax
import jax.numpy as jnp
from jax import lax
from jax.experimental import pallas as pl
from jax.experimental.pallas import tpu as pltpu
from jax.sharding import PartitionSpec as P


MESH = pl.DeviceIdType.MESH


def _lines():
    me_ax = lax.axis_index("ax")
    me_sec = lax.axis_index("sec")
    x = me_ax % 4
    z = (me_ax // 4) % 8
    ylo = me_ax // 32
    core = me_sec % 2
    yhi = me_sec // 2
    y = yhi * 2 + ylo
    return [
        (2, core, lambda c: (me_ax, yhi * 2 + c)),
        (4, x, lambda c: (me_ax - x + c, me_sec)),
        (4, y, lambda c: (me_ax - ylo * 32 + (c % 2) * 32, (c // 2) * 2 + core)),
        (8, z, lambda c: (me_ax - z * 4 + c * 4, me_sec)),
    ]


def _ar_kernel(x_ref, o_ref, r0, r1, r2, r3, own, send_sems, recv_sems):
    recvs = (r0, r1, r2, r3)
    lines = _lines()
    for r in recvs:
        r[...] = jnp.zeros_like(r)
    barrier = pltpu.get_barrier_semaphore()
    count = 0
    for n, mine, dev in lines:
        for d in range(1, n):
            pl.semaphore_signal(barrier, inc=1, device_id=dev((mine + d) % n), device_id_type=MESH)
            count += 1
    pl.semaphore_wait(barrier, count)
    src = x_ref
    base = 0
    for r, (n, mine, dev) in enumerate(lines):
        copies = []
        for d in range(1, n):
            cp = pltpu.make_async_remote_copy(
                src_ref=src,
                dst_ref=recvs[r].at[mine],
                send_sem=send_sems.at[base + d],
                recv_sem=recv_sems.at[base + d],
                device_id=dev((mine + d) % n),
                device_id_type=MESH,
            )
            cp.start()
            copies.append(cp)
        mine_val = src[...]
        for cp in copies:
            cp.wait_recv()
        total = None
        for c in range(n):
            v = jnp.where(mine == c, mine_val, recvs[r][c])
            total = v if total is None else total + v
        for cp in copies:
            cp.wait_send()
        base += n
        if r + 1 < len(lines):
            own[r] = total
            src = own.at[r]
        else:
            o_ref[...] = total


def all_sum(part, cid):
    return pl.pallas_call(
        _ar_kernel,
        out_shape=jax.ShapeDtypeStruct(part.shape, jnp.float32),
        in_specs=[pl.BlockSpec(memory_space=pltpu.VMEM)],
        out_specs=pl.BlockSpec(memory_space=pltpu.VMEM),
        scratch_shapes=[
            pltpu.VMEM((2,) + part.shape, jnp.float32),
            pltpu.VMEM((4,) + part.shape, jnp.float32),
            pltpu.VMEM((4,) + part.shape, jnp.float32),
            pltpu.VMEM((8,) + part.shape, jnp.float32),
            pltpu.VMEM((3,) + part.shape, jnp.float32),
            pltpu.SemaphoreType.DMA((18,)),
            pltpu.SemaphoreType.DMA((18,)),
        ],
        compiler_params=pltpu.CompilerParams(collective_id=cid, has_side_effects=True),
    )(part)


def with_halo(x, sides, width, wrap):
    for axis, dim in sides:
        size, length = (lax.axis_size(axis), x.shape[dim])
        up = [(i, (i + 1) % size) for i in range(size if wrap else size - 1)]
        down = [(j, i) for i, j in up]
        last = lax.slice_in_dim(x, length - width, length, axis=dim)
        first = lax.slice_in_dim(x, 0, width, axis=dim)
        before = lax.ppermute(last, axis, up)
        after = lax.ppermute(first, axis, down)
        x = jnp.concatenate([before, x, after], axis=dim)
    return x


def swap_radial(field):
    extent = field.shape
    folded = field.reshape(extent[0], extent[1] // 2, 2, extent[2])
    return jnp.flip(folded, axis=2).reshape(extent)


def apply_operator(field, stiffness):
    axial_pad = with_halo(field, (("ax", 0),), 1, False)
    sector_pad = with_halo(field, (("sec", 2),), 1, True)
    beside = axial_pad[2:] + axial_pad[:-2]
    beside = beside + sector_pad[:, :, 2:] + sector_pad[:, :, :-2]
    return (stiffness + 4.5) * field - beside - 0.5 * swap_radial(field)


def harmonic_table(row_index, col_index, length):
    product = row_index[:, None] * col_index[None, :] % length
    angle = 2.0 * math.pi / length * product.astype(jnp.float32)
    return jnp.concatenate([jnp.cos(angle), jnp.sin(angle)], axis=1)


def scale_harmonics(block_inverse, spectrum):
    doubled = jnp.concatenate([block_inverse, block_inverse], axis=2)
    return jnp.sum(doubled[None] * spectrum[:, None], axis=2)


def shards(load, disp, stiff, hole, section_class, class_table, precond):
    slab_count, comp_count, sector_width = disp.shape
    sector_count = lax.axis_size("sec")
    around_cells = sector_width * sector_count
    total_axial = slab_count * lax.axis_size("ax")
    position = lax.axis_index("ax") * slab_count + jnp.arange(slab_count)
    taper = 1.0 + 2.0 * position.astype(jnp.float32) / (total_axial - 1)
    one_hot = (section_class[:, None] == jnp.arange(class_table.shape[0])[None, :]).astype(
        jnp.float32
    )
    factors = jnp.dot(one_hot, class_table, precision=lax.Precision.HIGHEST)
    stiffness = stiff * (factors * taper[:, None])[:, :, None]
    solid = (1 - hole).astype(jnp.float32)[:, None, :]
    residual = solid * (load - apply_operator(disp, stiffness))
    sector = lax.axis_index("sec")
    own_index = sector * sector_width + jnp.arange(sector_width)
    table = harmonic_table(jnp.arange(around_cells), own_index, around_cells)
    own_inverse = lax.dynamic_slice_in_dim(precond, sector * sector_width, sector_width, 2)
    initial = jnp.zeros((slab_count, comp_count, 2 * sector_width), jnp.float32)
    piece = lax.all_gather(residual, "sec", axis=2, tiled=True)
    span = piece.shape[2]
    table_rows = table
    flat = piece.reshape(-1, span)
    spectrum = jnp.dot(flat, table_rows, precision=lax.Precision.HIGHEST).reshape(initial.shape)
    scaled = scale_harmonics(own_inverse, spectrum).reshape(-1, 2 * sector_width)
    table_rows = table
    shares = lax.psum_scatter(
        lax.dot_general(
            table_rows, scaled, (((1,), (1,)), ((), ())), precision=lax.Precision.HIGHEST
        )
        / around_cells,
        "sec",
        scatter_dimension=0,
        tiled=True,
    )
    smoothed = shares.T.reshape(slab_count, comp_count, sector_width)
    prec = solid * smoothed
    image = solid * apply_operator(prec, stiffness)
    cell_total = slab_count * lax.axis_size("ax") * comp_count * around_cells
    parts = jnp.stack(
        [
            jnp.sum(residual * prec),
            jnp.sum(prec * image),
            jnp.sum(residual * residual),
            jnp.sum(residual * image),
            jnp.sum(image * image),
        ]
    )
    packed = jnp.zeros((8, 128), jnp.float32).at[0, :5].set(parts)
    totals = all_sum(packed, 0)[0]
    inner_rz = totals[0] / cell_total
    inner_zq = totals[1] / cell_total
    alpha = inner_rz / inner_zq
    residual_new = residual - alpha * image
    square_new = (totals[2] - alpha * (2.0 * totals[3] - alpha * totals[4])) / cell_total
    disp_new = disp + alpha * prec
    return (disp_new, residual_new, jnp.stack([inner_rz, inner_zq, square_new]))


def solution(mesh):
    in_specs = (
        P("ax", None, "sec"),
        P("ax", None, "sec"),
        P("ax", None, "sec"),
        P("ax", "sec"),
        P("ax"),
        P(),
        P(),
    )
    out_specs = (P("ax", None, "sec"), P("ax", None, "sec"), P())
    return jax.shard_map(shards, mesh=mesh, in_specs=in_specs, out_specs=out_specs, check_vma=False)
```

```python
import functools
import math

import jax
import jax.numpy as jnp
from jax import lax
from jax.experimental import pallas as pl
from jax.experimental.pallas import tpu as pltpu
from jax.sharding import PartitionSpec as P


MESH = pl.DeviceIdType.MESH


def _lines():
    me_ax = lax.axis_index("ax")
    me_sec = lax.axis_index("sec")
    x = me_ax % 4
    z = (me_ax // 4) % 8
    ylo = me_ax // 32
    core = me_sec % 2
    yhi = me_sec // 2
    y = yhi * 2 + ylo
    return [
        (2, core, lambda c: (me_ax, yhi * 2 + c)),
        (4, x, lambda c: (me_ax - x + c, me_sec)),
        (4, y, lambda c: (me_ax - ylo * 32 + (c % 2) * 32, (c // 2) * 2 + core)),
        (8, z, lambda c: (me_ax - z * 4 + c * 4, me_sec)),
    ]


def _ar_kernel(x_ref, o_ref, r0, r1, r2, r3, own, send_sems, recv_sems):
    recvs = (r0, r1, r2, r3)
    lines = _lines()
    for r in recvs:
        r[...] = jnp.zeros_like(r)
    barrier = pltpu.get_barrier_semaphore()
    count = 0
    for n, mine, dev in lines:
        for d in range(1, n):
            pl.semaphore_signal(barrier, inc=1, device_id=dev((mine + d) % n), device_id_type=MESH)
            count += 1
    pl.semaphore_wait(barrier, count)
    src = x_ref
    base = 0
    for r, (n, mine, dev) in enumerate(lines):
        copies = []
        for d in range(1, n):
            cp = pltpu.make_async_remote_copy(
                src_ref=src,
                dst_ref=recvs[r].at[mine],
                send_sem=send_sems.at[base + d],
                recv_sem=recv_sems.at[base + d],
                device_id=dev((mine + d) % n),
                device_id_type=MESH,
            )
            cp.start()
            copies.append(cp)
        mine_val = src[...]
        for cp in copies:
            cp.wait_recv()
        total = None
        for c in range(n):
            v = jnp.where(mine == c, mine_val, recvs[r][c])
            total = v if total is None else total + v
        for cp in copies:
            cp.wait_send()
        base += n
        if r + 1 < len(lines):
            own[r] = total
            src = own.at[r]
        else:
            o_ref[...] = total


def all_sum(part, cid):
    return pl.pallas_call(
        _ar_kernel,
        out_shape=jax.ShapeDtypeStruct(part.shape, jnp.float32),
        in_specs=[pl.BlockSpec(memory_space=pltpu.VMEM)],
        out_specs=pl.BlockSpec(memory_space=pltpu.VMEM),
        scratch_shapes=[
            pltpu.VMEM((2,) + part.shape, jnp.float32),
            pltpu.VMEM((4,) + part.shape, jnp.float32),
            pltpu.VMEM((4,) + part.shape, jnp.float32),
            pltpu.VMEM((8,) + part.shape, jnp.float32),
            pltpu.VMEM((3,) + part.shape, jnp.float32),
            pltpu.SemaphoreType.DMA((18,)),
            pltpu.SemaphoreType.DMA((18,)),
        ],
        compiler_params=pltpu.CompilerParams(collective_id=cid, has_side_effects=True),
    )(part)


def _to_lines_kernel(n, x_ref, o_ref, send_sems, recv_sems, local_sem):
    me = lax.axis_index("sec")
    ax = lax.axis_index("ax")
    rows, width = o_ref.shape[1], x_ref.shape[2]
    barrier = pltpu.get_barrier_semaphore()
    for d in range(1, n):
        pl.semaphore_signal(barrier, inc=1, device_id=(ax, (me + d) % n), device_id_type=MESH)
    pl.semaphore_wait(barrier, n - 1)
    dst = o_ref.at[:, :, pl.ds(pl.multiple_of(me * width, width), width)]
    copies = []
    for d in range(1, n):
        peer = (me + d) % n
        cp = pltpu.make_async_remote_copy(
            src_ref=x_ref.at[:, pl.ds(pl.multiple_of(peer * rows, rows), rows), :],
            dst_ref=dst,
            send_sem=send_sems.at[d],
            recv_sem=recv_sems.at[d],
            device_id=(ax, peer),
            device_id_type=MESH,
        )
        cp.start()
        copies.append(cp)
    local = pltpu.make_async_copy(
        x_ref.at[:, pl.ds(pl.multiple_of(me * rows, rows), rows), :], dst, local_sem
    )
    local.start()
    local.wait()
    for cp in copies:
        cp.wait()


def _from_lines_kernel(n, x_ref, o_ref, send_sems, recv_sems, local_sem):
    me = lax.axis_index("sec")
    ax = lax.axis_index("ax")
    rows, width = x_ref.shape[1], o_ref.shape[2]
    barrier = pltpu.get_barrier_semaphore()
    for d in range(1, n):
        pl.semaphore_signal(barrier, inc=1, device_id=(ax, (me + d) % n), device_id_type=MESH)
    pl.semaphore_wait(barrier, n - 1)
    dst = o_ref.at[:, pl.ds(pl.multiple_of(me * rows, rows), rows), :]
    copies = []
    for d in range(1, n):
        peer = (me + d) % n
        cp = pltpu.make_async_remote_copy(
            src_ref=x_ref.at[:, :, pl.ds(pl.multiple_of(peer * width, width), width)],
            dst_ref=dst,
            send_sem=send_sems.at[d],
            recv_sem=recv_sems.at[d],
            device_id=(ax, peer),
            device_id_type=MESH,
        )
        cp.start()
        copies.append(cp)
    local = pltpu.make_async_copy(
        x_ref.at[:, :, pl.ds(pl.multiple_of(me * width, width), width)], dst, local_sem
    )
    local.start()
    local.wait()
    for cp in copies:
        cp.wait()


def _exchange(body, out_shape, cid, n, x):
    return pl.pallas_call(
        functools.partial(body, n),
        out_shape=jax.ShapeDtypeStruct(out_shape, x.dtype),
        in_specs=[pl.BlockSpec(memory_space=pltpu.VMEM)],
        out_specs=pl.BlockSpec(memory_space=pltpu.VMEM),
        scratch_shapes=[
            pltpu.SemaphoreType.DMA((n,)),
            pltpu.SemaphoreType.DMA((n,)),
            pltpu.SemaphoreType.DMA,
        ],
        compiler_params=pltpu.CompilerParams(collective_id=cid, has_side_effects=True),
    )(x)


def to_lines(x, n):
    comps, rows, width = x.shape
    return _exchange(_to_lines_kernel, (comps, rows // n, width * n), 1, n, x)


def from_lines(x, n):
    comps, rows, around = x.shape
    return _exchange(_from_lines_kernel, (comps, rows * n, around // n), 2, n, x)


def dft_table(length):
    half = length // 2
    root = int(round(math.sqrt(length)))
    cols = jnp.concatenate([jnp.arange(half + 1), jnp.arange(1, half)])
    is_sin = jnp.arange(length) > half
    step = 2.0 * math.pi / length
    coarse = (root * jnp.arange(length // root)[:, None] * cols[None, :]) % length
    fine = (jnp.arange(root)[:, None] * cols[None, :]) % length
    coarse_c, coarse_s = jnp.cos(step * coarse.astype(jnp.float32)), jnp.sin(step * coarse.astype(jnp.float32))
    fine_c, fine_s = jnp.cos(step * fine.astype(jnp.float32)), jnp.sin(step * fine.astype(jnp.float32))
    cos_part = coarse_c[:, None] * fine_c[None] - coarse_s[:, None] * fine_s[None]
    sin_part = coarse_s[:, None] * fine_c[None] + coarse_c[:, None] * fine_s[None]
    return jnp.where(is_sin[None, None], sin_part, cos_part).reshape(length, length)


def paired_inverse(precond):
    length = precond.shape[2]
    half = length // 2
    low = precond[:, :, : half + 1]
    mirror = jnp.flip(precond[:, :, half + 1 :], axis=2)
    inner = jnp.concatenate([jnp.zeros_like(low[:, :, :1]), mirror, jnp.zeros_like(low[:, :, :1])], axis=2)
    paired = low + inner
    return jnp.concatenate([paired, paired[:, :, 1:half]], axis=2)


def with_halo(x, sides, width, wrap):
    for axis, dim in sides:
        size, length = (lax.axis_size(axis), x.shape[dim])
        up = [(i, (i + 1) % size) for i in range(size if wrap else size - 1)]
        down = [(j, i) for i, j in up]
        last = lax.slice_in_dim(x, length - width, length, axis=dim)
        first = lax.slice_in_dim(x, 0, width, axis=dim)
        before = lax.ppermute(last, axis, up)
        after = lax.ppermute(first, axis, down)
        x = jnp.concatenate([before, x, after], axis=dim)
    return x


def swap_radial(field):
    extent = field.shape
    folded = field.reshape(extent[0], extent[1] // 2, 2, extent[2])
    return jnp.flip(folded, axis=2).reshape(extent)


def apply_operator(field, stiffness):
    axial_pad = with_halo(field, (("ax", 0),), 1, False)
    sector_pad = with_halo(field, (("sec", 2),), 1, True)
    beside = axial_pad[2:] + axial_pad[:-2]
    beside = beside + sector_pad[:, :, 2:] + sector_pad[:, :, :-2]
    return (stiffness + 4.5) * field - beside - 0.5 * swap_radial(field)


def shards(load, disp, stiff, hole, section_class, class_table, precond):
    slab_count, comp_count, sector_width = disp.shape
    sector_count = lax.axis_size("sec")
    around_cells = sector_width * sector_count
    total_axial = slab_count * lax.axis_size("ax")
    position = lax.axis_index("ax") * slab_count + jnp.arange(slab_count)
    taper = 1.0 + 2.0 * position.astype(jnp.float32) / (total_axial - 1)
    one_hot = (section_class[:, None] == jnp.arange(class_table.shape[0])[None, :]).astype(
        jnp.float32
    )
    factors = jnp.dot(one_hot, class_table, precision=lax.Precision.HIGHEST)
    stiffness = stiff * (factors * taper[:, None])[:, :, None]
    solid = (1 - hole).astype(jnp.float32)[:, None, :]
    residual = solid * (load - apply_operator(disp, stiffness))
    lines = to_lines(jnp.transpose(residual, (1, 0, 2)), sector_count)
    spectrum = jnp.dot(
        lines.reshape(-1, around_cells), dft_table(around_cells), precision=lax.Precision.HIGH
    ).reshape(lines.shape)
    mixed = jnp.sum(paired_inverse(precond)[:, :, None] * spectrum[None], axis=1)
    smoothed_lines = lax.dot_general(
        mixed.reshape(-1, around_cells),
        dft_table(around_cells),
        (((1,), (1,)), ((), ())),
        precision=lax.Precision.HIGH,
    ) / around_cells
    smoothed = jnp.transpose(
        from_lines(smoothed_lines.reshape(lines.shape), sector_count), (1, 0, 2)
    )
    prec = solid * smoothed
    image = solid * apply_operator(prec, stiffness)
    cell_total = slab_count * lax.axis_size("ax") * comp_count * around_cells
    parts = jnp.stack(
        [
            jnp.sum(residual * prec),
            jnp.sum(prec * image),
            jnp.sum(residual * residual),
            jnp.sum(residual * image),
            jnp.sum(image * image),
        ]
    )
    packed = jnp.zeros((8, 128), jnp.float32).at[0, :5].set(parts)
    totals = all_sum(packed, 0)[0]
    inner_rz = totals[0] / cell_total
    inner_zq = totals[1] / cell_total
    alpha = inner_rz / inner_zq
    residual_new = residual - alpha * image
    square_new = (totals[2] - alpha * (2.0 * totals[3] - alpha * totals[4])) / cell_total
    disp_new = disp + alpha * prec
    return (disp_new, residual_new, jnp.stack([inner_rz, inner_zq, square_new]))


def solution(mesh):
    in_specs = (
        P("ax", None, "sec"),
        P("ax", None, "sec"),
        P("ax", None, "sec"),
        P("ax", "sec"),
        P("ax"),
        P(),
        P(),
    )
    out_specs = (P("ax", None, "sec"), P("ax", None, "sec"), P())
    return jax.shard_map(shards, mesh=mesh, in_specs=in_specs, out_specs=out_specs, check_vma=False)
```

```python
import functools
import math

import jax
import jax.numpy as jnp
from jax import lax
from jax.experimental import pallas as pl
from jax.experimental.pallas import tpu as pltpu
from jax.sharding import PartitionSpec as P


MESH = pl.DeviceIdType.MESH


def _lines():
    me_ax = lax.axis_index("ax")
    me_sec = lax.axis_index("sec")
    x = me_ax % 4
    z = (me_ax // 4) % 8
    ylo = me_ax // 32
    core = me_sec % 2
    yhi = me_sec // 2
    y = yhi * 2 + ylo
    return [
        (2, core, lambda c: (me_ax, yhi * 2 + c)),
        (4, x, lambda c: (me_ax - x + c, me_sec)),
        (4, y, lambda c: (me_ax - ylo * 32 + (c % 2) * 32, (c // 2) * 2 + core)),
        (8, z, lambda c: (me_ax - z * 4 + c * 4, me_sec)),
    ]


def _ar_kernel(x_ref, o_ref, r0, r1, r2, r3, own, send_sems, recv_sems):
    recvs = (r0, r1, r2, r3)
    lines = _lines()
    for r in recvs:
        r[...] = jnp.zeros_like(r)
    barrier = pltpu.get_barrier_semaphore()
    count = 0
    for n, mine, dev in lines:
        for d in range(1, n):
            pl.semaphore_signal(barrier, inc=1, device_id=dev((mine + d) % n), device_id_type=MESH)
            count += 1
    pl.semaphore_wait(barrier, count)
    src = x_ref
    base = 0
    for r, (n, mine, dev) in enumerate(lines):
        copies = []
        for d in range(1, n):
            cp = pltpu.make_async_remote_copy(
                src_ref=src,
                dst_ref=recvs[r].at[mine],
                send_sem=send_sems.at[base + d],
                recv_sem=recv_sems.at[base + d],
                device_id=dev((mine + d) % n),
                device_id_type=MESH,
            )
            cp.start()
            copies.append(cp)
        mine_val = src[...]
        for cp in copies:
            cp.wait_recv()
        total = None
        for c in range(n):
            v = jnp.where(mine == c, mine_val, recvs[r][c])
            total = v if total is None else total + v
        for cp in copies:
            cp.wait_send()
        base += n
        if r + 1 < len(lines):
            own[r] = total
            src = own.at[r]
        else:
            o_ref[...] = total


def all_sum(part, cid):
    return pl.pallas_call(
        _ar_kernel,
        out_shape=jax.ShapeDtypeStruct(part.shape, jnp.float32),
        in_specs=[pl.BlockSpec(memory_space=pltpu.VMEM)],
        out_specs=pl.BlockSpec(memory_space=pltpu.VMEM),
        scratch_shapes=[
            pltpu.VMEM((2,) + part.shape, jnp.float32),
            pltpu.VMEM((4,) + part.shape, jnp.float32),
            pltpu.VMEM((4,) + part.shape, jnp.float32),
            pltpu.VMEM((8,) + part.shape, jnp.float32),
            pltpu.VMEM((3,) + part.shape, jnp.float32),
            pltpu.SemaphoreType.DMA((18,)),
            pltpu.SemaphoreType.DMA((18,)),
        ],
        compiler_params=pltpu.CompilerParams(collective_id=cid, has_side_effects=True),
    )(part)


def _to_lines_kernel(n, x_ref, o_ref, send_sems, recv_sems, local_sem):
    me = lax.axis_index("sec")
    ax = lax.axis_index("ax")
    rows, width = o_ref.shape[1], x_ref.shape[2]
    barrier = pltpu.get_barrier_semaphore()
    for d in range(1, n):
        pl.semaphore_signal(barrier, inc=1, device_id=(ax, (me + d) % n), device_id_type=MESH)
    pl.semaphore_wait(barrier, n - 1)
    dst = o_ref.at[:, :, pl.ds(pl.multiple_of(me * width, width), width)]
    copies = []
    for d in range(1, n):
        peer = (me + d) % n
        cp = pltpu.make_async_remote_copy(
            src_ref=x_ref.at[:, pl.ds(pl.multiple_of(peer * rows, rows), rows), :],
            dst_ref=dst,
            send_sem=send_sems.at[d],
            recv_sem=recv_sems.at[d],
            device_id=(ax, peer),
            device_id_type=MESH,
        )
        cp.start()
        copies.append(cp)
    local = pltpu.make_async_copy(
        x_ref.at[:, pl.ds(pl.multiple_of(me * rows, rows), rows), :], dst, local_sem
    )
    local.start()
    local.wait()
    for cp in copies:
        cp.wait()


def _from_lines_kernel(n, x_ref, o_ref, send_sems, recv_sems, local_sem):
    me = lax.axis_index("sec")
    ax = lax.axis_index("ax")
    rows, width = x_ref.shape[1], o_ref.shape[2]
    barrier = pltpu.get_barrier_semaphore()
    for d in range(1, n):
        pl.semaphore_signal(barrier, inc=1, device_id=(ax, (me + d) % n), device_id_type=MESH)
    pl.semaphore_wait(barrier, n - 1)
    dst = o_ref.at[:, pl.ds(pl.multiple_of(me * rows, rows), rows), :]
    copies = []
    for d in range(1, n):
        peer = (me + d) % n
        cp = pltpu.make_async_remote_copy(
            src_ref=x_ref.at[:, :, pl.ds(pl.multiple_of(peer * width, width), width)],
            dst_ref=dst,
            send_sem=send_sems.at[d],
            recv_sem=recv_sems.at[d],
            device_id=(ax, peer),
            device_id_type=MESH,
        )
        cp.start()
        copies.append(cp)
    local = pltpu.make_async_copy(
        x_ref.at[:, :, pl.ds(pl.multiple_of(me * width, width), width)], dst, local_sem
    )
    local.start()
    local.wait()
    for cp in copies:
        cp.wait()


def _exchange(body, out_shape, cid, n, x):
    return pl.pallas_call(
        functools.partial(body, n),
        out_shape=jax.ShapeDtypeStruct(out_shape, x.dtype),
        in_specs=[pl.BlockSpec(memory_space=pltpu.VMEM)],
        out_specs=pl.BlockSpec(memory_space=pltpu.VMEM),
        scratch_shapes=[
            pltpu.SemaphoreType.DMA((n,)),
            pltpu.SemaphoreType.DMA((n,)),
            pltpu.SemaphoreType.DMA,
        ],
        compiler_params=pltpu.CompilerParams(collective_id=cid, has_side_effects=True),
    )(x)


def to_lines(x, n):
    comps, rows, width = x.shape
    return _exchange(_to_lines_kernel, (comps, rows // n, width * n), 1, n, x)


def from_lines(x, n):
    comps, rows, around = x.shape
    return _exchange(_from_lines_kernel, (comps, rows * n, around // n), 2, n, x)


def dft_table(length):
    half = length // 2
    root = int(round(math.sqrt(length)))
    cols = jnp.concatenate([jnp.arange(half + 1), jnp.arange(1, half)])
    is_sin = jnp.arange(length) > half
    step = 2.0 * math.pi / length
    coarse = (root * jnp.arange(length // root)[:, None] * cols[None, :]) % length
    fine = (jnp.arange(root)[:, None] * cols[None, :]) % length
    coarse_c, coarse_s = jnp.cos(step * coarse.astype(jnp.float32)), jnp.sin(step * coarse.astype(jnp.float32))
    fine_c, fine_s = jnp.cos(step * fine.astype(jnp.float32)), jnp.sin(step * fine.astype(jnp.float32))
    cos_part = coarse_c[:, None] * fine_c[None] - coarse_s[:, None] * fine_s[None]
    sin_part = coarse_s[:, None] * fine_c[None] + coarse_c[:, None] * fine_s[None]
    return jnp.where(is_sin[None, None], sin_part, cos_part).reshape(length, length)


def paired_inverse(precond):
    length = precond.shape[2]
    half = length // 2
    low = precond[:, :, : half + 1]
    mirror = jnp.flip(precond[:, :, half + 1 :], axis=2)
    inner = jnp.concatenate([jnp.zeros_like(low[:, :, :1]), mirror, jnp.zeros_like(low[:, :, :1])], axis=2)
    paired = low + inner
    return jnp.concatenate([paired, paired[:, :, 1:half]], axis=2)


def _halo_kernel(sizes, x_ref, o_ref, send_sems, recv_sems):
    n_ax, n_sec = sizes
    ax = lax.axis_index("ax")
    sec = lax.axis_index("sec")
    peers = [
        ((ax + n_ax - 1) % n_ax, sec),
        ((ax + 1) % n_ax, sec),
        (ax, (sec + n_sec - 1) % n_sec),
        (ax, (sec + 1) % n_sec),
    ]
    barrier = pltpu.get_barrier_semaphore()
    for peer in peers:
        pl.semaphore_signal(barrier, inc=1, device_id=peer, device_id_type=MESH)
    pl.semaphore_wait(barrier, len(peers))
    copies = []
    for i, peer in enumerate(peers):
        cp = pltpu.make_async_remote_copy(
            src_ref=x_ref.at[i],
            dst_ref=o_ref.at[i],
            send_sem=send_sems.at[i],
            recv_sem=recv_sems.at[i],
            device_id=peer,
            device_id_type=MESH,
        )
        cp.start()
        copies.append(cp)
    for cp in copies:
        cp.wait()


def halo_exchange(field, cid):
    rows, comps, width = field.shape
    lanes = max(width, rows)
    subl = -(-comps // 8) * 8

    def fit(plane):
        return jnp.pad(plane, ((0, subl - plane.shape[0]), (0, lanes - plane.shape[1])))

    edges = jnp.stack(
        [fit(field[0]), fit(field[-1]), fit(field[:, :, 0].T), fit(field[:, :, -1].T)]
    )
    got = pl.pallas_call(
        functools.partial(_halo_kernel, (lax.axis_size("ax"), lax.axis_size("sec"))),
        out_shape=jax.ShapeDtypeStruct(edges.shape, edges.dtype),
        in_specs=[pl.BlockSpec(memory_space=pltpu.VMEM)],
        out_specs=pl.BlockSpec(memory_space=pltpu.VMEM),
        scratch_shapes=[pltpu.SemaphoreType.DMA((4,)), pltpu.SemaphoreType.DMA((4,))],
        compiler_params=pltpu.CompilerParams(collective_id=cid, has_side_effects=True),
    )(edges)
    ax = lax.axis_index("ax")
    after_row = jnp.where(ax == lax.axis_size("ax") - 1, 0.0, got[0, :comps, :width])
    before_row = jnp.where(ax == 0, 0.0, got[1, :comps, :width])
    after_col = got[2, :comps, :rows].T
    before_col = got[3, :comps, :rows].T
    down = jnp.concatenate([field[1:], after_row[None]], axis=0)
    up = jnp.concatenate([before_row[None], field[:-1]], axis=0)
    right = jnp.concatenate([field[:, :, 1:], after_col[:, :, None]], axis=2)
    left = jnp.concatenate([before_col[:, :, None], field[:, :, :-1]], axis=2)
    return up + down + left + right


def swap_radial(field):
    extent = field.shape
    folded = field.reshape(extent[0], extent[1] // 2, 2, extent[2])
    return jnp.flip(folded, axis=2).reshape(extent)


def apply_operator(field, stiffness, cid):
    beside = halo_exchange(field, cid)
    return (stiffness + 4.5) * field - beside - 0.5 * swap_radial(field)


def shards(load, disp, stiff, hole, section_class, class_table, precond):
    slab_count, comp_count, sector_width = disp.shape
    sector_count = lax.axis_size("sec")
    around_cells = sector_width * sector_count
    total_axial = slab_count * lax.axis_size("ax")
    position = lax.axis_index("ax") * slab_count + jnp.arange(slab_count)
    taper = 1.0 + 2.0 * position.astype(jnp.float32) / (total_axial - 1)
    one_hot = (section_class[:, None] == jnp.arange(class_table.shape[0])[None, :]).astype(
        jnp.float32
    )
    factors = jnp.dot(one_hot, class_table, precision=lax.Precision.HIGHEST)
    stiffness = stiff * (factors * taper[:, None])[:, :, None]
    solid = (1 - hole).astype(jnp.float32)[:, None, :]
    residual = solid * (load - apply_operator(disp, stiffness, 3))
    lines = to_lines(jnp.transpose(residual, (1, 0, 2)), sector_count)
    spectrum = jnp.dot(
        lines.reshape(-1, around_cells), dft_table(around_cells), precision=lax.Precision.HIGH
    ).reshape(lines.shape)
    mixed = jnp.sum(paired_inverse(precond)[:, :, None] * spectrum[None], axis=1)
    smoothed_lines = lax.dot_general(
        mixed.reshape(-1, around_cells),
        dft_table(around_cells),
        (((1,), (1,)), ((), ())),
        precision=lax.Precision.HIGH,
    ) / around_cells
    smoothed = jnp.transpose(
        from_lines(smoothed_lines.reshape(lines.shape), sector_count), (1, 0, 2)
    )
    prec = solid * smoothed
    image = solid * apply_operator(prec, stiffness, 4)
    cell_total = slab_count * lax.axis_size("ax") * comp_count * around_cells
    parts = jnp.stack(
        [
            jnp.sum(residual * prec),
            jnp.sum(prec * image),
            jnp.sum(residual * residual),
            jnp.sum(residual * image),
            jnp.sum(image * image),
        ]
    )
    packed = jnp.zeros((8, 128), jnp.float32).at[0, :5].set(parts)
    totals = all_sum(packed, 0)[0]
    inner_rz = totals[0] / cell_total
    inner_zq = totals[1] / cell_total
    alpha = inner_rz / inner_zq
    residual_new = residual - alpha * image
    square_new = (totals[2] - alpha * (2.0 * totals[3] - alpha * totals[4])) / cell_total
    disp_new = disp + alpha * prec
    return (disp_new, residual_new, jnp.stack([inner_rz, inner_zq, square_new]))


def solution(mesh):
    in_specs = (
        P("ax", None, "sec"),
        P("ax", None, "sec"),
        P("ax", None, "sec"),
        P("ax", "sec"),
        P("ax"),
        P(),
        P(),
    )
    out_specs = (P("ax", None, "sec"), P("ax", None, "sec"), P())
    return jax.shard_map(shards, mesh=mesh, in_specs=in_specs, out_specs=out_specs, check_vma=False)
```

```python
import functools
import math

import jax
import jax.numpy as jnp
from jax import lax
from jax.experimental import pallas as pl
from jax.experimental.pallas import tpu as pltpu
from jax.sharding import PartitionSpec as P


MESH = pl.DeviceIdType.MESH


def _groups():
    me_ax = lax.axis_index("ax")
    me_sec = lax.axis_index("sec")
    x = me_ax % 4
    z = (me_ax // 4) % 8
    ylo = me_ax // 32
    core = me_sec % 2
    yhi = me_sec // 2

    def plane_peer(c):
        y = c % 4
        return ((y % 2) * 32 + z * 4 + (c // 4) % 4, (y // 2) * 2 + c // 16)

    return [
        (32, (core * 4 + x) * 4 + yhi * 2 + ylo, plane_peer),
        (8, z, lambda c: (me_ax - z * 4 + c * 4, me_sec)),
    ]


def _local_sums(r_ref, p_ref, i_ref):
    rows = r_ref.shape[0]
    plane = r_ref.shape[1:]

    def body(k, acc):
        r, p, i = r_ref[k], p_ref[k], i_ref[k]
        return (acc[0] + r * p, acc[1] + p * i, acc[2] + r * r, acc[3] + r * i, acc[4] + i * i)

    zero = jnp.zeros(plane, jnp.float32)
    acc = lax.fori_loop(0, rows, body, (zero,) * 5, unroll=8)
    lane = lax.broadcasted_iota(jnp.int32, (8, 128), 1)
    row = lax.broadcasted_iota(jnp.int32, (8, 128), 0)
    packed = jnp.zeros((8, 128), jnp.float32)
    for k, a in enumerate(acc):
        packed = jnp.where((row == 0) & (lane == k), jnp.sum(a), packed)
    return packed


def _ar_kernel(r_ref, p_ref, i_ref, o_ref, recv_a, recv_b, own, send_sems, recv_sems):
    recvs = (recv_a, recv_b)
    groups = _groups()
    for r in recvs:
        r[...] = jnp.zeros_like(r)
    barrier = pltpu.get_barrier_semaphore()
    count = 0
    for n, mine, dev in groups:
        for d in range(1, n):
            pl.semaphore_signal(barrier, inc=1, device_id=dev((mine + d) % n), device_id_type=MESH)
            count += 1
    own[0] = _local_sums(r_ref, p_ref, i_ref)
    pl.semaphore_wait(barrier, count)
    base = 0
    for g, (n, mine, dev) in enumerate(groups):
        src = own.at[g]
        copies = []
        for d in range(1, n):
            cp = pltpu.make_async_remote_copy(
                src_ref=src,
                dst_ref=recvs[g].at[mine],
                send_sem=send_sems.at[base + d],
                recv_sem=recv_sems.at[base + d],
                device_id=dev((mine + d) % n),
                device_id_type=MESH,
            )
            cp.start()
            copies.append(cp)
        mine_val = src[...]
        for cp in copies:
            cp.wait_recv()
        total = None
        for c in range(n):
            v = jnp.where(mine == c, mine_val, recvs[g][c])
            total = v if total is None else total + v
        for cp in copies:
            cp.wait_send()
        base += n
        if g + 1 < len(groups):
            own[g + 1] = total
        else:
            o_ref[...] = total


def all_sums(residual, prec, image, cid):
    return pl.pallas_call(
        _ar_kernel,
        out_shape=jax.ShapeDtypeStruct((8, 128), jnp.float32),
        in_specs=[pl.BlockSpec(memory_space=pltpu.VMEM)] * 3,
        out_specs=pl.BlockSpec(memory_space=pltpu.VMEM),
        scratch_shapes=[
            pltpu.VMEM((32, 8, 128), jnp.float32),
            pltpu.VMEM((8, 8, 128), jnp.float32),
            pltpu.VMEM((2, 8, 128), jnp.float32),
            pltpu.SemaphoreType.DMA((40,)),
            pltpu.SemaphoreType.DMA((40,)),
        ],
        compiler_params=pltpu.CompilerParams(collective_id=cid, has_side_effects=True),
    )(residual, prec, image)


def _to_lines_kernel(n, x_ref, o_ref, send_sems, recv_sems, local_sem):
    me = lax.axis_index("sec")
    ax = lax.axis_index("ax")
    rows, width = o_ref.shape[1], x_ref.shape[2]
    barrier = pltpu.get_barrier_semaphore()
    for d in range(1, n):
        pl.semaphore_signal(barrier, inc=1, device_id=(ax, (me + d) % n), device_id_type=MESH)
    pl.semaphore_wait(barrier, n - 1)
    dst = o_ref.at[:, :, pl.ds(pl.multiple_of(me * width, width), width)]
    copies = []
    for d in range(1, n):
        peer = (me + d) % n
        cp = pltpu.make_async_remote_copy(
            src_ref=x_ref.at[:, pl.ds(pl.multiple_of(peer * rows, rows), rows), :],
            dst_ref=dst,
            send_sem=send_sems.at[d],
            recv_sem=recv_sems.at[d],
            device_id=(ax, peer),
            device_id_type=MESH,
        )
        cp.start()
        copies.append(cp)
    local = pltpu.make_async_copy(
        x_ref.at[:, pl.ds(pl.multiple_of(me * rows, rows), rows), :], dst, local_sem
    )
    local.start()
    local.wait()
    for cp in copies:
        cp.wait()


def _from_lines_kernel(n, x_ref, o_ref, send_sems, recv_sems, local_sem):
    me = lax.axis_index("sec")
    ax = lax.axis_index("ax")
    rows, width = x_ref.shape[1], o_ref.shape[2]
    barrier = pltpu.get_barrier_semaphore()
    for d in range(1, n):
        pl.semaphore_signal(barrier, inc=1, device_id=(ax, (me + d) % n), device_id_type=MESH)
    pl.semaphore_wait(barrier, n - 1)
    dst = o_ref.at[:, pl.ds(pl.multiple_of(me * rows, rows), rows), :]
    copies = []
    for d in range(1, n):
        peer = (me + d) % n
        cp = pltpu.make_async_remote_copy(
            src_ref=x_ref.at[:, :, pl.ds(pl.multiple_of(peer * width, width), width)],
            dst_ref=dst,
            send_sem=send_sems.at[d],
            recv_sem=recv_sems.at[d],
            device_id=(ax, peer),
            device_id_type=MESH,
        )
        cp.start()
        copies.append(cp)
    local = pltpu.make_async_copy(
        x_ref.at[:, :, pl.ds(pl.multiple_of(me * width, width), width)], dst, local_sem
    )
    local.start()
    local.wait()
    for cp in copies:
        cp.wait()


def _exchange(body, out_shape, cid, n, x):
    return pl.pallas_call(
        functools.partial(body, n),
        out_shape=jax.ShapeDtypeStruct(out_shape, x.dtype),
        in_specs=[pl.BlockSpec(memory_space=pltpu.VMEM)],
        out_specs=pl.BlockSpec(memory_space=pltpu.VMEM),
        scratch_shapes=[
            pltpu.SemaphoreType.DMA((n,)),
            pltpu.SemaphoreType.DMA((n,)),
            pltpu.SemaphoreType.DMA,
        ],
        compiler_params=pltpu.CompilerParams(collective_id=cid, has_side_effects=True),
    )(x)


def to_lines(x, n):
    comps, rows, width = x.shape
    return _exchange(_to_lines_kernel, (comps, rows // n, width * n), 1, n, x)


def from_lines(x, n):
    comps, rows, around = x.shape
    return _exchange(_from_lines_kernel, (comps, rows * n, around // n), 2, n, x)


def dft_table(length):
    half = length // 2
    root = int(round(math.sqrt(length)))
    cols = jnp.concatenate([jnp.arange(half + 1), jnp.arange(1, half)])
    is_sin = jnp.arange(length) > half
    step = 2.0 * math.pi / length
    coarse = (root * jnp.arange(length // root)[:, None] * cols[None, :]) % length
    fine = (jnp.arange(root)[:, None] * cols[None, :]) % length
    coarse_c, coarse_s = jnp.cos(step * coarse.astype(jnp.float32)), jnp.sin(step * coarse.astype(jnp.float32))
    fine_c, fine_s = jnp.cos(step * fine.astype(jnp.float32)), jnp.sin(step * fine.astype(jnp.float32))
    cos_part = coarse_c[:, None] * fine_c[None] - coarse_s[:, None] * fine_s[None]
    sin_part = coarse_s[:, None] * fine_c[None] + coarse_c[:, None] * fine_s[None]
    return jnp.where(is_sin[None, None], sin_part, cos_part).reshape(length, length)


def paired_inverse(precond):
    length = precond.shape[2]
    half = length // 2
    low = precond[:, :, : half + 1]
    mirror = jnp.flip(precond[:, :, half + 1 :], axis=2)
    inner = jnp.concatenate([jnp.zeros_like(low[:, :, :1]), mirror, jnp.zeros_like(low[:, :, :1])], axis=2)
    paired = low + inner
    return jnp.concatenate([paired, paired[:, :, 1:half]], axis=2)


def with_halo(x, sides, width, wrap):
    for axis, dim in sides:
        size, length = (lax.axis_size(axis), x.shape[dim])
        up = [(i, (i + 1) % size) for i in range(size if wrap else size - 1)]
        down = [(j, i) for i, j in up]
        last = lax.slice_in_dim(x, length - width, length, axis=dim)
        first = lax.slice_in_dim(x, 0, width, axis=dim)
        before = lax.ppermute(last, axis, up)
        after = lax.ppermute(first, axis, down)
        x = jnp.concatenate([before, x, after], axis=dim)
    return x


def swap_radial(field):
    extent = field.shape
    folded = field.reshape(extent[0], extent[1] // 2, 2, extent[2])
    return jnp.flip(folded, axis=2).reshape(extent)


def apply_operator(field, stiffness):
    axial_pad = with_halo(field, (("ax", 0),), 1, False)
    sector_pad = with_halo(field, (("sec", 2),), 1, True)
    beside = axial_pad[2:] + axial_pad[:-2]
    beside = beside + sector_pad[:, :, 2:] + sector_pad[:, :, :-2]
    return (stiffness + 4.5) * field - beside - 0.5 * swap_radial(field)


def shards(load, disp, stiff, hole, section_class, class_table, precond):
    slab_count, comp_count, sector_width = disp.shape
    sector_count = lax.axis_size("sec")
    around_cells = sector_width * sector_count
    total_axial = slab_count * lax.axis_size("ax")
    position = lax.axis_index("ax") * slab_count + jnp.arange(slab_count)
    taper = 1.0 + 2.0 * position.astype(jnp.float32) / (total_axial - 1)
    one_hot = (section_class[:, None] == jnp.arange(class_table.shape[0])[None, :]).astype(
        jnp.float32
    )
    factors = jnp.dot(one_hot, class_table, precision=lax.Precision.HIGHEST)
    stiffness = stiff * (factors * taper[:, None])[:, :, None]
    solid = (1 - hole).astype(jnp.float32)[:, None, :]
    residual = solid * (load - apply_operator(disp, stiffness))
    lines = to_lines(jnp.transpose(residual, (1, 0, 2)), sector_count)
    spectrum = jnp.dot(
        lines.reshape(-1, around_cells), dft_table(around_cells), precision=lax.Precision.HIGH
    ).reshape(lines.shape)
    mixed = jnp.sum(paired_inverse(precond)[:, :, None] * spectrum[None], axis=1)
    smoothed_lines = lax.dot_general(
        mixed.reshape(-1, around_cells),
        dft_table(around_cells),
        (((1,), (1,)), ((), ())),
        precision=lax.Precision.HIGH,
    ) / around_cells
    smoothed = jnp.transpose(
        from_lines(smoothed_lines.reshape(lines.shape), sector_count), (1, 0, 2)
    )
    prec = solid * smoothed
    image = solid * apply_operator(prec, stiffness)
    cell_total = slab_count * lax.axis_size("ax") * comp_count * around_cells
    totals = all_sums(residual, prec, image, 0)[0]
    inner_rz = totals[0] / cell_total
    inner_zq = totals[1] / cell_total
    alpha = inner_rz / inner_zq
    residual_new = residual - alpha * image
    square_new = (totals[2] - alpha * (2.0 * totals[3] - alpha * totals[4])) / cell_total
    disp_new = disp + alpha * prec
    return (disp_new, residual_new, jnp.stack([inner_rz, inner_zq, square_new]))


def solution(mesh):
    in_specs = (
        P("ax", None, "sec"),
        P("ax", None, "sec"),
        P("ax", None, "sec"),
        P("ax", "sec"),
        P("ax"),
        P(),
        P(),
    )
    out_specs = (P("ax", None, "sec"), P("ax", None, "sec"), P())
    return jax.shard_map(shards, mesh=mesh, in_specs=in_specs, out_specs=out_specs, check_vma=False)
```

```python
import functools
import math

import jax
import jax.numpy as jnp
from jax import lax
from jax.experimental import pallas as pl
from jax.experimental.pallas import tpu as pltpu
from jax.sharding import PartitionSpec as P


MESH = pl.DeviceIdType.MESH


def _groups():
    me_ax = lax.axis_index("ax")
    me_sec = lax.axis_index("sec")
    x = me_ax % 4
    z = (me_ax // 4) % 8
    ylo = me_ax // 32
    core = me_sec % 2
    yhi = me_sec // 2

    def plane_peer(c):
        y = c % 4
        return ((y % 2) * 32 + z * 4 + (c // 4) % 4, (y // 2) * 2 + c // 16)

    return [
        (32, (core * 4 + x) * 4 + yhi * 2 + ylo, plane_peer),
        (8, z, lambda c: (me_ax - z * 4 + c * 4, me_sec)),
    ]


def _local_sums(r_ref, p_ref, i_ref):
    rows = r_ref.shape[0]
    plane = r_ref.shape[1:]

    def body(k, acc):
        r, p, i = r_ref[k], p_ref[k], i_ref[k]
        return (acc[0] + r * p, acc[1] + p * i, acc[2] + r * r, acc[3] + r * i, acc[4] + i * i)

    zero = jnp.zeros(plane, jnp.float32)
    acc = lax.fori_loop(0, rows, body, (zero,) * 5, unroll=8)
    lane = lax.broadcasted_iota(jnp.int32, (8, 128), 1)
    row = lax.broadcasted_iota(jnp.int32, (8, 128), 0)
    packed = jnp.zeros((8, 128), jnp.float32)
    for k, a in enumerate(acc):
        packed = jnp.where((row == 0) & (lane == k), jnp.sum(a), packed)
    return packed


def _ar_kernel(r_ref, p_ref, i_ref, o_ref, recv_a, recv_b, own, send_sems, recv_sems):
    recvs = (recv_a, recv_b)
    groups = _groups()
    for r in recvs:
        r[...] = jnp.zeros_like(r)
    barrier = pltpu.get_barrier_semaphore()
    count = 0
    for n, mine, dev in groups:
        for d in range(1, n):
            pl.semaphore_signal(barrier, inc=1, device_id=dev((mine + d) % n), device_id_type=MESH)
            count += 1
    own[0] = _local_sums(r_ref, p_ref, i_ref)
    pl.semaphore_wait(barrier, count)
    base = 0
    for g, (n, mine, dev) in enumerate(groups):
        src = own.at[g]
        copies = []
        for d in range(1, n):
            cp = pltpu.make_async_remote_copy(
                src_ref=src,
                dst_ref=recvs[g].at[mine],
                send_sem=send_sems.at[base + d],
                recv_sem=recv_sems.at[base + d],
                device_id=dev((mine + d) % n),
                device_id_type=MESH,
            )
            cp.start()
            copies.append(cp)
        mine_val = src[...]
        for cp in copies:
            cp.wait_recv()
        total = None
        for c in range(n):
            v = jnp.where(mine == c, mine_val, recvs[g][c])
            total = v if total is None else total + v
        for cp in copies:
            cp.wait_send()
        base += n
        if g + 1 < len(groups):
            own[g + 1] = total
        else:
            o_ref[...] = total


def all_sums(residual, prec, image, cid):
    return pl.pallas_call(
        _ar_kernel,
        out_shape=jax.ShapeDtypeStruct((8, 128), jnp.float32),
        in_specs=[pl.BlockSpec(memory_space=pltpu.VMEM)] * 3,
        out_specs=pl.BlockSpec(memory_space=pltpu.VMEM),
        scratch_shapes=[
            pltpu.VMEM((32, 8, 128), jnp.float32),
            pltpu.VMEM((8, 8, 128), jnp.float32),
            pltpu.VMEM((2, 8, 128), jnp.float32),
            pltpu.SemaphoreType.DMA((40,)),
            pltpu.SemaphoreType.DMA((40,)),
        ],
        compiler_params=pltpu.CompilerParams(collective_id=cid, has_side_effects=True),
    )(residual, prec, image)


def _to_lines_kernel(n, x_ref, o_ref, send_sems, recv_sems, local_sem):
    me = lax.axis_index("sec")
    ax = lax.axis_index("ax")
    rows, width = o_ref.shape[1], x_ref.shape[2]
    barrier = pltpu.get_barrier_semaphore()
    for d in range(1, n):
        pl.semaphore_signal(barrier, inc=1, device_id=(ax, (me + d) % n), device_id_type=MESH)
    pl.semaphore_wait(barrier, n - 1)
    dst = o_ref.at[:, :, pl.ds(pl.multiple_of(me * width, width), width)]
    copies = []
    for d in range(1, n):
        peer = (me + d) % n
        cp = pltpu.make_async_remote_copy(
            src_ref=x_ref.at[:, pl.ds(pl.multiple_of(peer * rows, rows), rows), :],
            dst_ref=dst,
            send_sem=send_sems.at[d],
            recv_sem=recv_sems.at[d],
            device_id=(ax, peer),
            device_id_type=MESH,
        )
        cp.start()
        copies.append(cp)
    local = pltpu.make_async_copy(
        x_ref.at[:, pl.ds(pl.multiple_of(me * rows, rows), rows), :], dst, local_sem
    )
    local.start()
    local.wait()
    for cp in copies:
        cp.wait()


def _from_lines_kernel(sizes, x_ref, cpk_ref, last_ref, first_ref, o_ref, cols_ref, before_ref,
                       after_ref, send_sems, recv_sems, local_sems):
    n_ax, n = sizes
    me = lax.axis_index("sec")
    ax = lax.axis_index("ax")
    rows, width = x_ref.shape[1], o_ref.shape[2]
    up_ax, down_ax = (ax + 1) % n_ax, (ax + n_ax - 1) % n_ax
    peers = [(ax, (me + d) % n) for d in range(1, n)]
    peers += [(up_ax, s) for s in range(n)] + [(down_ax, s) for s in range(n)]
    barrier = pltpu.get_barrier_semaphore()
    for peer in peers:
        pl.semaphore_signal(barrier, inc=1, device_id=peer, device_id_type=MESH)
    pl.semaphore_wait(barrier, len(peers))
    dst = o_ref.at[:, pl.ds(pl.multiple_of(me * rows, rows), rows), :]
    sends, recvs = [], []
    for d in range(1, n):
        peer = (me + d) % n
        for k, (src, out) in enumerate(
            (
                (x_ref.at[:, :, pl.ds(pl.multiple_of(peer * width, width), width)], dst),
                (cpk_ref.at[peer], cols_ref.at[me]),
            )
        ):
            cp = pltpu.make_async_remote_copy(
                src_ref=src,
                dst_ref=out,
                send_sem=send_sems.at[k * n + d],
                recv_sem=recv_sems.at[k * n + d],
                device_id=(ax, peer),
                device_id_type=MESH,
            )
            cp.start()
            sends.append(cp)
        origin = (me + n - d) % n
        for k, (src, out) in enumerate(
            (
                (x_ref.at[:, :, pl.ds(0, width)], o_ref.at[:, pl.ds(pl.multiple_of(origin * rows, rows), rows), :]),
                (cpk_ref.at[0], cols_ref.at[origin]),
            )
        ):
            recvs.append(
                pltpu.make_async_remote_copy(
                    src_ref=src,
                    dst_ref=out,
                    send_sem=send_sems.at[k * n + d],
                    recv_sem=recv_sems.at[k * n + d],
                    device_id=(ax, origin),
                    device_id_type=MESH,
                )
            )
    for s in range(n):
        for k, (src, out, target) in enumerate(
            ((last_ref.at[s], before_ref.at[me], up_ax), (first_ref.at[s], after_ref.at[me], down_ax))
        ):
            base = (2 + k) * n
            cp = pltpu.make_async_remote_copy(
                src_ref=src,
                dst_ref=out,
                send_sem=send_sems.at[base + s],
                recv_sem=recv_sems.at[base + me],
                device_id=(target, s),
                device_id_type=MESH,
            )
            cp.start()
            sends.append(cp)
            recvs.append(
                pltpu.make_async_remote_copy(
                    src_ref=src,
                    dst_ref=(before_ref, after_ref)[k].at[s],
                    send_sem=send_sems.at[base + s],
                    recv_sem=recv_sems.at[base + s],
                    device_id=(target, s),
                    device_id_type=MESH,
                )
            )
    local = [
        pltpu.make_async_copy(
            x_ref.at[:, :, pl.ds(pl.multiple_of(me * width, width), width)], dst, local_sems.at[0]
        ),
        pltpu.make_async_copy(cpk_ref.at[me], cols_ref.at[me], local_sems.at[1]),
    ]
    for cp in local:
        cp.start()
    for cp in local:
        cp.wait()
    for cp in recvs:
        cp.wait_recv()
    for cp in sends:
        cp.wait_send()


def from_lines_with_halo(x, cpk, last, first, n):
    comps, rows, around = x.shape
    n_ax = lax.axis_size("ax")
    shapes = [
        (comps, rows * n, around // n),
        cpk.shape,
        (n,) + last.shape[1:],
        (n,) + first.shape[1:],
    ]
    return pl.pallas_call(
        functools.partial(_from_lines_kernel, (n_ax, n)),
        out_shape=[jax.ShapeDtypeStruct(s, x.dtype) for s in shapes],
        in_specs=[pl.BlockSpec(memory_space=pltpu.VMEM)] * 4,
        out_specs=[pl.BlockSpec(memory_space=pltpu.VMEM)] * 4,
        scratch_shapes=[
            pltpu.SemaphoreType.DMA((4 * n,)),
            pltpu.SemaphoreType.DMA((4 * n,)),
            pltpu.SemaphoreType.DMA((2,)),
        ],
        compiler_params=pltpu.CompilerParams(collective_id=2, has_side_effects=True),
    )(x, cpk, last, first)


def _exchange(body, out_shape, cid, n, x):
    return pl.pallas_call(
        functools.partial(body, n),
        out_shape=jax.ShapeDtypeStruct(out_shape, x.dtype),
        in_specs=[pl.BlockSpec(memory_space=pltpu.VMEM)],
        out_specs=pl.BlockSpec(memory_space=pltpu.VMEM),
        scratch_shapes=[
            pltpu.SemaphoreType.DMA((n,)),
            pltpu.SemaphoreType.DMA((n,)),
            pltpu.SemaphoreType.DMA,
        ],
        compiler_params=pltpu.CompilerParams(collective_id=cid, has_side_effects=True),
    )(x)


def to_lines(x, n):
    comps, rows, width = x.shape
    return _exchange(_to_lines_kernel, (comps, rows // n, width * n), 1, n, x)


def dft_table(length):
    half = length // 2
    root = int(round(math.sqrt(length)))
    cols = jnp.concatenate([jnp.arange(half + 1), jnp.arange(1, half)])
    is_sin = jnp.arange(length) > half
    step = 2.0 * math.pi / length
    coarse = (root * jnp.arange(length // root)[:, None] * cols[None, :]) % length
    fine = (jnp.arange(root)[:, None] * cols[None, :]) % length
    coarse_c, coarse_s = jnp.cos(step * coarse.astype(jnp.float32)), jnp.sin(step * coarse.astype(jnp.float32))
    fine_c, fine_s = jnp.cos(step * fine.astype(jnp.float32)), jnp.sin(step * fine.astype(jnp.float32))
    cos_part = coarse_c[:, None] * fine_c[None] - coarse_s[:, None] * fine_s[None]
    sin_part = coarse_s[:, None] * fine_c[None] + coarse_c[:, None] * fine_s[None]
    return jnp.where(is_sin[None, None], sin_part, cos_part).reshape(length, length)


def paired_inverse(precond):
    length = precond.shape[2]
    half = length // 2
    low = precond[:, :, : half + 1]
    mirror = jnp.flip(precond[:, :, half + 1 :], axis=2)
    inner = jnp.concatenate([jnp.zeros_like(low[:, :, :1]), mirror, jnp.zeros_like(low[:, :, :1])], axis=2)
    paired = low + inner
    return jnp.concatenate([paired, paired[:, :, 1:half]], axis=2)


def with_halo(x, sides, width, wrap):
    for axis, dim in sides:
        size, length = (lax.axis_size(axis), x.shape[dim])
        up = [(i, (i + 1) % size) for i in range(size if wrap else size - 1)]
        down = [(j, i) for i, j in up]
        last = lax.slice_in_dim(x, length - width, length, axis=dim)
        first = lax.slice_in_dim(x, 0, width, axis=dim)
        before = lax.ppermute(last, axis, up)
        after = lax.ppermute(first, axis, down)
        x = jnp.concatenate([before, x, after], axis=dim)
    return x


def stencil_from_halo(field, before_row, after_row, before_col, after_col):
    down = jnp.concatenate([field[:, 1:], after_row[:, None]], axis=1)
    up = jnp.concatenate([before_row[:, None], field[:, :-1]], axis=1)
    right = jnp.concatenate([field[:, :, 1:], after_col[:, :, None]], axis=2)
    left = jnp.concatenate([before_col[:, :, None], field[:, :, :-1]], axis=2)
    return down + up + right + left


def swap_channels(field):
    extent = field.shape
    folded = field.reshape((extent[0] // 2, 2) + extent[1:])
    return jnp.flip(folded, axis=1).reshape(extent)


def swap_radial(field):
    extent = field.shape
    folded = field.reshape(extent[0], extent[1] // 2, 2, extent[2])
    return jnp.flip(folded, axis=2).reshape(extent)


def apply_operator(field, stiffness):
    axial_pad = with_halo(field, (("ax", 0),), 1, False)
    sector_pad = with_halo(field, (("sec", 2),), 1, True)
    beside = axial_pad[2:] + axial_pad[:-2]
    beside = beside + sector_pad[:, :, 2:] + sector_pad[:, :, :-2]
    return (stiffness + 4.5) * field - beside - 0.5 * swap_radial(field)


def shards(load, disp, stiff, hole, section_class, class_table, precond):
    slab_count, comp_count, sector_width = disp.shape
    sector_count = lax.axis_size("sec")
    around_cells = sector_width * sector_count
    total_axial = slab_count * lax.axis_size("ax")
    position = lax.axis_index("ax") * slab_count + jnp.arange(slab_count)
    taper = 1.0 + 2.0 * position.astype(jnp.float32) / (total_axial - 1)
    one_hot = (section_class[:, None] == jnp.arange(class_table.shape[0])[None, :]).astype(
        jnp.float32
    )
    factors = jnp.dot(one_hot, class_table, precision=lax.Precision.HIGHEST)
    stiffness = stiff * (factors * taper[:, None])[:, :, None]
    solid = (1 - hole).astype(jnp.float32)[:, None, :]
    residual = solid * (load - apply_operator(disp, stiffness))
    residual_t = jnp.transpose(residual, (1, 0, 2))
    solid_t = jnp.transpose(solid, (1, 0, 2))
    lines_all = to_lines(jnp.concatenate([residual_t, solid_t], axis=0), sector_count)
    lines = lines_all[:comp_count]
    spectrum = jnp.dot(
        lines.reshape(-1, around_cells), dft_table(around_cells), precision=lax.Precision.HIGH
    ).reshape(lines.shape)
    mixed = jnp.sum(paired_inverse(precond)[:, :, None] * spectrum[None], axis=1)
    smoothed_lines = lax.dot_general(
        mixed.reshape(-1, around_cells),
        dft_table(around_cells),
        (((1,), (1,)), ((), ())),
        precision=lax.Precision.HIGH,
    ) / around_cells
    prec_lines = lines_all[comp_count:] * smoothed_lines.reshape(lines.shape)
    group_rows = lines.shape[1]
    lanes = -(-2 * group_rows // 128) * 128
    subl = -(-comp_count // 8) * 8
    edge_b = [(p * sector_width - 1) % around_cells for p in range(sector_count)]
    edge_a = [((p + 1) * sector_width) % around_cells for p in range(sector_count)]
    cols = jnp.concatenate([prec_lines[:, :, edge_b], prec_lines[:, :, edge_a]], axis=1)
    cpk = jnp.pad(
        jnp.transpose(cols.reshape(comp_count, 2 * group_rows, sector_count), (2, 0, 1)),
        ((0, 0), (0, subl - comp_count), (0, lanes - 2 * group_rows)),
    )

    def row_pack(row):
        split = jnp.transpose(row.reshape(comp_count, sector_count, sector_width), (1, 0, 2))
        return jnp.pad(split, ((0, 0), (0, subl - comp_count), (0, 0)))

    prec_t, halo_cols, before_rows, after_rows = from_lines_with_halo(
        prec_lines, cpk, row_pack(prec_lines[:, -1]), row_pack(prec_lines[:, 0]), sector_count
    )
    ax = lax.axis_index("ax")
    before_row = jnp.where(ax == 0, 0.0, before_rows[sector_count - 1, :comp_count])
    after_row = jnp.where(ax == lax.axis_size("ax") - 1, 0.0, after_rows[0, :comp_count])
    got_cols = jnp.transpose(halo_cols[:, :comp_count, : 2 * group_rows], (1, 0, 2))
    got_cols = got_cols.reshape(comp_count, sector_count, 2, group_rows)
    before_col = got_cols[:, :, 0].reshape(comp_count, slab_count)
    after_col = got_cols[:, :, 1].reshape(comp_count, slab_count)
    beside = stencil_from_halo(prec_t, before_row, after_row, before_col, after_col)
    stiffness_t = jnp.transpose(stiffness, (1, 0, 2))
    image_t = solid_t * ((stiffness_t + 4.5) * prec_t - beside - 0.5 * swap_channels(prec_t))
    cell_total = slab_count * lax.axis_size("ax") * comp_count * around_cells
    totals = all_sums(residual_t, prec_t, image_t, 0)[0]
    inner_rz = totals[0] / cell_total
    inner_zq = totals[1] / cell_total
    alpha = inner_rz / inner_zq
    residual_new = residual - alpha * jnp.transpose(image_t, (1, 0, 2))
    square_new = (totals[2] - alpha * (2.0 * totals[3] - alpha * totals[4])) / cell_total
    disp_new = disp + alpha * jnp.transpose(prec_t, (1, 0, 2))
    return (disp_new, residual_new, jnp.stack([inner_rz, inner_zq, square_new]))


def solution(mesh):
    in_specs = (
        P("ax", None, "sec"),
        P("ax", None, "sec"),
        P("ax", None, "sec"),
        P("ax", "sec"),
        P("ax"),
        P(),
        P(),
    )
    out_specs = (P("ax", None, "sec"), P("ax", None, "sec"), P())
    return jax.shard_map(shards, mesh=mesh, in_specs=in_specs, out_specs=out_specs, check_vma=False)
```

```python
import functools
import math

import jax
import jax.numpy as jnp
from jax import lax
from jax.experimental import pallas as pl
from jax.experimental.pallas import tpu as pltpu
from jax.sharding import PartitionSpec as P


MESH = pl.DeviceIdType.MESH


def _groups():
    me_ax = lax.axis_index("ax")
    me_sec = lax.axis_index("sec")
    x = me_ax % 4
    z = (me_ax // 4) % 8
    ylo = me_ax // 32
    core = me_sec % 2
    yhi = me_sec // 2

    def plane_peer(c):
        y = c % 4
        return ((y % 2) * 32 + z * 4 + (c // 4) % 4, (y // 2) * 2 + c // 16)

    return [
        (32, (core * 4 + x) * 4 + yhi * 2 + ylo, plane_peer),
        (8, z, lambda c: (me_ax - z * 4 + c * 4, me_sec)),
    ]


def _local_sums(r_ref, p_ref, i_ref):
    rows = r_ref.shape[0]
    plane = r_ref.shape[1:]

    def body(k, acc):
        r, p, i = r_ref[k], p_ref[k], i_ref[k]
        return (acc[0] + r * p, acc[1] + p * i, acc[2] + r * r, acc[3] + r * i, acc[4] + i * i)

    zero = jnp.zeros(plane, jnp.float32)
    acc = lax.fori_loop(0, rows, body, (zero,) * 5, unroll=8)
    lane = lax.broadcasted_iota(jnp.int32, (8, 128), 1)
    row = lax.broadcasted_iota(jnp.int32, (8, 128), 0)
    packed = jnp.zeros((8, 128), jnp.float32)
    for k, a in enumerate(acc):
        packed = jnp.where((row == 0) & (lane == k), jnp.sum(a), packed)
    return packed


def _ar_kernel(r_ref, p_ref, i_ref, o_ref, recv_a, recv_b, own, send_sems, recv_sems):
    recvs = (recv_a, recv_b)
    groups = _groups()
    for r in recvs:
        r[...] = jnp.zeros_like(r)
    barrier = pltpu.get_barrier_semaphore()
    count = 0
    for n, mine, dev in groups:
        for d in range(1, n):
            pl.semaphore_signal(barrier, inc=1, device_id=dev((mine + d) % n), device_id_type=MESH)
            count += 1
    own[0] = _local_sums(r_ref, p_ref, i_ref)
    pl.semaphore_wait(barrier, count)
    base = 0
    for g, (n, mine, dev) in enumerate(groups):
        src = own.at[g]
        copies = []
        for d in range(1, n):
            cp = pltpu.make_async_remote_copy(
                src_ref=src,
                dst_ref=recvs[g].at[mine],
                send_sem=send_sems.at[base + d],
                recv_sem=recv_sems.at[base + d],
                device_id=dev((mine + d) % n),
                device_id_type=MESH,
            )
            cp.start()
            copies.append(cp)
        mine_val = src[...]
        for cp in copies:
            cp.wait_recv()
        total = None
        for c in range(n):
            v = jnp.where(mine == c, mine_val, recvs[g][c])
            total = v if total is None else total + v
        for cp in copies:
            cp.wait_send()
        base += n
        if g + 1 < len(groups):
            own[g + 1] = total
        else:
            o_ref[...] = total


def all_sums(residual, prec, image, cid):
    return pl.pallas_call(
        _ar_kernel,
        out_shape=jax.ShapeDtypeStruct((8, 128), jnp.float32),
        in_specs=[pl.BlockSpec(memory_space=pltpu.VMEM)] * 3,
        out_specs=pl.BlockSpec(memory_space=pltpu.VMEM),
        scratch_shapes=[
            pltpu.VMEM((32, 8, 128), jnp.float32),
            pltpu.VMEM((8, 8, 128), jnp.float32),
            pltpu.VMEM((2, 8, 128), jnp.float32),
            pltpu.SemaphoreType.DMA((40,)),
            pltpu.SemaphoreType.DMA((40,)),
        ],
        compiler_params=pltpu.CompilerParams(collective_id=cid, has_side_effects=True),
    )(residual, prec, image)


def _to_lines_kernel(n, x_ref, o_ref, send_sems, recv_sems, local_sem):
    me = lax.axis_index("sec")
    ax = lax.axis_index("ax")
    rows, width = o_ref.shape[1], x_ref.shape[2]
    barrier = pltpu.get_barrier_semaphore()
    for d in range(1, n):
        pl.semaphore_signal(barrier, inc=1, device_id=(ax, (me + d) % n), device_id_type=MESH)
    pl.semaphore_wait(barrier, n - 1)
    dst = o_ref.at[:, :, pl.ds(pl.multiple_of(me * width, width), width)]
    copies = []
    for d in range(1, n):
        peer = (me + d) % n
        cp = pltpu.make_async_remote_copy(
            src_ref=x_ref.at[:, pl.ds(pl.multiple_of(peer * rows, rows), rows), :],
            dst_ref=dst,
            send_sem=send_sems.at[d],
            recv_sem=recv_sems.at[d],
            device_id=(ax, peer),
            device_id_type=MESH,
        )
        cp.start()
        copies.append(cp)
    local = pltpu.make_async_copy(
        x_ref.at[:, pl.ds(pl.multiple_of(me * rows, rows), rows), :], dst, local_sem
    )
    local.start()
    local.wait()
    for cp in copies:
        cp.wait()


def _from_lines_kernel(sizes, x_ref, cpk_ref, last_ref, first_ref, o_ref, cols_ref, before_ref,
                       after_ref, send_sems, recv_sems, local_sems):
    n_ax, n = sizes
    me = lax.axis_index("sec")
    ax = lax.axis_index("ax")
    rows, width = x_ref.shape[1], o_ref.shape[2]
    up_ax, down_ax = (ax + 1) % n_ax, (ax + n_ax - 1) % n_ax
    peers = [(ax, (me + d) % n) for d in range(1, n)]
    peers += [(up_ax, s) for s in range(n)] + [(down_ax, s) for s in range(n)]
    barrier = pltpu.get_barrier_semaphore()
    for peer in peers:
        pl.semaphore_signal(barrier, inc=1, device_id=peer, device_id_type=MESH)
    pl.semaphore_wait(barrier, len(peers))
    dst = o_ref.at[:, pl.ds(pl.multiple_of(me * rows, rows), rows), :]
    sends, recvs = [], []
    for d in range(1, n):
        peer = (me + d) % n
        for k, (src, out) in enumerate(
            (
                (x_ref.at[:, :, pl.ds(pl.multiple_of(peer * width, width), width)], dst),
                (cpk_ref.at[peer], cols_ref.at[me]),
            )
        ):
            cp = pltpu.make_async_remote_copy(
                src_ref=src,
                dst_ref=out,
                send_sem=send_sems.at[k * n + d],
                recv_sem=recv_sems.at[k * n + d],
                device_id=(ax, peer),
                device_id_type=MESH,
            )
            cp.start()
            sends.append(cp)
        origin = (me + n - d) % n
        for k, (src, out) in enumerate(
            (
                (x_ref.at[:, :, pl.ds(0, width)], o_ref.at[:, pl.ds(pl.multiple_of(origin * rows, rows), rows), :]),
                (cpk_ref.at[0], cols_ref.at[origin]),
            )
        ):
            recvs.append(
                pltpu.make_async_remote_copy(
                    src_ref=src,
                    dst_ref=out,
                    send_sem=send_sems.at[k * n + d],
                    recv_sem=recv_sems.at[k * n + d],
                    device_id=(ax, origin),
                    device_id_type=MESH,
                )
            )
    for s in range(n):
        for k, (src, out, target) in enumerate(
            ((last_ref.at[s], before_ref.at[me], up_ax), (first_ref.at[s], after_ref.at[me], down_ax))
        ):
            base = (2 + k) * n
            cp = pltpu.make_async_remote_copy(
                src_ref=src,
                dst_ref=out,
                send_sem=send_sems.at[base + s],
                recv_sem=recv_sems.at[base + me],
                device_id=(target, s),
                device_id_type=MESH,
            )
            cp.start()
            sends.append(cp)
            recvs.append(
                pltpu.make_async_remote_copy(
                    src_ref=src,
                    dst_ref=(before_ref, after_ref)[k].at[s],
                    send_sem=send_sems.at[base + s],
                    recv_sem=recv_sems.at[base + s],
                    device_id=(target, s),
                    device_id_type=MESH,
                )
            )
    local = [
        pltpu.make_async_copy(
            x_ref.at[:, :, pl.ds(pl.multiple_of(me * width, width), width)], dst, local_sems.at[0]
        ),
        pltpu.make_async_copy(cpk_ref.at[me], cols_ref.at[me], local_sems.at[1]),
    ]
    for cp in local:
        cp.start()
    for cp in local:
        cp.wait()
    for cp in recvs:
        cp.wait_recv()
    for cp in sends:
        cp.wait_send()


def from_lines_with_halo(x, cpk, last, first, n):
    comps, rows, around = x.shape
    n_ax = lax.axis_size("ax")
    shapes = [
        (comps, rows * n, around // n),
        cpk.shape,
        (n,) + last.shape[1:],
        (n,) + first.shape[1:],
    ]
    return pl.pallas_call(
        functools.partial(_from_lines_kernel, (n_ax, n)),
        out_shape=[jax.ShapeDtypeStruct(s, x.dtype) for s in shapes],
        in_specs=[pl.BlockSpec(memory_space=pltpu.VMEM)] * 4,
        out_specs=[pl.BlockSpec(memory_space=pltpu.VMEM)] * 4,
        scratch_shapes=[
            pltpu.SemaphoreType.DMA((4 * n,)),
            pltpu.SemaphoreType.DMA((4 * n,)),
            pltpu.SemaphoreType.DMA((2,)),
        ],
        compiler_params=pltpu.CompilerParams(collective_id=2, has_side_effects=True),
    )(x, cpk, last, first)


def _exchange(body, out_shape, cid, n, x):
    return pl.pallas_call(
        functools.partial(body, n),
        out_shape=jax.ShapeDtypeStruct(out_shape, x.dtype),
        in_specs=[pl.BlockSpec(memory_space=pltpu.VMEM)],
        out_specs=pl.BlockSpec(memory_space=pltpu.VMEM),
        scratch_shapes=[
            pltpu.SemaphoreType.DMA((n,)),
            pltpu.SemaphoreType.DMA((n,)),
            pltpu.SemaphoreType.DMA,
        ],
        compiler_params=pltpu.CompilerParams(collective_id=cid, has_side_effects=True),
    )(x)


def to_lines(x, n):
    comps, rows, width = x.shape
    return _exchange(_to_lines_kernel, (comps, rows // n, width * n), 1, n, x)


def dft_table(length):
    half = length // 2
    root = int(round(math.sqrt(length)))
    cols = jnp.concatenate([jnp.arange(half + 1), jnp.arange(1, half)])
    phase = jnp.where(jnp.arange(length) > half, 0.5 * math.pi, 0.0).astype(jnp.float32)
    step = 2.0 * math.pi / length
    coarse = step * ((root * jnp.arange(length // root)[:, None] * cols[None, :]) % length).astype(jnp.float32)
    fine = step * ((jnp.arange(root)[:, None] * cols[None, :]) % length).astype(jnp.float32) - phase
    table = jnp.cos(coarse)[:, None] * jnp.cos(fine)[None] - jnp.sin(coarse)[:, None] * jnp.sin(fine)[None]
    return table.reshape(length, length)


def paired_inverse(precond):
    length = precond.shape[2]
    half = length // 2
    low = precond[:, :, : half + 1]
    mirror = jnp.flip(precond[:, :, half + 1 :], axis=2)
    inner = jnp.concatenate([jnp.zeros_like(low[:, :, :1]), mirror, jnp.zeros_like(low[:, :, :1])], axis=2)
    paired = low + inner
    return jnp.concatenate([paired, paired[:, :, 1:half]], axis=2)


def with_halo(x, sides, width, wrap):
    for axis, dim in sides:
        size, length = (lax.axis_size(axis), x.shape[dim])
        up = [(i, (i + 1) % size) for i in range(size if wrap else size - 1)]
        down = [(j, i) for i, j in up]
        last = lax.slice_in_dim(x, length - width, length, axis=dim)
        first = lax.slice_in_dim(x, 0, width, axis=dim)
        before = lax.ppermute(last, axis, up)
        after = lax.ppermute(first, axis, down)
        x = jnp.concatenate([before, x, after], axis=dim)
    return x


def stencil_from_halo(field, before_row, after_row, before_col, after_col):
    down = jnp.concatenate([field[:, 1:], after_row[:, None]], axis=1)
    up = jnp.concatenate([before_row[:, None], field[:, :-1]], axis=1)
    right = jnp.concatenate([field[:, :, 1:], after_col[:, :, None]], axis=2)
    left = jnp.concatenate([before_col[:, :, None], field[:, :, :-1]], axis=2)
    return down + up + right + left


def swap_channels(field):
    extent = field.shape
    folded = field.reshape((extent[0] // 2, 2) + extent[1:])
    return jnp.flip(folded, axis=1).reshape(extent)


def swap_radial(field):
    extent = field.shape
    folded = field.reshape(extent[0], extent[1] // 2, 2, extent[2])
    return jnp.flip(folded, axis=2).reshape(extent)


def apply_operator(field, stiffness):
    axial_pad = with_halo(field, (("ax", 0),), 1, False)
    sector_pad = with_halo(field, (("sec", 2),), 1, True)
    beside = axial_pad[2:] + axial_pad[:-2]
    beside = beside + sector_pad[:, :, 2:] + sector_pad[:, :, :-2]
    return (stiffness + 4.5) * field - beside - 0.5 * swap_radial(field)


def shards(load, disp, stiff, hole, section_class, class_table, precond):
    slab_count, comp_count, sector_width = disp.shape
    sector_count = lax.axis_size("sec")
    around_cells = sector_width * sector_count
    total_axial = slab_count * lax.axis_size("ax")
    position = lax.axis_index("ax") * slab_count + jnp.arange(slab_count)
    taper = 1.0 + 2.0 * position.astype(jnp.float32) / (total_axial - 1)
    one_hot = (section_class[:, None] == jnp.arange(class_table.shape[0])[None, :]).astype(
        jnp.float32
    )
    factors = jnp.dot(one_hot, class_table, precision=lax.Precision.HIGHEST)
    stiffness = stiff * (factors * taper[:, None])[:, :, None]
    solid = (1 - hole).astype(jnp.float32)[:, None, :]
    residual = solid * (load - apply_operator(disp, stiffness))
    residual_t = jnp.transpose(residual, (1, 0, 2))
    solid_t = jnp.transpose(solid, (1, 0, 2))
    lines_all = to_lines(jnp.concatenate([residual_t, solid_t], axis=0), sector_count)
    lines = lines_all[:comp_count]
    spectrum = jnp.dot(
        lines.reshape(-1, around_cells), dft_table(around_cells), precision=lax.Precision.HIGH
    ).reshape(lines.shape)
    mixed = jnp.sum(paired_inverse(precond)[:, :, None] * spectrum[None], axis=1)
    smoothed_lines = lax.dot_general(
        mixed.reshape(-1, around_cells),
        dft_table(around_cells),
        (((1,), (1,)), ((), ())),
        precision=lax.Precision.HIGH,
    ) / around_cells
    prec_lines = lines_all[comp_count:] * smoothed_lines.reshape(lines.shape)
    group_rows = lines.shape[1]
    lanes = -(-2 * group_rows // 128) * 128
    subl = -(-comp_count // 8) * 8
    blocks = prec_lines.reshape(comp_count, group_rows, sector_count, sector_width)
    cols = jnp.concatenate(
        [jnp.roll(blocks[..., -1], 1, axis=2), jnp.roll(blocks[..., 0], -1, axis=2)], axis=1
    )
    cpk = jnp.pad(
        jnp.transpose(cols.reshape(comp_count, 2 * group_rows, sector_count), (2, 0, 1)),
        ((0, 0), (0, subl - comp_count), (0, lanes - 2 * group_rows)),
    )

    def row_pack(row):
        split = jnp.transpose(row.reshape(comp_count, sector_count, sector_width), (1, 0, 2))
        return jnp.pad(split, ((0, 0), (0, subl - comp_count), (0, 0)))

    prec_t, halo_cols, before_rows, after_rows = from_lines_with_halo(
        prec_lines, cpk, row_pack(prec_lines[:, -1]), row_pack(prec_lines[:, 0]), sector_count
    )
    ax = lax.axis_index("ax")
    before_row = jnp.where(ax == 0, 0.0, before_rows[sector_count - 1, :comp_count])
    after_row = jnp.where(ax == lax.axis_size("ax") - 1, 0.0, after_rows[0, :comp_count])
    got_cols = jnp.transpose(halo_cols[:, :comp_count, : 2 * group_rows], (1, 0, 2))
    got_cols = got_cols.reshape(comp_count, sector_count, 2, group_rows)
    before_col = got_cols[:, :, 0].reshape(comp_count, slab_count)
    after_col = got_cols[:, :, 1].reshape(comp_count, slab_count)
    beside = stencil_from_halo(prec_t, before_row, after_row, before_col, after_col)
    stiffness_t = jnp.transpose(stiffness, (1, 0, 2))
    image_t = solid_t * ((stiffness_t + 4.5) * prec_t - beside - 0.5 * swap_channels(prec_t))
    cell_total = slab_count * lax.axis_size("ax") * comp_count * around_cells
    totals = all_sums(residual_t, prec_t, image_t, 0)[0]
    inner_rz = totals[0] / cell_total
    inner_zq = totals[1] / cell_total
    alpha = inner_rz / inner_zq
    residual_new = residual - alpha * jnp.transpose(image_t, (1, 0, 2))
    square_new = (totals[2] - alpha * (2.0 * totals[3] - alpha * totals[4])) / cell_total
    disp_new = disp + alpha * jnp.transpose(prec_t, (1, 0, 2))
    return (disp_new, residual_new, jnp.stack([inner_rz, inner_zq, square_new]))


def solution(mesh):
    in_specs = (
        P("ax", None, "sec"),
        P("ax", None, "sec"),
        P("ax", None, "sec"),
        P("ax", "sec"),
        P("ax"),
        P(),
        P(),
    )
    out_specs = (P("ax", None, "sec"), P("ax", None, "sec"), P())
    return jax.shard_map(shards, mesh=mesh, in_specs=in_specs, out_specs=out_specs, check_vma=False)
```

```python
import functools
import math

import jax
import jax.numpy as jnp
from jax import lax
from jax.experimental import pallas as pl
from jax.experimental.pallas import tpu as pltpu
from jax.sharding import PartitionSpec as P


MESH = pl.DeviceIdType.MESH


def _groups():
    me_ax = lax.axis_index("ax")
    me_sec = lax.axis_index("sec")
    x = me_ax % 4
    z = (me_ax // 4) % 8
    ylo = me_ax // 32
    core = me_sec % 2
    yhi = me_sec // 2

    def plane_peer(c):
        y = c % 4
        return ((y % 2) * 32 + z * 4 + (c // 4) % 4, (y // 2) * 2 + c // 16)

    return [
        (32, (core * 4 + x) * 4 + yhi * 2 + ylo, plane_peer),
        (8, z, lambda c: (me_ax - z * 4 + c * 4, me_sec)),
    ]


def _local_sums(r_ref, p_ref, i_ref):
    rows = r_ref.shape[0]
    plane = r_ref.shape[1:]

    def body(k, acc):
        r, p, i = r_ref[k], p_ref[k], i_ref[k]
        return (acc[0] + r * p, acc[1] + p * i, acc[2] + r * r, acc[3] + r * i, acc[4] + i * i)

    zero = jnp.zeros(plane, jnp.float32)
    acc = lax.fori_loop(0, rows, body, (zero,) * 5, unroll=8)
    lane = lax.broadcasted_iota(jnp.int32, (8, 128), 1)
    row = lax.broadcasted_iota(jnp.int32, (8, 128), 0)
    packed = jnp.zeros((8, 128), jnp.float32)
    for k, a in enumerate(acc):
        packed = jnp.where((row == 0) & (lane == k), jnp.sum(a), packed)
    return packed


def _finish(total, cell_total):
    lane = lax.broadcasted_iota(jnp.int32, total.shape, 1)
    row = lax.broadcasted_iota(jnp.int32, total.shape, 0)

    def pick(k):
        return jnp.sum(jnp.where((row == 0) & (lane == k), total, 0.0), keepdims=True)

    inner_rz = pick(0) / cell_total
    inner_zq = pick(1) / cell_total
    alpha = inner_rz / inner_zq
    square_new = (pick(2) - alpha * (2.0 * pick(3) - alpha * pick(4))) / cell_total
    out = jnp.zeros(total.shape, jnp.float32)
    for k, v in enumerate((alpha, inner_rz, inner_zq, square_new)):
        out = jnp.where((row == 0) & (lane == k), v, out)
    return out


def _ar_kernel(cell_total, r_ref, p_ref, i_ref, o_ref, recv_a, recv_b, own, send_sems, recv_sems):
    recvs = (recv_a, recv_b)
    groups = _groups()
    for r in recvs:
        r[...] = jnp.zeros_like(r)
    barrier = pltpu.get_barrier_semaphore()
    count = 0
    for n, mine, dev in groups:
        for d in range(1, n):
            pl.semaphore_signal(barrier, inc=1, device_id=dev((mine + d) % n), device_id_type=MESH)
            count += 1
    own[0] = _local_sums(r_ref, p_ref, i_ref)
    pl.semaphore_wait(barrier, count)
    base = 0
    for g, (n, mine, dev) in enumerate(groups):
        src = own.at[g]
        copies = []
        for d in range(1, n):
            cp = pltpu.make_async_remote_copy(
                src_ref=src,
                dst_ref=recvs[g].at[mine],
                send_sem=send_sems.at[base + d],
                recv_sem=recv_sems.at[base + d],
                device_id=dev((mine + d) % n),
                device_id_type=MESH,
            )
            cp.start()
            copies.append(cp)
        mine_val = src[...]
        for cp in copies:
            cp.wait_recv()
        total = None
        for c in range(n):
            v = jnp.where(mine == c, mine_val, recvs[g][c])
            total = v if total is None else total + v
        for cp in copies:
            cp.wait_send()
        base += n
        if g + 1 < len(groups):
            own[g + 1] = total
        else:
            o_ref[...] = _finish(total, cell_total)


def all_sums(residual, prec, image, cell_total, cid):
    return pl.pallas_call(
        functools.partial(_ar_kernel, float(cell_total)),
        out_shape=jax.ShapeDtypeStruct((8, 128), jnp.float32),
        in_specs=[pl.BlockSpec(memory_space=pltpu.VMEM)] * 3,
        out_specs=pl.BlockSpec(memory_space=pltpu.VMEM),
        scratch_shapes=[
            pltpu.VMEM((32, 8, 128), jnp.float32),
            pltpu.VMEM((8, 8, 128), jnp.float32),
            pltpu.VMEM((2, 8, 128), jnp.float32),
            pltpu.SemaphoreType.DMA((40,)),
            pltpu.SemaphoreType.DMA((40,)),
        ],
        compiler_params=pltpu.CompilerParams(collective_id=cid, has_side_effects=True),
    )(residual, prec, image)


def _to_lines_kernel(n, x_ref, o_ref, send_sems, recv_sems, local_sem):
    me = lax.axis_index("sec")
    ax = lax.axis_index("ax")
    rows, width = o_ref.shape[1], x_ref.shape[2]
    barrier = pltpu.get_barrier_semaphore()
    for d in range(1, n):
        pl.semaphore_signal(barrier, inc=1, device_id=(ax, (me + d) % n), device_id_type=MESH)
    pl.semaphore_wait(barrier, n - 1)
    dst = o_ref.at[:, :, pl.ds(pl.multiple_of(me * width, width), width)]
    copies = []
    for d in range(1, n):
        peer = (me + d) % n
        cp = pltpu.make_async_remote_copy(
            src_ref=x_ref.at[:, pl.ds(pl.multiple_of(peer * rows, rows), rows), :],
            dst_ref=dst,
            send_sem=send_sems.at[d],
            recv_sem=recv_sems.at[d],
            device_id=(ax, peer),
            device_id_type=MESH,
        )
        cp.start()
        copies.append(cp)
    local = pltpu.make_async_copy(
        x_ref.at[:, pl.ds(pl.multiple_of(me * rows, rows), rows), :], dst, local_sem
    )
    local.start()
    local.wait()
    for cp in copies:
        cp.wait()


def _from_lines_kernel(sizes, x_ref, cpk_ref, last_ref, first_ref, o_ref, cols_ref, before_ref,
                       after_ref, send_sems, recv_sems, local_sems):
    n_ax, n = sizes
    me = lax.axis_index("sec")
    ax = lax.axis_index("ax")
    rows, width = x_ref.shape[1], o_ref.shape[2]
    up_ax, down_ax = (ax + 1) % n_ax, (ax + n_ax - 1) % n_ax
    peers = [(ax, (me + d) % n) for d in range(1, n)]
    peers += [(up_ax, s) for s in range(n)] + [(down_ax, s) for s in range(n)]
    barrier = pltpu.get_barrier_semaphore()
    for peer in peers:
        pl.semaphore_signal(barrier, inc=1, device_id=peer, device_id_type=MESH)
    pl.semaphore_wait(barrier, len(peers))
    dst = o_ref.at[:, pl.ds(pl.multiple_of(me * rows, rows), rows), :]
    sends, recvs = [], []
    for d in range(1, n):
        peer = (me + d) % n
        for k, (src, out) in enumerate(
            (
                (x_ref.at[:, :, pl.ds(pl.multiple_of(peer * width, width), width)], dst),
                (cpk_ref.at[peer], cols_ref.at[me]),
            )
        ):
            cp = pltpu.make_async_remote_copy(
                src_ref=src,
                dst_ref=out,
                send_sem=send_sems.at[k * n + d],
                recv_sem=recv_sems.at[k * n + d],
                device_id=(ax, peer),
                device_id_type=MESH,
            )
            cp.start()
            sends.append(cp)
        origin = (me + n - d) % n
        for k, (src, out) in enumerate(
            (
                (x_ref.at[:, :, pl.ds(0, width)], o_ref.at[:, pl.ds(pl.multiple_of(origin * rows, rows), rows), :]),
                (cpk_ref.at[0], cols_ref.at[origin]),
            )
        ):
            recvs.append(
                pltpu.make_async_remote_copy(
                    src_ref=src,
                    dst_ref=out,
                    send_sem=send_sems.at[k * n + d],
                    recv_sem=recv_sems.at[k * n + d],
                    device_id=(ax, origin),
                    device_id_type=MESH,
                )
            )
    for s in range(n):
        for k, (src, out, target) in enumerate(
            ((last_ref.at[s], before_ref.at[me], up_ax), (first_ref.at[s], after_ref.at[me], down_ax))
        ):
            base = (2 + k) * n
            cp = pltpu.make_async_remote_copy(
                src_ref=src,
                dst_ref=out,
                send_sem=send_sems.at[base + s],
                recv_sem=recv_sems.at[base + me],
                device_id=(target, s),
                device_id_type=MESH,
            )
            cp.start()
            sends.append(cp)
            recvs.append(
                pltpu.make_async_remote_copy(
                    src_ref=src,
                    dst_ref=(before_ref, after_ref)[k].at[s],
                    send_sem=send_sems.at[base + s],
                    recv_sem=recv_sems.at[base + s],
                    device_id=(target, s),
                    device_id_type=MESH,
                )
            )
    local = [
        pltpu.make_async_copy(
            x_ref.at[:, :, pl.ds(pl.multiple_of(me * width, width), width)], dst, local_sems.at[0]
        ),
        pltpu.make_async_copy(cpk_ref.at[me], cols_ref.at[me], local_sems.at[1]),
    ]
    for cp in local:
        cp.start()
    for cp in local:
        cp.wait()
    for cp in recvs:
        cp.wait_recv()
    for cp in sends:
        cp.wait_send()


def from_lines_with_halo(x, cpk, last, first, n):
    comps, rows, around = x.shape
    n_ax = lax.axis_size("ax")
    shapes = [
        (comps, rows * n, around // n),
        cpk.shape,
        (n,) + last.shape[1:],
        (n,) + first.shape[1:],
    ]
    return pl.pallas_call(
        functools.partial(_from_lines_kernel, (n_ax, n)),
        out_shape=[jax.ShapeDtypeStruct(s, x.dtype) for s in shapes],
        in_specs=[pl.BlockSpec(memory_space=pltpu.VMEM)] * 4,
        out_specs=[pl.BlockSpec(memory_space=pltpu.VMEM)] * 4,
        scratch_shapes=[
            pltpu.SemaphoreType.DMA((4 * n,)),
            pltpu.SemaphoreType.DMA((4 * n,)),
            pltpu.SemaphoreType.DMA((2,)),
        ],
        compiler_params=pltpu.CompilerParams(collective_id=2, has_side_effects=True),
    )(x, cpk, last, first)


def _exchange(body, out_shape, cid, n, x):
    return pl.pallas_call(
        functools.partial(body, n),
        out_shape=jax.ShapeDtypeStruct(out_shape, x.dtype),
        in_specs=[pl.BlockSpec(memory_space=pltpu.VMEM)],
        out_specs=pl.BlockSpec(memory_space=pltpu.VMEM),
        scratch_shapes=[
            pltpu.SemaphoreType.DMA((n,)),
            pltpu.SemaphoreType.DMA((n,)),
            pltpu.SemaphoreType.DMA,
        ],
        compiler_params=pltpu.CompilerParams(collective_id=cid, has_side_effects=True),
    )(x)


def to_lines(x, n):
    comps, rows, width = x.shape
    return _exchange(_to_lines_kernel, (comps, rows // n, width * n), 1, n, x)


def dft_table(length):
    half = length // 2
    root = int(round(math.sqrt(length)))
    cols = jnp.concatenate([jnp.arange(half + 1), jnp.arange(1, half)])
    phase = jnp.where(jnp.arange(length) > half, 0.5 * math.pi, 0.0).astype(jnp.float32)
    step = 2.0 * math.pi / length
    coarse = step * ((root * jnp.arange(length // root)[:, None] * cols[None, :]) % length).astype(jnp.float32)
    fine = step * ((jnp.arange(root)[:, None] * cols[None, :]) % length).astype(jnp.float32) - phase
    table = jnp.cos(coarse)[:, None] * jnp.cos(fine)[None] - jnp.sin(coarse)[:, None] * jnp.sin(fine)[None]
    return table.reshape(length, length)


def paired_inverse(precond):
    length = precond.shape[2]
    half = length // 2
    low = precond[:, :, : half + 1]
    mirror = jnp.flip(precond[:, :, half + 1 :], axis=2)
    inner = jnp.concatenate([jnp.zeros_like(low[:, :, :1]), mirror, jnp.zeros_like(low[:, :, :1])], axis=2)
    paired = low + inner
    return jnp.concatenate([paired, paired[:, :, 1:half]], axis=2)


def with_halo(x, sides, width, wrap):
    for axis, dim in sides:
        size, length = (lax.axis_size(axis), x.shape[dim])
        up = [(i, (i + 1) % size) for i in range(size if wrap else size - 1)]
        down = [(j, i) for i, j in up]
        last = lax.slice_in_dim(x, length - width, length, axis=dim)
        first = lax.slice_in_dim(x, 0, width, axis=dim)
        before = lax.ppermute(last, axis, up)
        after = lax.ppermute(first, axis, down)
        x = jnp.concatenate([before, x, after], axis=dim)
    return x


def stencil_from_halo(field, before_row, after_row, before_col, after_col):
    down = jnp.concatenate([field[:, 1:], after_row[:, None]], axis=1)
    up = jnp.concatenate([before_row[:, None], field[:, :-1]], axis=1)
    right = jnp.concatenate([field[:, :, 1:], after_col[:, :, None]], axis=2)
    left = jnp.concatenate([before_col[:, :, None], field[:, :, :-1]], axis=2)
    return down + up + right + left


def swap_channels(field):
    extent = field.shape
    folded = field.reshape((extent[0] // 2, 2) + extent[1:])
    return jnp.flip(folded, axis=1).reshape(extent)


def swap_radial(field):
    extent = field.shape
    folded = field.reshape(extent[0], extent[1] // 2, 2, extent[2])
    return jnp.flip(folded, axis=2).reshape(extent)


def apply_operator(field, stiffness):
    axial_pad = with_halo(field, (("ax", 0),), 1, False)
    sector_pad = with_halo(field, (("sec", 2),), 1, True)
    beside = axial_pad[2:] + axial_pad[:-2]
    beside = beside + sector_pad[:, :, 2:] + sector_pad[:, :, :-2]
    return (stiffness + 4.5) * field - beside - 0.5 * swap_radial(field)


def shards(load, disp, stiff, hole, section_class, class_table, precond):
    slab_count, comp_count, sector_width = disp.shape
    sector_count = lax.axis_size("sec")
    around_cells = sector_width * sector_count
    total_axial = slab_count * lax.axis_size("ax")
    position = lax.axis_index("ax") * slab_count + jnp.arange(slab_count)
    taper = 1.0 + 2.0 * position.astype(jnp.float32) / (total_axial - 1)
    one_hot = (section_class[:, None] == jnp.arange(class_table.shape[0])[None, :]).astype(
        jnp.float32
    )
    factors = jnp.dot(one_hot, class_table, precision=lax.Precision.HIGHEST)
    stiffness = stiff * (factors * taper[:, None])[:, :, None]
    solid = (1 - hole).astype(jnp.float32)[:, None, :]
    residual = solid * (load - apply_operator(disp, stiffness))
    residual_t = jnp.transpose(residual, (1, 0, 2))
    solid_t = jnp.transpose(solid, (1, 0, 2))
    lines_all = to_lines(jnp.concatenate([residual_t, solid_t], axis=0), sector_count)
    lines = lines_all[:comp_count]
    spectrum = jnp.dot(
        lines.reshape(-1, around_cells), dft_table(around_cells), precision=lax.Precision.HIGH
    ).reshape(lines.shape)
    mixed = jnp.sum(paired_inverse(precond)[:, :, None] * spectrum[None], axis=1)
    smoothed_lines = lax.dot_general(
        mixed.reshape(-1, around_cells),
        dft_table(around_cells),
        (((1,), (1,)), ((), ())),
        precision=lax.Precision.HIGH,
    ) / around_cells
    prec_lines = lines_all[comp_count:] * smoothed_lines.reshape(lines.shape)
    group_rows = lines.shape[1]
    lanes = -(-2 * group_rows // 128) * 128
    subl = -(-comp_count // 8) * 8
    edge_at = [(p * sector_width - 1) % around_cells for p in range(sector_count)]
    edge_at += [((p + 1) * sector_width) % around_cells for p in range(sector_count)]
    pick = (jnp.arange(around_cells)[None, :] == jnp.array(edge_at)[:, None]).astype(jnp.float32)
    edges = lax.dot_general(
        pick,
        prec_lines.reshape(-1, around_cells),
        (((1,), (1,)), ((), ())),
        precision=lax.Precision.HIGHEST,
    ).reshape(2, sector_count, comp_count, group_rows)
    cpk = jnp.pad(
        jnp.transpose(edges, (1, 2, 0, 3)).reshape(sector_count, comp_count, 2 * group_rows),
        ((0, 0), (0, subl - comp_count), (0, lanes - 2 * group_rows)),
    )

    def row_pack(row):
        split = jnp.transpose(row.reshape(comp_count, sector_count, sector_width), (1, 0, 2))
        return jnp.pad(split, ((0, 0), (0, subl - comp_count), (0, 0)))

    prec_t, halo_cols, before_rows, after_rows = from_lines_with_halo(
        prec_lines, cpk, row_pack(prec_lines[:, -1]), row_pack(prec_lines[:, 0]), sector_count
    )
    ax = lax.axis_index("ax")
    before_row = jnp.where(ax == 0, 0.0, before_rows[sector_count - 1, :comp_count])
    after_row = jnp.where(ax == lax.axis_size("ax") - 1, 0.0, after_rows[0, :comp_count])
    got_cols = jnp.transpose(halo_cols[:, :comp_count, : 2 * group_rows], (1, 0, 2))
    got_cols = got_cols.reshape(comp_count, sector_count, 2, group_rows)
    before_col = got_cols[:, :, 0].reshape(comp_count, slab_count)
    after_col = got_cols[:, :, 1].reshape(comp_count, slab_count)
    beside = stencil_from_halo(prec_t, before_row, after_row, before_col, after_col)
    stiffness_t = jnp.transpose(stiffness, (1, 0, 2))
    image_t = solid_t * ((stiffness_t + 4.5) * prec_t - beside - 0.5 * swap_channels(prec_t))
    cell_total = slab_count * lax.axis_size("ax") * comp_count * around_cells
    finished = all_sums(residual_t, prec_t, image_t, cell_total, 0)[0]
    alpha = finished[0]
    residual_new = residual - alpha * jnp.transpose(image_t, (1, 0, 2))
    disp_new = disp + alpha * jnp.transpose(prec_t, (1, 0, 2))
    return (disp_new, residual_new, finished[1:4])


def solution(mesh):
    in_specs = (
        P("ax", None, "sec"),
        P("ax", None, "sec"),
        P("ax", None, "sec"),
        P("ax", "sec"),
        P("ax"),
        P(),
        P(),
    )
    out_specs = (P("ax", None, "sec"), P("ax", None, "sec"), P())
    return jax.shard_map(shards, mesh=mesh, in_specs=in_specs, out_specs=out_specs, check_vma=False)
```

```python
import functools
import math

import jax
import jax.numpy as jnp
from jax import lax
from jax.experimental import pallas as pl
from jax.experimental.pallas import tpu as pltpu
from jax.sharding import PartitionSpec as P


MESH = pl.DeviceIdType.MESH


def _groups():
    me_ax = lax.axis_index("ax")
    me_sec = lax.axis_index("sec")
    x = me_ax % 4
    z = (me_ax // 4) % 8
    ylo = me_ax // 32
    core = me_sec % 2
    yhi = me_sec // 2

    def plane_peer(c):
        y = c % 4
        return ((y % 2) * 32 + z * 4 + (c // 4) % 4, (y // 2) * 2 + c // 16)

    return [
        (32, (core * 4 + x) * 4 + yhi * 2 + ylo, plane_peer),
        (8, z, lambda c: (me_ax - z * 4 + c * 4, me_sec)),
    ]


def _image_and_sums(r_ref, p_ref, s_ref, m_ref, hr_ref, hc_ref, img_ref):
    comps, rows, width = p_ref.shape
    row = lax.broadcasted_iota(jnp.int32, (rows, width), 0)
    lane = lax.broadcasted_iota(jnp.int32, (rows, width), 1)
    solid = m_ref[...]
    acc = [jnp.zeros((1, width), jnp.float32) for _ in range(5)]
    for q in range(comps):
        field = p_ref[q]
        up = jnp.where(row == 0, hr_ref[0, q : q + 1, :], pltpu.roll(field, 1, 0))
        down = jnp.where(row == rows - 1, hr_ref[1, q : q + 1, :], pltpu.roll(field, rows - 1, 0))
        left = jnp.where(lane == 0, hc_ref[0, q], pltpu.roll(field, 1, 1))
        right = jnp.where(lane == width - 1, hc_ref[1, q], pltpu.roll(field, width - 1, 1))
        beside = down + up + right + left
        image = solid * ((s_ref[q] + 4.5) * field - beside - 0.5 * p_ref[q ^ 1])
        img_ref[q] = image
        res = r_ref[q]
        for k, prod in enumerate((res * field, field * image, res * res, res * image, image * image)):
            acc[k] = acc[k] + jnp.sum(prod, axis=0, keepdims=True)
    lane8 = lax.broadcasted_iota(jnp.int32, (8, 128), 1)
    row8 = lax.broadcasted_iota(jnp.int32, (8, 128), 0)
    packed = jnp.zeros((8, 128), jnp.float32)
    for k, a in enumerate(acc):
        packed = jnp.where((row8 == 0) & (lane8 == k), jnp.sum(a), packed)
    return packed


def _finish(total, cell_total):
    lane = lax.broadcasted_iota(jnp.int32, total.shape, 1)
    row = lax.broadcasted_iota(jnp.int32, total.shape, 0)

    def pick(k):
        return jnp.sum(jnp.where((row == 0) & (lane == k), total, 0.0), keepdims=True)

    inner_rz = pick(0) / cell_total
    inner_zq = pick(1) / cell_total
    alpha = inner_rz / inner_zq
    square_new = (pick(2) - alpha * (2.0 * pick(3) - alpha * pick(4))) / cell_total
    out = jnp.zeros(total.shape, jnp.float32)
    for k, v in enumerate((alpha, inner_rz, inner_zq, square_new)):
        out = jnp.where((row == 0) & (lane == k), v, out)
    return out


def _ar_kernel(cell_total, r_ref, p_ref, s_ref, m_ref, hr_ref, hc_ref, o_ref, img_ref, recv_a, recv_b, own, send_sems, recv_sems):
    recvs = (recv_a, recv_b)
    groups = _groups()
    for r in recvs:
        r[...] = jnp.zeros_like(r)
    barrier = pltpu.get_barrier_semaphore()
    count = 0
    for n, mine, dev in groups:
        for d in range(1, n):
            pl.semaphore_signal(barrier, inc=1, device_id=dev((mine + d) % n), device_id_type=MESH)
            count += 1
    own[0] = _image_and_sums(r_ref, p_ref, s_ref, m_ref, hr_ref, hc_ref, img_ref)
    pl.semaphore_wait(barrier, count)
    base = 0
    for g, (n, mine, dev) in enumerate(groups):
        src = own.at[g]
        copies = []
        for d in range(1, n):
            cp = pltpu.make_async_remote_copy(
                src_ref=src,
                dst_ref=recvs[g].at[mine],
                send_sem=send_sems.at[base + d],
                recv_sem=recv_sems.at[base + d],
                device_id=dev((mine + d) % n),
                device_id_type=MESH,
            )
            cp.start()
            copies.append(cp)
        mine_val = src[...]
        for cp in copies:
            cp.wait_recv()
        total = None
        for c in range(n):
            v = jnp.where(mine == c, mine_val, recvs[g][c])
            total = v if total is None else total + v
        for cp in copies:
            cp.wait_send()
        base += n
        if g + 1 < len(groups):
            own[g + 1] = total
        else:
            o_ref[...] = _finish(total, cell_total)


def image_and_totals(residual, prec, stiffness, solid, halo_rows, halo_cols, cell_total, cid):
    return pl.pallas_call(
        functools.partial(_ar_kernel, float(cell_total)),
        out_shape=[
            jax.ShapeDtypeStruct((8, 128), jnp.float32),
            jax.ShapeDtypeStruct(prec.shape, jnp.float32),
        ],
        in_specs=[pl.BlockSpec(memory_space=pltpu.VMEM)] * 6,
        out_specs=[pl.BlockSpec(memory_space=pltpu.VMEM)] * 2,
        scratch_shapes=[
            pltpu.VMEM((32, 8, 128), jnp.float32),
            pltpu.VMEM((8, 8, 128), jnp.float32),
            pltpu.VMEM((2, 8, 128), jnp.float32),
            pltpu.SemaphoreType.DMA((40,)),
            pltpu.SemaphoreType.DMA((40,)),
        ],
        compiler_params=pltpu.CompilerParams(collective_id=cid, has_side_effects=True),
    )(residual, prec, stiffness, solid, halo_rows, halo_cols)


def _to_lines_kernel(n, x_ref, o_ref, send_sems, recv_sems, local_sem):
    me = lax.axis_index("sec")
    ax = lax.axis_index("ax")
    rows, width = o_ref.shape[1], x_ref.shape[2]
    barrier = pltpu.get_barrier_semaphore()
    for d in range(1, n):
        pl.semaphore_signal(barrier, inc=1, device_id=(ax, (me + d) % n), device_id_type=MESH)
    pl.semaphore_wait(barrier, n - 1)
    dst = o_ref.at[:, :, pl.ds(pl.multiple_of(me * width, width), width)]
    copies = []
    for d in range(1, n):
        peer = (me + d) % n
        cp = pltpu.make_async_remote_copy(
            src_ref=x_ref.at[:, pl.ds(pl.multiple_of(peer * rows, rows), rows), :],
            dst_ref=dst,
            send_sem=send_sems.at[d],
            recv_sem=recv_sems.at[d],
            device_id=(ax, peer),
            device_id_type=MESH,
        )
        cp.start()
        copies.append(cp)
    local = pltpu.make_async_copy(
        x_ref.at[:, pl.ds(pl.multiple_of(me * rows, rows), rows), :], dst, local_sem
    )
    local.start()
    local.wait()
    for cp in copies:
        cp.wait()


def _from_lines_kernel(sizes, x_ref, cpk_ref, last_ref, first_ref, o_ref, cols_ref, before_ref,
                       after_ref, send_sems, recv_sems, local_sems):
    n_ax, n = sizes
    me = lax.axis_index("sec")
    ax = lax.axis_index("ax")
    rows, width = x_ref.shape[1], o_ref.shape[2]
    up_ax, down_ax = (ax + 1) % n_ax, (ax + n_ax - 1) % n_ax
    peers = [(ax, (me + d) % n) for d in range(1, n)]
    peers += [(up_ax, s) for s in range(n)] + [(down_ax, s) for s in range(n)]
    barrier = pltpu.get_barrier_semaphore()
    for peer in peers:
        pl.semaphore_signal(barrier, inc=1, device_id=peer, device_id_type=MESH)
    pl.semaphore_wait(barrier, len(peers))
    dst = o_ref.at[:, pl.ds(pl.multiple_of(me * rows, rows), rows), :]
    sends, recvs = [], []
    for d in range(1, n):
        peer = (me + d) % n
        for k, (src, out) in enumerate(
            (
                (x_ref.at[:, :, pl.ds(pl.multiple_of(peer * width, width), width)], dst),
                (cpk_ref.at[peer], cols_ref.at[me]),
            )
        ):
            cp = pltpu.make_async_remote_copy(
                src_ref=src,
                dst_ref=out,
                send_sem=send_sems.at[k * n + d],
                recv_sem=recv_sems.at[k * n + d],
                device_id=(ax, peer),
                device_id_type=MESH,
            )
            cp.start()
            sends.append(cp)
        origin = (me + n - d) % n
        for k, (src, out) in enumerate(
            (
                (x_ref.at[:, :, pl.ds(0, width)], o_ref.at[:, pl.ds(pl.multiple_of(origin * rows, rows), rows), :]),
                (cpk_ref.at[0], cols_ref.at[origin]),
            )
        ):
            recvs.append(
                pltpu.make_async_remote_copy(
                    src_ref=src,
                    dst_ref=out,
                    send_sem=send_sems.at[k * n + d],
                    recv_sem=recv_sems.at[k * n + d],
                    device_id=(ax, origin),
                    device_id_type=MESH,
                )
            )
    for s in range(n):
        for k, (src, out, target) in enumerate(
            ((last_ref.at[s], before_ref.at[me], up_ax), (first_ref.at[s], after_ref.at[me], down_ax))
        ):
            base = (2 + k) * n
            cp = pltpu.make_async_remote_copy(
                src_ref=src,
                dst_ref=out,
                send_sem=send_sems.at[base + s],
                recv_sem=recv_sems.at[base + me],
                device_id=(target, s),
                device_id_type=MESH,
            )
            cp.start()
            sends.append(cp)
            recvs.append(
                pltpu.make_async_remote_copy(
                    src_ref=src,
                    dst_ref=(before_ref, after_ref)[k].at[s],
                    send_sem=send_sems.at[base + s],
                    recv_sem=recv_sems.at[base + s],
                    device_id=(target, s),
                    device_id_type=MESH,
                )
            )
    local = [
        pltpu.make_async_copy(
            x_ref.at[:, :, pl.ds(pl.multiple_of(me * width, width), width)], dst, local_sems.at[0]
        ),
        pltpu.make_async_copy(cpk_ref.at[me], cols_ref.at[me], local_sems.at[1]),
    ]
    for cp in local:
        cp.start()
    for cp in local:
        cp.wait()
    for cp in recvs:
        cp.wait_recv()
    for cp in sends:
        cp.wait_send()


def from_lines_with_halo(x, cpk, last, first, n):
    comps, rows, around = x.shape
    n_ax = lax.axis_size("ax")
    shapes = [
        (comps, rows * n, around // n),
        cpk.shape,
        (n,) + last.shape[1:],
        (n,) + first.shape[1:],
    ]
    return pl.pallas_call(
        functools.partial(_from_lines_kernel, (n_ax, n)),
        out_shape=[jax.ShapeDtypeStruct(s, x.dtype) for s in shapes],
        in_specs=[pl.BlockSpec(memory_space=pltpu.VMEM)] * 4,
        out_specs=[pl.BlockSpec(memory_space=pltpu.VMEM)] * 4,
        scratch_shapes=[
            pltpu.SemaphoreType.DMA((4 * n,)),
            pltpu.SemaphoreType.DMA((4 * n,)),
            pltpu.SemaphoreType.DMA((2,)),
        ],
        compiler_params=pltpu.CompilerParams(collective_id=2, has_side_effects=True),
    )(x, cpk, last, first)


def _exchange(body, out_shape, cid, n, x):
    return pl.pallas_call(
        functools.partial(body, n),
        out_shape=jax.ShapeDtypeStruct(out_shape, x.dtype),
        in_specs=[pl.BlockSpec(memory_space=pltpu.VMEM)],
        out_specs=pl.BlockSpec(memory_space=pltpu.VMEM),
        scratch_shapes=[
            pltpu.SemaphoreType.DMA((n,)),
            pltpu.SemaphoreType.DMA((n,)),
            pltpu.SemaphoreType.DMA,
        ],
        compiler_params=pltpu.CompilerParams(collective_id=cid, has_side_effects=True),
    )(x)


def to_lines(x, n):
    comps, rows, width = x.shape
    return _exchange(_to_lines_kernel, (comps, rows // n, width * n), 1, n, x)


def dft_table(length):
    half = length // 2
    root = int(round(math.sqrt(length)))
    cols = jnp.concatenate([jnp.arange(half + 1), jnp.arange(1, half)])
    phase = jnp.where(jnp.arange(length) > half, 0.5 * math.pi, 0.0).astype(jnp.float32)
    step = 2.0 * math.pi / length
    coarse = step * ((root * jnp.arange(length // root)[:, None] * cols[None, :]) % length).astype(jnp.float32)
    fine = step * ((jnp.arange(root)[:, None] * cols[None, :]) % length).astype(jnp.float32) - phase
    table = jnp.cos(coarse)[:, None] * jnp.cos(fine)[None] - jnp.sin(coarse)[:, None] * jnp.sin(fine)[None]
    return table.reshape(length, length)


def paired_inverse(precond):
    length = precond.shape[2]
    half = length // 2
    low = precond[:, :, : half + 1]
    mirror = jnp.flip(precond[:, :, half + 1 :], axis=2)
    inner = jnp.concatenate([jnp.zeros_like(low[:, :, :1]), mirror, jnp.zeros_like(low[:, :, :1])], axis=2)
    paired = low + inner
    return jnp.concatenate([paired, paired[:, :, 1:half]], axis=2)


def with_halo(x, sides, width, wrap):
    for axis, dim in sides:
        size, length = (lax.axis_size(axis), x.shape[dim])
        up = [(i, (i + 1) % size) for i in range(size if wrap else size - 1)]
        down = [(j, i) for i, j in up]
        last = lax.slice_in_dim(x, length - width, length, axis=dim)
        first = lax.slice_in_dim(x, 0, width, axis=dim)
        before = lax.ppermute(last, axis, up)
        after = lax.ppermute(first, axis, down)
        x = jnp.concatenate([before, x, after], axis=dim)
    return x


def swap_channels(field):
    extent = field.shape
    folded = field.reshape((extent[0] // 2, 2) + extent[1:])
    return jnp.flip(folded, axis=1).reshape(extent)


def swap_radial(field):
    extent = field.shape
    folded = field.reshape(extent[0], extent[1] // 2, 2, extent[2])
    return jnp.flip(folded, axis=2).reshape(extent)


def apply_operator(field, stiffness):
    axial_pad = with_halo(field, (("ax", 0),), 1, False)
    sector_pad = with_halo(field, (("sec", 2),), 1, True)
    beside = axial_pad[2:] + axial_pad[:-2]
    beside = beside + sector_pad[:, :, 2:] + sector_pad[:, :, :-2]
    return (stiffness + 4.5) * field - beside - 0.5 * swap_radial(field)


def shards(load, disp, stiff, hole, section_class, class_table, precond):
    slab_count, comp_count, sector_width = disp.shape
    sector_count = lax.axis_size("sec")
    around_cells = sector_width * sector_count
    total_axial = slab_count * lax.axis_size("ax")
    position = lax.axis_index("ax") * slab_count + jnp.arange(slab_count)
    taper = 1.0 + 2.0 * position.astype(jnp.float32) / (total_axial - 1)
    one_hot = (section_class[:, None] == jnp.arange(class_table.shape[0])[None, :]).astype(
        jnp.float32
    )
    factors = jnp.dot(one_hot, class_table, precision=lax.Precision.HIGHEST)
    stiffness = stiff * (factors * taper[:, None])[:, :, None]
    solid = (1 - hole).astype(jnp.float32)[:, None, :]
    residual = solid * (load - apply_operator(disp, stiffness))
    residual_t = jnp.transpose(residual, (1, 0, 2))
    solid_t = jnp.transpose(solid, (1, 0, 2))
    lines_all = to_lines(jnp.concatenate([residual_t, solid_t], axis=0), sector_count)
    lines = lines_all[:comp_count]
    spectrum = jnp.dot(
        lines.reshape(-1, around_cells), dft_table(around_cells), precision=lax.Precision.HIGH
    ).reshape(lines.shape)
    mixed = jnp.sum(paired_inverse(precond)[:, :, None] * spectrum[None], axis=1)
    smoothed_lines = lax.dot_general(
        mixed.reshape(-1, around_cells),
        dft_table(around_cells),
        (((1,), (1,)), ((), ())),
        precision=lax.Precision.HIGH,
    ) / around_cells
    prec_lines = lines_all[comp_count:] * smoothed_lines.reshape(lines.shape)
    group_rows = lines.shape[1]
    lanes = -(-2 * group_rows // 128) * 128
    subl = -(-comp_count // 8) * 8
    edge_at = [(p * sector_width - 1) % around_cells for p in range(sector_count)]
    edge_at += [((p + 1) * sector_width) % around_cells for p in range(sector_count)]
    pick = (jnp.arange(around_cells)[None, :] == jnp.array(edge_at)[:, None]).astype(jnp.float32)
    edges = lax.dot_general(
        pick,
        prec_lines.reshape(-1, around_cells),
        (((1,), (1,)), ((), ())),
        precision=lax.Precision.HIGHEST,
    ).reshape(2, sector_count, comp_count, group_rows)
    cpk = jnp.pad(
        jnp.transpose(edges, (1, 2, 0, 3)).reshape(sector_count, comp_count, 2 * group_rows),
        ((0, 0), (0, subl - comp_count), (0, lanes - 2 * group_rows)),
    )

    def row_pack(row):
        split = jnp.transpose(row.reshape(comp_count, sector_count, sector_width), (1, 0, 2))
        return jnp.pad(split, ((0, 0), (0, subl - comp_count), (0, 0)))

    prec_t, halo_cols, before_rows, after_rows = from_lines_with_halo(
        prec_lines, cpk, row_pack(prec_lines[:, -1]), row_pack(prec_lines[:, 0]), sector_count
    )
    ax = lax.axis_index("ax")
    before_row = jnp.where(ax == 0, 0.0, before_rows[sector_count - 1, :comp_count])
    after_row = jnp.where(ax == lax.axis_size("ax") - 1, 0.0, after_rows[0, :comp_count])
    got_cols = jnp.transpose(halo_cols[:, :comp_count, : 2 * group_rows], (1, 0, 2))
    got_cols = got_cols.reshape(comp_count, sector_count, 2, group_rows)
    before_col = got_cols[:, :, 0].reshape(comp_count, slab_count)
    after_col = got_cols[:, :, 1].reshape(comp_count, slab_count)
    stiffness_t = jnp.transpose(stiffness, (1, 0, 2))
    halo_rows = jnp.pad(jnp.stack([before_row, after_row]), ((0, 0), (0, subl - comp_count), (0, 0)))
    halo_cols = jnp.stack([before_col, after_col])[..., None]
    cell_total = slab_count * lax.axis_size("ax") * comp_count * around_cells
    finished, image_t = image_and_totals(
        residual_t, prec_t, stiffness_t, solid_t[0], halo_rows, halo_cols, cell_total, 0
    )
    finished = finished[0]
    alpha = finished[0]
    residual_new = residual - alpha * jnp.transpose(image_t, (1, 0, 2))
    disp_new = disp + alpha * jnp.transpose(prec_t, (1, 0, 2))
    return (disp_new, residual_new, finished[1:4])


def solution(mesh):
    in_specs = (
        P("ax", None, "sec"),
        P("ax", None, "sec"),
        P("ax", None, "sec"),
        P("ax", "sec"),
        P("ax"),
        P(),
        P(),
    )
    out_specs = (P("ax", None, "sec"), P("ax", None, "sec"), P())
    return jax.shard_map(shards, mesh=mesh, in_specs=in_specs, out_specs=out_specs, check_vma=False)
```

```python
import functools
import math

import jax
import jax.numpy as jnp
from jax import lax
from jax.experimental import pallas as pl
from jax.experimental.pallas import tpu as pltpu
from jax.sharding import PartitionSpec as P


MESH = pl.DeviceIdType.MESH


def _groups():
    me_ax = lax.axis_index("ax")
    me_sec = lax.axis_index("sec")
    x = me_ax % 4
    z = (me_ax // 4) % 8
    ylo = me_ax // 32
    core = me_sec % 2
    yhi = me_sec // 2

    def plane_peer(c):
        y = c % 4
        return ((y % 2) * 32 + z * 4 + (c // 4) % 4, (y // 2) * 2 + c // 16)

    return [
        (32, (core * 4 + x) * 4 + yhi * 2 + ylo, plane_peer),
        (8, z, lambda c: (me_ax - z * 4 + c * 4, me_sec)),
    ]


def _image_and_sums(r_ref, p_ref, s_ref, m_ref, hr_ref, hc_ref, img_ref):
    comps, rows, width = p_ref.shape
    row = lax.broadcasted_iota(jnp.int32, (rows, width), 0)
    lane = lax.broadcasted_iota(jnp.int32, (rows, width), 1)
    solid = m_ref[...]
    acc = [jnp.zeros((1, width), jnp.float32) for _ in range(5)]
    for q in range(comps):
        field = p_ref[q]
        up = jnp.where(row == 0, hr_ref[0, q : q + 1, :], pltpu.roll(field, 1, 0))
        down = jnp.where(row == rows - 1, hr_ref[1, q : q + 1, :], pltpu.roll(field, rows - 1, 0))
        left = jnp.where(lane == 0, hc_ref[0, q], pltpu.roll(field, 1, 1))
        right = jnp.where(lane == width - 1, hc_ref[1, q], pltpu.roll(field, width - 1, 1))
        beside = down + up + right + left
        image = solid * ((s_ref[q] + 4.5) * field - beside - 0.5 * p_ref[q ^ 1])
        img_ref[q] = image
        res = r_ref[q]
        for k, prod in enumerate((res * field, field * image, res * res, res * image, image * image)):
            acc[k] = acc[k] + jnp.sum(prod, axis=0, keepdims=True)
    lane8 = lax.broadcasted_iota(jnp.int32, (8, 128), 1)
    row8 = lax.broadcasted_iota(jnp.int32, (8, 128), 0)
    packed = jnp.zeros((8, 128), jnp.float32)
    for k, a in enumerate(acc):
        packed = jnp.where((row8 == 0) & (lane8 == k), jnp.sum(a), packed)
    return packed


def _finish(total, cell_total):
    lane = lax.broadcasted_iota(jnp.int32, total.shape, 1)
    row = lax.broadcasted_iota(jnp.int32, total.shape, 0)

    def pick(k):
        return jnp.sum(jnp.where((row == 0) & (lane == k), total, 0.0), keepdims=True)

    inner_rz = pick(0) / cell_total
    inner_zq = pick(1) / cell_total
    alpha = inner_rz / inner_zq
    square_new = (pick(2) - alpha * (2.0 * pick(3) - alpha * pick(4))) / cell_total
    out = jnp.zeros(total.shape, jnp.float32)
    for k, v in enumerate((alpha, inner_rz, inner_zq, square_new)):
        out = jnp.where((row == 0) & (lane == k), v, out)
    return out


def _ar_kernel(cell_total, r_ref, p_ref, s_ref, m_ref, hr_ref, hc_ref, d_ref, o_ref, img_ref, dn_ref,
               rn_ref, recv_a, recv_b, own, send_sems, recv_sems):
    recvs = (recv_a, recv_b)
    groups = _groups()
    for r in recvs:
        r[...] = jnp.zeros_like(r)
    barrier = pltpu.get_barrier_semaphore()
    count = 0
    for n, mine, dev in groups:
        for d in range(1, n):
            pl.semaphore_signal(barrier, inc=1, device_id=dev((mine + d) % n), device_id_type=MESH)
            count += 1
    own[0] = _image_and_sums(r_ref, p_ref, s_ref, m_ref, hr_ref, hc_ref, img_ref)
    pl.semaphore_wait(barrier, count)
    base = 0
    for g, (n, mine, dev) in enumerate(groups):
        src = own.at[g]
        copies = []
        for d in range(1, n):
            cp = pltpu.make_async_remote_copy(
                src_ref=src,
                dst_ref=recvs[g].at[mine],
                send_sem=send_sems.at[base + d],
                recv_sem=recv_sems.at[base + d],
                device_id=dev((mine + d) % n),
                device_id_type=MESH,
            )
            cp.start()
            copies.append(cp)
        mine_val = src[...]
        for cp in copies:
            cp.wait_recv()
        total = None
        for c in range(n):
            v = jnp.where(mine == c, mine_val, recvs[g][c])
            total = v if total is None else total + v
        for cp in copies:
            cp.wait_send()
        base += n
        if g + 1 < len(groups):
            own[g + 1] = total
        else:
            finished = _finish(total, cell_total)
            o_ref[...] = finished
            alpha = finished[0:1, 0:1]
            for q in range(p_ref.shape[0]):
                dn_ref[q] = d_ref[q] + alpha * p_ref[q]
                rn_ref[q] = r_ref[q] - alpha * img_ref[q]


def image_and_totals(residual, prec, stiffness, solid, halo_rows, halo_cols, disp, cell_total, cid):
    return pl.pallas_call(
        functools.partial(_ar_kernel, float(cell_total)),
        out_shape=[
            jax.ShapeDtypeStruct((8, 128), jnp.float32),
            jax.ShapeDtypeStruct(prec.shape, jnp.float32),
            jax.ShapeDtypeStruct(prec.shape, jnp.float32),
            jax.ShapeDtypeStruct(prec.shape, jnp.float32),
        ],
        in_specs=[pl.BlockSpec(memory_space=pltpu.VMEM)] * 7,
        out_specs=[pl.BlockSpec(memory_space=pltpu.VMEM)] * 4,
        scratch_shapes=[
            pltpu.VMEM((32, 8, 128), jnp.float32),
            pltpu.VMEM((8, 8, 128), jnp.float32),
            pltpu.VMEM((2, 8, 128), jnp.float32),
            pltpu.SemaphoreType.DMA((40,)),
            pltpu.SemaphoreType.DMA((40,)),
        ],
        compiler_params=pltpu.CompilerParams(collective_id=cid, has_side_effects=True),
    )(residual, prec, stiffness, solid, halo_rows, halo_cols, disp)


def _to_lines_kernel(n, count, *refs):
    x_refs, o_refs = refs[:count], refs[count : 2 * count]
    send_sems, recv_sems, local_sems = refs[2 * count :]
    me = lax.axis_index("sec")
    ax = lax.axis_index("ax")
    barrier = pltpu.get_barrier_semaphore()
    for d in range(1, n):
        pl.semaphore_signal(barrier, inc=1, device_id=(ax, (me + d) % n), device_id_type=MESH)
    pl.semaphore_wait(barrier, n - 1)
    copies, local = [], []
    for i, (x_ref, o_ref) in enumerate(zip(x_refs, o_refs)):
        rows, width = o_ref.shape[1], x_ref.shape[2]
        dst = o_ref.at[:, :, pl.ds(pl.multiple_of(me * width, width), width)]
        for d in range(1, n):
            peer = (me + d) % n
            cp = pltpu.make_async_remote_copy(
                src_ref=x_ref.at[:, pl.ds(pl.multiple_of(peer * rows, rows), rows), :],
                dst_ref=dst,
                send_sem=send_sems.at[i * n + d],
                recv_sem=recv_sems.at[i * n + d],
                device_id=(ax, peer),
                device_id_type=MESH,
            )
            cp.start()
            copies.append(cp)
        local.append(
            pltpu.make_async_copy(
                x_ref.at[:, pl.ds(pl.multiple_of(me * rows, rows), rows), :], dst, local_sems.at[i]
            )
        )
        local[-1].start()
    for cp in local:
        cp.wait()
    for cp in copies:
        cp.wait()


def to_lines(arrays, n):
    count = len(arrays)
    shapes = [(x.shape[0], x.shape[1] // n, x.shape[2] * n) for x in arrays]
    return pl.pallas_call(
        functools.partial(_to_lines_kernel, n, count),
        out_shape=[jax.ShapeDtypeStruct(s, x.dtype) for s, x in zip(shapes, arrays)],
        in_specs=[pl.BlockSpec(memory_space=pltpu.VMEM)] * count,
        out_specs=[pl.BlockSpec(memory_space=pltpu.VMEM)] * count,
        scratch_shapes=[
            pltpu.SemaphoreType.DMA((count * n,)),
            pltpu.SemaphoreType.DMA((count * n,)),
            pltpu.SemaphoreType.DMA((count,)),
        ],
        compiler_params=pltpu.CompilerParams(collective_id=1, has_side_effects=True),
    )(*arrays)


def _from_lines_kernel(sizes, x_ref, cpk_ref, last_ref, first_ref, o_ref, cols_ref, before_ref,
                       after_ref, send_sems, recv_sems, local_sems):
    n_ax, n = sizes
    me = lax.axis_index("sec")
    ax = lax.axis_index("ax")
    rows, width = x_ref.shape[1], o_ref.shape[2]
    up_ax, down_ax = (ax + 1) % n_ax, (ax + n_ax - 1) % n_ax
    peers = [(ax, (me + d) % n) for d in range(1, n)]
    peers += [(up_ax, s) for s in range(n)] + [(down_ax, s) for s in range(n)]
    barrier = pltpu.get_barrier_semaphore()
    for peer in peers:
        pl.semaphore_signal(barrier, inc=1, device_id=peer, device_id_type=MESH)
    pl.semaphore_wait(barrier, len(peers))
    dst = o_ref.at[:, pl.ds(pl.multiple_of(me * rows, rows), rows), :]
    sends, recvs = [], []
    for d in range(1, n):
        peer = (me + d) % n
        for k, (src, out) in enumerate(
            (
                (x_ref.at[:, :, pl.ds(pl.multiple_of(peer * width, width), width)], dst),
                (cpk_ref.at[peer], cols_ref.at[me]),
            )
        ):
            cp = pltpu.make_async_remote_copy(
                src_ref=src,
                dst_ref=out,
                send_sem=send_sems.at[k * n + d],
                recv_sem=recv_sems.at[k * n + d],
                device_id=(ax, peer),
                device_id_type=MESH,
            )
            cp.start()
            sends.append(cp)
        origin = (me + n - d) % n
        for k, (src, out) in enumerate(
            (
                (x_ref.at[:, :, pl.ds(0, width)], o_ref.at[:, pl.ds(pl.multiple_of(origin * rows, rows), rows), :]),
                (cpk_ref.at[0], cols_ref.at[origin]),
            )
        ):
            recvs.append(
                pltpu.make_async_remote_copy(
                    src_ref=src,
                    dst_ref=out,
                    send_sem=send_sems.at[k * n + d],
                    recv_sem=recv_sems.at[k * n + d],
                    device_id=(ax, origin),
                    device_id_type=MESH,
                )
            )
    for s in range(n):
        for k, (src, out, target) in enumerate(
            ((last_ref.at[s], before_ref.at[me], up_ax), (first_ref.at[s], after_ref.at[me], down_ax))
        ):
            base = (2 + k) * n
            cp = pltpu.make_async_remote_copy(
                src_ref=src,
                dst_ref=out,
                send_sem=send_sems.at[base + s],
                recv_sem=recv_sems.at[base + me],
                device_id=(target, s),
                device_id_type=MESH,
            )
            cp.start()
            sends.append(cp)
            recvs.append(
                pltpu.make_async_remote_copy(
                    src_ref=src,
                    dst_ref=(before_ref, after_ref)[k].at[s],
                    send_sem=send_sems.at[base + s],
                    recv_sem=recv_sems.at[base + s],
                    device_id=(target, s),
                    device_id_type=MESH,
                )
            )
    local = [
        pltpu.make_async_copy(
            x_ref.at[:, :, pl.ds(pl.multiple_of(me * width, width), width)], dst, local_sems.at[0]
        ),
        pltpu.make_async_copy(cpk_ref.at[me], cols_ref.at[me], local_sems.at[1]),
    ]
    for cp in local:
        cp.start()
    for cp in local:
        cp.wait()
    for cp in recvs:
        cp.wait_recv()
    for cp in sends:
        cp.wait_send()


def from_lines_with_halo(x, cpk, last, first, n):
    comps, rows, around = x.shape
    n_ax = lax.axis_size("ax")
    shapes = [
        (comps, rows * n, around // n),
        cpk.shape,
        (n,) + last.shape[1:],
        (n,) + first.shape[1:],
    ]
    return pl.pallas_call(
        functools.partial(_from_lines_kernel, (n_ax, n)),
        out_shape=[jax.ShapeDtypeStruct(s, x.dtype) for s in shapes],
        in_specs=[pl.BlockSpec(memory_space=pltpu.VMEM)] * 4,
        out_specs=[pl.BlockSpec(memory_space=pltpu.VMEM)] * 4,
        scratch_shapes=[
            pltpu.SemaphoreType.DMA((4 * n,)),
            pltpu.SemaphoreType.DMA((4 * n,)),
            pltpu.SemaphoreType.DMA((2,)),
        ],
        compiler_params=pltpu.CompilerParams(collective_id=2, has_side_effects=True),
    )(x, cpk, last, first)


def dft_table(length):
    half = length // 2
    root = int(round(math.sqrt(length)))
    cols = jnp.concatenate([jnp.arange(half + 1), jnp.arange(1, half)])
    phase = jnp.where(jnp.arange(length) > half, 0.5 * math.pi, 0.0).astype(jnp.float32)
    step = 2.0 * math.pi / length
    coarse = step * ((root * jnp.arange(length // root)[:, None] * cols[None, :]) % length).astype(jnp.float32)
    fine = step * ((jnp.arange(root)[:, None] * cols[None, :]) % length).astype(jnp.float32) - phase
    table = jnp.cos(coarse)[:, None] * jnp.cos(fine)[None] - jnp.sin(coarse)[:, None] * jnp.sin(fine)[None]
    return table.reshape(length, length)


def paired_inverse(precond):
    length = precond.shape[2]
    half = length // 2
    low = precond[:, :, : half + 1]
    mirror = jnp.flip(precond[:, :, half + 1 :], axis=2)
    inner = jnp.concatenate([jnp.zeros_like(low[:, :, :1]), mirror, jnp.zeros_like(low[:, :, :1])], axis=2)
    paired = low + inner
    return jnp.concatenate([paired, paired[:, :, 1:half]], axis=2)


def with_halo(x, sides, width, wrap):
    for axis, dim in sides:
        size, length = (lax.axis_size(axis), x.shape[dim])
        up = [(i, (i + 1) % size) for i in range(size if wrap else size - 1)]
        down = [(j, i) for i, j in up]
        last = lax.slice_in_dim(x, length - width, length, axis=dim)
        first = lax.slice_in_dim(x, 0, width, axis=dim)
        before = lax.ppermute(last, axis, up)
        after = lax.ppermute(first, axis, down)
        x = jnp.concatenate([before, x, after], axis=dim)
    return x


def swap_channels(field):
    extent = field.shape
    folded = field.reshape((extent[0] // 2, 2) + extent[1:])
    return jnp.flip(folded, axis=1).reshape(extent)


def swap_radial(field):
    extent = field.shape
    folded = field.reshape(extent[0], extent[1] // 2, 2, extent[2])
    return jnp.flip(folded, axis=2).reshape(extent)


def apply_operator(field, stiffness):
    axial_pad = with_halo(field, (("ax", 0),), 1, False)
    sector_pad = with_halo(field, (("sec", 2),), 1, True)
    beside = axial_pad[2:] + axial_pad[:-2]
    beside = beside + sector_pad[:, :, 2:] + sector_pad[:, :, :-2]
    return (stiffness + 4.5) * field - beside - 0.5 * swap_radial(field)


def shards(load, disp, stiff, hole, section_class, class_table, precond):
    slab_count, comp_count, sector_width = disp.shape
    sector_count = lax.axis_size("sec")
    around_cells = sector_width * sector_count
    total_axial = slab_count * lax.axis_size("ax")
    position = lax.axis_index("ax") * slab_count + jnp.arange(slab_count)
    taper = 1.0 + 2.0 * position.astype(jnp.float32) / (total_axial - 1)
    one_hot = (section_class[:, None] == jnp.arange(class_table.shape[0])[None, :]).astype(
        jnp.float32
    )
    factors = jnp.dot(one_hot, class_table, precision=lax.Precision.HIGHEST)
    stiffness = stiff * (factors * taper[:, None])[:, :, None]
    solid = (1 - hole).astype(jnp.float32)[:, None, :]
    residual = solid * (load - apply_operator(disp, stiffness))
    residual_t = jnp.transpose(residual, (1, 0, 2))
    solid_t = jnp.transpose(solid, (1, 0, 2))
    lines, solid_lines = to_lines([residual_t, solid_t], sector_count)
    spectrum = jnp.dot(
        lines.reshape(-1, around_cells), dft_table(around_cells), precision=lax.Precision.HIGH
    ).reshape(lines.shape)
    mixed = jnp.sum(paired_inverse(precond)[:, :, None] * spectrum[None], axis=1)
    smoothed_lines = lax.dot_general(
        mixed.reshape(-1, around_cells),
        dft_table(around_cells),
        (((1,), (1,)), ((), ())),
        precision=lax.Precision.HIGH,
    ) / around_cells
    prec_lines = solid_lines * smoothed_lines.reshape(lines.shape)
    group_rows = lines.shape[1]
    lanes = -(-2 * group_rows // 128) * 128
    subl = -(-comp_count // 8) * 8
    edge_at = [(p * sector_width - 1) % around_cells for p in range(sector_count)]
    edge_at += [((p + 1) * sector_width) % around_cells for p in range(sector_count)]
    pick = (jnp.arange(around_cells)[None, :] == jnp.array(edge_at)[:, None]).astype(jnp.float32)
    edges = lax.dot_general(
        pick,
        prec_lines.reshape(-1, around_cells),
        (((1,), (1,)), ((), ())),
        precision=lax.Precision.HIGHEST,
    ).reshape(2, sector_count, comp_count, group_rows)
    cpk = jnp.pad(
        jnp.transpose(edges, (1, 2, 0, 3)).reshape(sector_count, comp_count, 2 * group_rows),
        ((0, 0), (0, subl - comp_count), (0, lanes - 2 * group_rows)),
    )

    def row_pack(row):
        split = jnp.transpose(row.reshape(comp_count, sector_count, sector_width), (1, 0, 2))
        return jnp.pad(split, ((0, 0), (0, subl - comp_count), (0, 0)))

    prec_t, halo_cols, before_rows, after_rows = from_lines_with_halo(
        prec_lines, cpk, row_pack(prec_lines[:, -1]), row_pack(prec_lines[:, 0]), sector_count
    )
    ax = lax.axis_index("ax")
    before_row = jnp.where(ax == 0, 0.0, before_rows[sector_count - 1, :comp_count])
    after_row = jnp.where(ax == lax.axis_size("ax") - 1, 0.0, after_rows[0, :comp_count])
    got_cols = jnp.transpose(halo_cols[:, :comp_count, : 2 * group_rows], (1, 0, 2))
    got_cols = got_cols.reshape(comp_count, sector_count, 2, group_rows)
    before_col = got_cols[:, :, 0].reshape(comp_count, slab_count)
    after_col = got_cols[:, :, 1].reshape(comp_count, slab_count)
    stiffness_t = jnp.transpose(stiffness, (1, 0, 2))
    halo_rows = jnp.pad(jnp.stack([before_row, after_row]), ((0, 0), (0, subl - comp_count), (0, 0)))
    halo_cols = jnp.stack([before_col, after_col])[..., None]
    cell_total = slab_count * lax.axis_size("ax") * comp_count * around_cells
    finished, _, disp_new_t, residual_new_t = image_and_totals(
        residual_t,
        prec_t,
        stiffness_t,
        solid_t[0],
        halo_rows,
        halo_cols,
        jnp.transpose(disp, (1, 0, 2)),
        cell_total,
        0,
    )
    return (
        jnp.transpose(disp_new_t, (1, 0, 2)),
        jnp.transpose(residual_new_t, (1, 0, 2)),
        finished[0, 1:4],
    )


def solution(mesh):
    in_specs = (
        P("ax", None, "sec"),
        P("ax", None, "sec"),
        P("ax", None, "sec"),
        P("ax", "sec"),
        P("ax"),
        P(),
        P(),
    )
    out_specs = (P("ax", None, "sec"), P("ax", None, "sec"), P())
    return jax.shard_map(shards, mesh=mesh, in_specs=in_specs, out_specs=out_specs, check_vma=False)
```

```python
import functools
import math

import jax
import jax.numpy as jnp
from jax import lax
from jax.experimental import pallas as pl
from jax.experimental.pallas import tpu as pltpu
from jax.sharding import PartitionSpec as P


MESH = pl.DeviceIdType.MESH


def _groups():
    me_ax = lax.axis_index("ax")
    me_sec = lax.axis_index("sec")
    x = me_ax % 4
    z = (me_ax // 4) % 8
    ylo = me_ax // 32
    core = me_sec % 2
    yhi = me_sec // 2

    def plane_peer(c):
        y = c % 4
        return ((y % 2) * 32 + z * 4 + (c // 4) % 4, (y // 2) * 2 + c // 16)

    return [
        (32, (core * 4 + x) * 4 + yhi * 2 + ylo, plane_peer),
        (8, z, lambda c: (me_ax - z * 4 + c * 4, me_sec)),
    ]


def _image_and_sums(r_ref, p_ref, s_ref, m_ref, hr_ref, hc_ref, img_ref):
    comps, rows, width = p_ref.shape
    row = lax.broadcasted_iota(jnp.int32, (rows, width), 0)
    lane = lax.broadcasted_iota(jnp.int32, (rows, width), 1)
    solid = m_ref[...]
    acc = [jnp.zeros((1, width), jnp.float32) for _ in range(5)]
    for q in range(comps):
        field = p_ref[q]
        up = jnp.where(row == 0, hr_ref[0, q : q + 1, :], pltpu.roll(field, 1, 0))
        down = jnp.where(row == rows - 1, hr_ref[1, q : q + 1, :], pltpu.roll(field, rows - 1, 0))
        left = jnp.where(lane == 0, hc_ref[0, q], pltpu.roll(field, 1, 1))
        right = jnp.where(lane == width - 1, hc_ref[1, q], pltpu.roll(field, width - 1, 1))
        beside = down + up + right + left
        image = solid * ((s_ref[q] + 4.5) * field - beside - 0.5 * p_ref[q ^ 1])
        img_ref[q] = image
        res = r_ref[q]
        for k, prod in enumerate((res * field, field * image, res * res, res * image, image * image)):
            acc[k] = acc[k] + jnp.sum(prod, axis=0, keepdims=True)
    lane8 = lax.broadcasted_iota(jnp.int32, (8, 128), 1)
    row8 = lax.broadcasted_iota(jnp.int32, (8, 128), 0)
    packed = jnp.zeros((8, 128), jnp.float32)
    for k, a in enumerate(acc):
        packed = jnp.where((row8 == 0) & (lane8 == k), jnp.sum(a), packed)
    return packed


def _finish(total, cell_total):
    lane = lax.broadcasted_iota(jnp.int32, total.shape, 1)
    row = lax.broadcasted_iota(jnp.int32, total.shape, 0)

    def pick(k):
        return jnp.sum(jnp.where((row == 0) & (lane == k), total, 0.0), keepdims=True)

    inner_rz = pick(0) / cell_total
    inner_zq = pick(1) / cell_total
    alpha = inner_rz / inner_zq
    square_new = (pick(2) - alpha * (2.0 * pick(3) - alpha * pick(4))) / cell_total
    out = jnp.zeros(total.shape, jnp.float32)
    for k, v in enumerate((alpha, inner_rz, inner_zq, square_new)):
        out = jnp.where((row == 0) & (lane == k), v, out)
    return out


def _ar_kernel(cell_total, r_ref, p_ref, s_ref, m_ref, hr_ref, hc_ref, d_ref, o_ref, img_ref, dn_ref,
               rn_ref, recv_a, recv_b, own, send_sems, recv_sems):
    recvs = (recv_a, recv_b)
    groups = _groups()
    for r in recvs:
        r[...] = jnp.zeros_like(r)
    barrier = pltpu.get_barrier_semaphore()
    count = 0
    for n, mine, dev in groups:
        for d in range(1, n):
            pl.semaphore_signal(barrier, inc=1, device_id=dev((mine + d) % n), device_id_type=MESH)
            count += 1
    own[0] = _image_and_sums(r_ref, p_ref, s_ref, m_ref, hr_ref, hc_ref, img_ref)
    pl.semaphore_wait(barrier, count)
    base = 0
    for g, (n, mine, dev) in enumerate(groups):
        src = own.at[g]
        copies = []
        for d in range(1, n):
            cp = pltpu.make_async_remote_copy(
                src_ref=src,
                dst_ref=recvs[g].at[mine],
                send_sem=send_sems.at[base + d],
                recv_sem=recv_sems.at[base + d],
                device_id=dev((mine + d) % n),
                device_id_type=MESH,
            )
            cp.start()
            copies.append(cp)
        mine_val = src[...]
        for cp in copies:
            cp.wait_recv()
        total = None
        for c in range(n):
            v = jnp.where(mine == c, mine_val, recvs[g][c])
            total = v if total is None else total + v
        for cp in copies:
            cp.wait_send()
        base += n
        if g + 1 < len(groups):
            own[g + 1] = total
        else:
            finished = _finish(total, cell_total)
            o_ref[...] = finished
            alpha = finished[0:1, 0:1]
            for q in range(p_ref.shape[0]):
                dn_ref[q] = d_ref[q] + alpha * p_ref[q]
                rn_ref[q] = r_ref[q] - alpha * img_ref[q]


def image_and_totals(residual, prec, stiffness, solid, halo_rows, halo_cols, disp, cell_total, cid):
    return pl.pallas_call(
        functools.partial(_ar_kernel, float(cell_total)),
        out_shape=[
            jax.ShapeDtypeStruct((8, 128), jnp.float32),
            jax.ShapeDtypeStruct(prec.shape, jnp.float32),
            jax.ShapeDtypeStruct(prec.shape, jnp.float32),
            jax.ShapeDtypeStruct(prec.shape, jnp.float32),
        ],
        in_specs=[pl.BlockSpec(memory_space=pltpu.VMEM)] * 7,
        out_specs=[pl.BlockSpec(memory_space=pltpu.VMEM)] * 4,
        scratch_shapes=[
            pltpu.VMEM((32, 8, 128), jnp.float32),
            pltpu.VMEM((8, 8, 128), jnp.float32),
            pltpu.VMEM((2, 8, 128), jnp.float32),
            pltpu.SemaphoreType.DMA((40,)),
            pltpu.SemaphoreType.DMA((40,)),
        ],
        compiler_params=pltpu.CompilerParams(collective_id=cid, has_side_effects=True),
    )(residual, prec, stiffness, solid, halo_rows, halo_cols, disp)


def _to_lines_kernel(n, count, *refs):
    x_refs, o_refs = refs[:count], refs[count : 2 * count]
    send_sems, recv_sems, local_sems = refs[2 * count :]
    me = lax.axis_index("sec")
    ax = lax.axis_index("ax")
    barrier = pltpu.get_barrier_semaphore()
    for d in range(1, n):
        pl.semaphore_signal(barrier, inc=1, device_id=(ax, (me + d) % n), device_id_type=MESH)
    pl.semaphore_wait(barrier, n - 1)
    copies, local = [], []
    for i, (x_ref, o_ref) in enumerate(zip(x_refs, o_refs)):
        rows, width = o_ref.shape[1], x_ref.shape[2]
        dst = o_ref.at[:, :, pl.ds(pl.multiple_of(me * width, width), width)]
        for d in range(1, n):
            peer = (me + d) % n
            cp = pltpu.make_async_remote_copy(
                src_ref=x_ref.at[:, pl.ds(pl.multiple_of(peer * rows, rows), rows), :],
                dst_ref=dst,
                send_sem=send_sems.at[i * n + d],
                recv_sem=recv_sems.at[i * n + d],
                device_id=(ax, peer),
                device_id_type=MESH,
            )
            cp.start()
            copies.append(cp)
        local.append(
            pltpu.make_async_copy(
                x_ref.at[:, pl.ds(pl.multiple_of(me * rows, rows), rows), :], dst, local_sems.at[i]
            )
        )
        local[-1].start()
    for cp in local:
        cp.wait()
    for cp in copies:
        cp.wait()


def to_lines(arrays, n):
    count = len(arrays)
    shapes = [(x.shape[0], x.shape[1] // n, x.shape[2] * n) for x in arrays]
    return pl.pallas_call(
        functools.partial(_to_lines_kernel, n, count),
        out_shape=[jax.ShapeDtypeStruct(s, x.dtype) for s, x in zip(shapes, arrays)],
        in_specs=[pl.BlockSpec(memory_space=pltpu.VMEM)] * count,
        out_specs=[pl.BlockSpec(memory_space=pltpu.VMEM)] * count,
        scratch_shapes=[
            pltpu.SemaphoreType.DMA((count * n,)),
            pltpu.SemaphoreType.DMA((count * n,)),
            pltpu.SemaphoreType.DMA((count,)),
        ],
        compiler_params=pltpu.CompilerParams(collective_id=1, has_side_effects=True),
    )(*arrays)


def _from_lines_kernel(sizes, x_ref, cpk_ref, last_ref, first_ref, o_ref, cols_ref, before_ref,
                       after_ref, send_sems, recv_sems, local_sems):
    n_ax, n = sizes
    me = lax.axis_index("sec")
    ax = lax.axis_index("ax")
    rows, width = x_ref.shape[1], o_ref.shape[2]
    up_ax, down_ax = (ax + 1) % n_ax, (ax + n_ax - 1) % n_ax
    peers = [(ax, (me + d) % n) for d in range(1, n)]
    peers += [(up_ax, s) for s in range(n)] + [(down_ax, s) for s in range(n)]
    barrier = pltpu.get_barrier_semaphore()
    for peer in peers:
        pl.semaphore_signal(barrier, inc=1, device_id=peer, device_id_type=MESH)
    pl.semaphore_wait(barrier, len(peers))
    dst = o_ref.at[:, pl.ds(pl.multiple_of(me * rows, rows), rows), :]
    sends, recvs = [], []
    for d in range(1, n):
        peer = (me + d) % n
        for k, (src, out) in enumerate(
            (
                (x_ref.at[:, :, pl.ds(pl.multiple_of(peer * width, width), width)], dst),
                (cpk_ref.at[peer], cols_ref.at[me]),
            )
        ):
            cp = pltpu.make_async_remote_copy(
                src_ref=src,
                dst_ref=out,
                send_sem=send_sems.at[k * n + d],
                recv_sem=recv_sems.at[k * n + d],
                device_id=(ax, peer),
                device_id_type=MESH,
            )
            cp.start()
            sends.append(cp)
        origin = (me + n - d) % n
        for k, (src, out) in enumerate(
            (
                (x_ref.at[:, :, pl.ds(0, width)], o_ref.at[:, pl.ds(pl.multiple_of(origin * rows, rows), rows), :]),
                (cpk_ref.at[0], cols_ref.at[origin]),
            )
        ):
            recvs.append(
                pltpu.make_async_remote_copy(
                    src_ref=src,
                    dst_ref=out,
                    send_sem=send_sems.at[k * n + d],
                    recv_sem=recv_sems.at[k * n + d],
                    device_id=(ax, origin),
                    device_id_type=MESH,
                )
            )
    for s in range(n):
        for k, (src, out, target) in enumerate(
            ((last_ref.at[s], before_ref.at[me], up_ax), (first_ref.at[s], after_ref.at[me], down_ax))
        ):
            base = (2 + k) * n
            cp = pltpu.make_async_remote_copy(
                src_ref=src,
                dst_ref=out,
                send_sem=send_sems.at[base + s],
                recv_sem=recv_sems.at[base + me],
                device_id=(target, s),
                device_id_type=MESH,
            )
            cp.start()
            sends.append(cp)
            recvs.append(
                pltpu.make_async_remote_copy(
                    src_ref=src,
                    dst_ref=(before_ref, after_ref)[k].at[s],
                    send_sem=send_sems.at[base + s],
                    recv_sem=recv_sems.at[base + s],
                    device_id=(target, s),
                    device_id_type=MESH,
                )
            )
    local = [
        pltpu.make_async_copy(
            x_ref.at[:, :, pl.ds(pl.multiple_of(me * width, width), width)], dst, local_sems.at[0]
        ),
        pltpu.make_async_copy(cpk_ref.at[me], cols_ref.at[me], local_sems.at[1]),
    ]
    for cp in local:
        cp.start()
    for cp in local:
        cp.wait()
    for cp in recvs:
        cp.wait_recv()
    for cp in sends:
        cp.wait_send()


def from_lines_with_halo(x, cpk, last, first, n):
    comps, rows, around = x.shape
    n_ax = lax.axis_size("ax")
    shapes = [
        (comps, rows * n, around // n),
        cpk.shape,
        (n,) + last.shape[1:],
        (n,) + first.shape[1:],
    ]
    return pl.pallas_call(
        functools.partial(_from_lines_kernel, (n_ax, n)),
        out_shape=[jax.ShapeDtypeStruct(s, x.dtype) for s in shapes],
        in_specs=[pl.BlockSpec(memory_space=pltpu.VMEM)] * 4,
        out_specs=[pl.BlockSpec(memory_space=pltpu.VMEM)] * 4,
        scratch_shapes=[
            pltpu.SemaphoreType.DMA((4 * n,)),
            pltpu.SemaphoreType.DMA((4 * n,)),
            pltpu.SemaphoreType.DMA((2,)),
        ],
        compiler_params=pltpu.CompilerParams(collective_id=2, has_side_effects=True),
    )(x, cpk, last, first)


def dft_table(length):
    half = length // 2
    root = int(round(math.sqrt(length)))
    cols = jnp.concatenate([jnp.arange(half + 1), jnp.arange(1, half)])
    phase = jnp.where(jnp.arange(length) > half, 0.5 * math.pi, 0.0).astype(jnp.float32)
    step = 2.0 * math.pi / length
    coarse = step * ((root * jnp.arange(length // root)[:, None] * cols[None, :]) % length).astype(jnp.float32)
    fine = step * ((jnp.arange(root)[:, None] * cols[None, :]) % length).astype(jnp.float32) - phase
    table = jnp.cos(coarse)[:, None] * jnp.cos(fine)[None] - jnp.sin(coarse)[:, None] * jnp.sin(fine)[None]
    return table.reshape(length, length)


def paired_inverse(precond):
    length = precond.shape[2]
    half = length // 2
    low = precond[:, :, : half + 1]
    mirror = jnp.flip(precond[:, :, half + 1 :], axis=2)
    inner = jnp.concatenate([jnp.zeros_like(low[:, :, :1]), mirror, jnp.zeros_like(low[:, :, :1])], axis=2)
    paired = low + inner
    return jnp.concatenate([paired, paired[:, :, 1:half]], axis=2)


def with_halo(x, sides, width, wrap):
    for axis, dim in sides:
        size, length = (lax.axis_size(axis), x.shape[dim])
        up = [(i, (i + 1) % size) for i in range(size if wrap else size - 1)]
        down = [(j, i) for i, j in up]
        last = lax.slice_in_dim(x, length - width, length, axis=dim)
        first = lax.slice_in_dim(x, 0, width, axis=dim)
        before = lax.ppermute(last, axis, up)
        after = lax.ppermute(first, axis, down)
        x = jnp.concatenate([before, x, after], axis=dim)
    return x


def swap_channels(field):
    extent = field.shape
    folded = field.reshape((extent[0] // 2, 2) + extent[1:])
    return jnp.flip(folded, axis=1).reshape(extent)


def swap_radial(field):
    comps = field.shape[1]
    return jnp.concatenate([field[:, q ^ 1 : (q ^ 1) + 1] for q in range(comps)], axis=1)


def apply_operator(field, stiffness):
    rows, comps, width = field.shape
    axial_pad = with_halo(field, (("ax", 0),), 1, False)
    pick = (jnp.arange(width)[None, :] == jnp.array([0, width - 1])[:, None]).astype(jnp.float32)
    edges = lax.dot_general(
        pick, field.reshape(-1, width), (((1,), (1,)), ((), ())), precision=lax.Precision.HIGHEST
    )
    size = lax.axis_size("sec")
    up = [(i, (i + 1) % size) for i in range(size)]
    down = [(j, i) for i, j in up]
    before_col = lax.ppermute(edges[1:], "sec", up).reshape(rows, comps, 1)
    after_col = lax.ppermute(edges[:1], "sec", down).reshape(rows, comps, 1)
    lane = lax.broadcasted_iota(jnp.int32, field.shape, 2)
    left = jnp.where(lane == 0, jnp.broadcast_to(before_col, field.shape), jnp.roll(field, 1, axis=2))
    right = jnp.where(
        lane == width - 1, jnp.broadcast_to(after_col, field.shape), jnp.roll(field, -1, axis=2)
    )
    beside = axial_pad[2:] + axial_pad[:-2]
    beside = beside + right + left
    return (stiffness + 4.5) * field - beside - 0.5 * swap_radial(field)


def shards(load, disp, stiff, hole, section_class, class_table, precond):
    slab_count, comp_count, sector_width = disp.shape
    sector_count = lax.axis_size("sec")
    around_cells = sector_width * sector_count
    total_axial = slab_count * lax.axis_size("ax")
    position = lax.axis_index("ax") * slab_count + jnp.arange(slab_count)
    taper = 1.0 + 2.0 * position.astype(jnp.float32) / (total_axial - 1)
    one_hot = (section_class[:, None] == jnp.arange(class_table.shape[0])[None, :]).astype(
        jnp.float32
    )
    factors = jnp.dot(one_hot, class_table, precision=lax.Precision.HIGHEST)
    stiffness = stiff * (factors * taper[:, None])[:, :, None]
    solid = (1 - hole).astype(jnp.float32)[:, None, :]
    residual = solid * (load - apply_operator(disp, stiffness))
    residual_t = jnp.transpose(residual, (1, 0, 2))
    solid_t = jnp.transpose(solid, (1, 0, 2))
    lines, solid_lines = to_lines([residual_t, solid_t], sector_count)
    spectrum = jnp.dot(
        lines.reshape(-1, around_cells), dft_table(around_cells), precision=lax.Precision.HIGH
    ).reshape(lines.shape)
    mixed = jnp.sum(paired_inverse(precond)[:, :, None] * spectrum[None], axis=1)
    smoothed_lines = lax.dot_general(
        mixed.reshape(-1, around_cells),
        dft_table(around_cells),
        (((1,), (1,)), ((), ())),
        precision=lax.Precision.HIGH,
    ) / around_cells
    prec_lines = solid_lines * smoothed_lines.reshape(lines.shape)
    group_rows = lines.shape[1]
    lanes = -(-2 * group_rows // 128) * 128
    subl = -(-comp_count // 8) * 8
    edge_at = [(p * sector_width - 1) % around_cells for p in range(sector_count)]
    edge_at += [((p + 1) * sector_width) % around_cells for p in range(sector_count)]
    pick = (jnp.arange(around_cells)[None, :] == jnp.array(edge_at)[:, None]).astype(jnp.float32)
    edges = lax.dot_general(
        pick,
        prec_lines.reshape(-1, around_cells),
        (((1,), (1,)), ((), ())),
        precision=lax.Precision.HIGHEST,
    ).reshape(2, sector_count, comp_count, group_rows)
    cpk = jnp.pad(
        jnp.transpose(edges, (1, 2, 0, 3)).reshape(sector_count, comp_count, 2 * group_rows),
        ((0, 0), (0, subl - comp_count), (0, lanes - 2 * group_rows)),
    )

    def row_pack(row):
        split = jnp.transpose(row.reshape(comp_count, sector_count, sector_width), (1, 0, 2))
        return jnp.pad(split, ((0, 0), (0, subl - comp_count), (0, 0)))

    prec_t, halo_cols, before_rows, after_rows = from_lines_with_halo(
        prec_lines, cpk, row_pack(prec_lines[:, -1]), row_pack(prec_lines[:, 0]), sector_count
    )
    ax = lax.axis_index("ax")
    before_row = jnp.where(ax == 0, 0.0, before_rows[sector_count - 1, :comp_count])
    after_row = jnp.where(ax == lax.axis_size("ax") - 1, 0.0, after_rows[0, :comp_count])
    got_cols = jnp.transpose(halo_cols[:, :comp_count, : 2 * group_rows], (1, 0, 2))
    got_cols = got_cols.reshape(comp_count, sector_count, 2, group_rows)
    before_col = got_cols[:, :, 0].reshape(comp_count, slab_count)
    after_col = got_cols[:, :, 1].reshape(comp_count, slab_count)
    stiffness_t = jnp.transpose(stiffness, (1, 0, 2))
    halo_rows = jnp.pad(jnp.stack([before_row, after_row]), ((0, 0), (0, subl - comp_count), (0, 0)))
    halo_cols = jnp.stack([before_col, after_col])[..., None]
    cell_total = slab_count * lax.axis_size("ax") * comp_count * around_cells
    finished, _, disp_new_t, residual_new_t = image_and_totals(
        residual_t,
        prec_t,
        stiffness_t,
        solid_t[0],
        halo_rows,
        halo_cols,
        jnp.transpose(disp, (1, 0, 2)),
        cell_total,
        0,
    )
    return (
        jnp.transpose(disp_new_t, (1, 0, 2)),
        jnp.transpose(residual_new_t, (1, 0, 2)),
        finished[0, 1:4],
    )


def solution(mesh):
    in_specs = (
        P("ax", None, "sec"),
        P("ax", None, "sec"),
        P("ax", None, "sec"),
        P("ax", "sec"),
        P("ax"),
        P(),
        P(),
    )
    out_specs = (P("ax", None, "sec"), P("ax", None, "sec"), P())
    return jax.shard_map(shards, mesh=mesh, in_specs=in_specs, out_specs=out_specs, check_vma=False)
```

```python
import functools
import math

import jax
import jax.numpy as jnp
from jax import lax
from jax.experimental import pallas as pl
from jax.experimental.pallas import tpu as pltpu
from jax.sharding import PartitionSpec as P


MESH = pl.DeviceIdType.MESH


def _groups():
    me_ax = lax.axis_index("ax")
    me_sec = lax.axis_index("sec")
    x = me_ax % 4
    z = (me_ax // 4) % 8
    ylo = me_ax // 32
    core = me_sec % 2
    yhi = me_sec // 2

    def plane_peer(c):
        y = c % 4
        return ((y % 2) * 32 + z * 4 + (c // 4) % 4, (y // 2) * 2 + c // 16)

    return [
        (32, (core * 4 + x) * 4 + yhi * 2 + ylo, plane_peer),
        (8, z, lambda c: (me_ax - z * 4 + c * 4, me_sec)),
    ]


def _image_and_sums(r_ref, p_ref, s_ref, m_ref, hr_ref, hc_ref, img_ref):
    comps, rows, width = p_ref.shape
    row = lax.broadcasted_iota(jnp.int32, (rows, width), 0)
    lane = lax.broadcasted_iota(jnp.int32, (rows, width), 1)
    solid = m_ref[...]
    acc = [jnp.zeros((1, width), jnp.float32) for _ in range(5)]
    for q in range(comps):
        field = p_ref[q]
        up = jnp.where(row == 0, hr_ref[0, q : q + 1, :], pltpu.roll(field, 1, 0))
        down = jnp.where(row == rows - 1, hr_ref[1, q : q + 1, :], pltpu.roll(field, rows - 1, 0))
        left = jnp.where(lane == 0, hc_ref[0, q], pltpu.roll(field, 1, 1))
        right = jnp.where(lane == width - 1, hc_ref[1, q], pltpu.roll(field, width - 1, 1))
        beside = down + up + right + left
        image = solid * ((s_ref[q] + 4.5) * field - beside - 0.5 * p_ref[q ^ 1])
        img_ref[q] = image
        res = r_ref[q]
        for k, prod in enumerate((res * field, field * image, res * res, res * image, image * image)):
            acc[k] = acc[k] + jnp.sum(prod, axis=0, keepdims=True)
    lane8 = lax.broadcasted_iota(jnp.int32, (8, 128), 1)
    row8 = lax.broadcasted_iota(jnp.int32, (8, 128), 0)
    packed = jnp.zeros((8, 128), jnp.float32)
    for k, a in enumerate(acc):
        packed = jnp.where((row8 == 0) & (lane8 == k), jnp.sum(a), packed)
    return packed


def _finish(total, cell_total):
    lane = lax.broadcasted_iota(jnp.int32, total.shape, 1)
    row = lax.broadcasted_iota(jnp.int32, total.shape, 0)

    def pick(k):
        return jnp.sum(jnp.where((row == 0) & (lane == k), total, 0.0), keepdims=True)

    inner_rz = pick(0) / cell_total
    inner_zq = pick(1) / cell_total
    alpha = inner_rz / inner_zq
    square_new = (pick(2) - alpha * (2.0 * pick(3) - alpha * pick(4))) / cell_total
    out = jnp.zeros(total.shape, jnp.float32)
    for k, v in enumerate((alpha, inner_rz, inner_zq, square_new)):
        out = jnp.where((row == 0) & (lane == k), v, out)
    return out


def _ar_kernel(cell_total, r_ref, p_ref, s_ref, m_ref, hr_ref, hc_ref, o_ref, img_ref, recv_a, recv_b, own, send_sems, recv_sems):
    recvs = (recv_a, recv_b)
    groups = _groups()
    for r in recvs:
        r[...] = jnp.zeros_like(r)
    barrier = pltpu.get_barrier_semaphore()
    count = 0
    for n, mine, dev in groups:
        for d in range(1, n):
            pl.semaphore_signal(barrier, inc=1, device_id=dev((mine + d) % n), device_id_type=MESH)
            count += 1
    own[0] = _image_and_sums(r_ref, p_ref, s_ref, m_ref, hr_ref, hc_ref, img_ref)
    pl.semaphore_wait(barrier, count)
    base = 0
    for g, (n, mine, dev) in enumerate(groups):
        src = own.at[g]
        copies = []
        for d in range(1, n):
            cp = pltpu.make_async_remote_copy(
                src_ref=src,
                dst_ref=recvs[g].at[mine],
                send_sem=send_sems.at[base + d],
                recv_sem=recv_sems.at[base + d],
                device_id=dev((mine + d) % n),
                device_id_type=MESH,
            )
            cp.start()
            copies.append(cp)
        mine_val = src[...]
        for cp in copies:
            cp.wait_recv()
        total = None
        for c in range(n):
            v = jnp.where(mine == c, mine_val, recvs[g][c])
            total = v if total is None else total + v
        for cp in copies:
            cp.wait_send()
        base += n
        if g + 1 < len(groups):
            own[g + 1] = total
        else:
            finished = _finish(total, cell_total)
            o_ref[...] = finished


def image_and_totals(residual, prec, stiffness, solid, halo_rows, halo_cols, cell_total, cid):
    return pl.pallas_call(
        functools.partial(_ar_kernel, float(cell_total)),
        out_shape=[
            jax.ShapeDtypeStruct((8, 128), jnp.float32),
            jax.ShapeDtypeStruct(prec.shape, jnp.float32),
        ],
        in_specs=[pl.BlockSpec(memory_space=pltpu.VMEM)] * 6,
        out_specs=[pl.BlockSpec(memory_space=pltpu.VMEM)] * 2,
        scratch_shapes=[
            pltpu.VMEM((32, 8, 128), jnp.float32),
            pltpu.VMEM((8, 8, 128), jnp.float32),
            pltpu.VMEM((2, 8, 128), jnp.float32),
            pltpu.SemaphoreType.DMA((40,)),
            pltpu.SemaphoreType.DMA((40,)),
        ],
        compiler_params=pltpu.CompilerParams(collective_id=cid, has_side_effects=True),
    )(residual, prec, stiffness, solid, halo_rows, halo_cols)


def _update_kernel(f_ref, d_ref, p_ref, r_ref, i_ref, dn_ref, rn_ref):
    alpha = f_ref[0:1, 0:1]
    dn_ref[0] = d_ref[0] + alpha * p_ref[0]
    rn_ref[0] = r_ref[0] - alpha * i_ref[0]


def apply_step(finished, disp, prec, residual, image):
    comps, rows, width = prec.shape
    plane = pl.BlockSpec((1, rows, width), lambda q: (q, 0, 0))
    return pl.pallas_call(
        _update_kernel,
        grid=(comps,),
        out_shape=[jax.ShapeDtypeStruct(prec.shape, jnp.float32)] * 2,
        in_specs=[pl.BlockSpec((8, 128), lambda q: (0, 0))] + [plane] * 4,
        out_specs=[plane] * 2,
    )(finished, disp, prec, residual, image)


def _to_lines_kernel(n, count, *refs):
    x_refs, o_refs = refs[:count], refs[count : 2 * count]
    send_sems, recv_sems, local_sems = refs[2 * count :]
    me = lax.axis_index("sec")
    ax = lax.axis_index("ax")
    barrier = pltpu.get_barrier_semaphore()
    for d in range(1, n):
        pl.semaphore_signal(barrier, inc=1, device_id=(ax, (me + d) % n), device_id_type=MESH)
    pl.semaphore_wait(barrier, n - 1)
    copies, local = [], []
    for i, (x_ref, o_ref) in enumerate(zip(x_refs, o_refs)):
        rows, width = o_ref.shape[1], x_ref.shape[2]
        dst = o_ref.at[:, :, pl.ds(pl.multiple_of(me * width, width), width)]
        for d in range(1, n):
            peer = (me + d) % n
            cp = pltpu.make_async_remote_copy(
                src_ref=x_ref.at[:, pl.ds(pl.multiple_of(peer * rows, rows), rows), :],
                dst_ref=dst,
                send_sem=send_sems.at[i * n + d],
                recv_sem=recv_sems.at[i * n + d],
                device_id=(ax, peer),
                device_id_type=MESH,
            )
            cp.start()
            copies.append(cp)
        local.append(
            pltpu.make_async_copy(
                x_ref.at[:, pl.ds(pl.multiple_of(me * rows, rows), rows), :], dst, local_sems.at[i]
            )
        )
        local[-1].start()
    for cp in local:
        cp.wait()
    for cp in copies:
        cp.wait()


def to_lines(arrays, n):
    count = len(arrays)
    shapes = [(x.shape[0], x.shape[1] // n, x.shape[2] * n) for x in arrays]
    return pl.pallas_call(
        functools.partial(_to_lines_kernel, n, count),
        out_shape=[jax.ShapeDtypeStruct(s, x.dtype) for s, x in zip(shapes, arrays)],
        in_specs=[pl.BlockSpec(memory_space=pltpu.VMEM)] * count,
        out_specs=[pl.BlockSpec(memory_space=pltpu.VMEM)] * count,
        scratch_shapes=[
            pltpu.SemaphoreType.DMA((count * n,)),
            pltpu.SemaphoreType.DMA((count * n,)),
            pltpu.SemaphoreType.DMA((count,)),
        ],
        compiler_params=pltpu.CompilerParams(collective_id=1, has_side_effects=True),
    )(*arrays)


def _from_lines_kernel(sizes, x_ref, cpk_ref, last_ref, first_ref, o_ref, cols_ref, before_ref,
                       after_ref, send_sems, recv_sems, local_sems):
    n_ax, n = sizes
    me = lax.axis_index("sec")
    ax = lax.axis_index("ax")
    rows, width = x_ref.shape[1], o_ref.shape[2]
    up_ax, down_ax = (ax + 1) % n_ax, (ax + n_ax - 1) % n_ax
    peers = [(ax, (me + d) % n) for d in range(1, n)]
    peers += [(up_ax, s) for s in range(n)] + [(down_ax, s) for s in range(n)]
    barrier = pltpu.get_barrier_semaphore()
    for peer in peers:
        pl.semaphore_signal(barrier, inc=1, device_id=peer, device_id_type=MESH)
    pl.semaphore_wait(barrier, len(peers))
    dst = o_ref.at[:, pl.ds(pl.multiple_of(me * rows, rows), rows), :]
    sends, recvs = [], []
    for d in range(1, n):
        peer = (me + d) % n
        for k, (src, out) in enumerate(
            (
                (x_ref.at[:, :, pl.ds(pl.multiple_of(peer * width, width), width)], dst),
                (cpk_ref.at[peer], cols_ref.at[me]),
            )
        ):
            cp = pltpu.make_async_remote_copy(
                src_ref=src,
                dst_ref=out,
                send_sem=send_sems.at[k * n + d],
                recv_sem=recv_sems.at[k * n + d],
                device_id=(ax, peer),
                device_id_type=MESH,
            )
            cp.start()
            sends.append(cp)
        origin = (me + n - d) % n
        for k, (src, out) in enumerate(
            (
                (x_ref.at[:, :, pl.ds(0, width)], o_ref.at[:, pl.ds(pl.multiple_of(origin * rows, rows), rows), :]),
                (cpk_ref.at[0], cols_ref.at[origin]),
            )
        ):
            recvs.append(
                pltpu.make_async_remote_copy(
                    src_ref=src,
                    dst_ref=out,
                    send_sem=send_sems.at[k * n + d],
                    recv_sem=recv_sems.at[k * n + d],
                    device_id=(ax, origin),
                    device_id_type=MESH,
                )
            )
    for s in range(n):
        for k, (src, out, target) in enumerate(
            ((last_ref.at[s], before_ref.at[me], up_ax), (first_ref.at[s], after_ref.at[me], down_ax))
        ):
            base = (2 + k) * n
            cp = pltpu.make_async_remote_copy(
                src_ref=src,
                dst_ref=out,
                send_sem=send_sems.at[base + s],
                recv_sem=recv_sems.at[base + me],
                device_id=(target, s),
                device_id_type=MESH,
            )
            cp.start()
            sends.append(cp)
            recvs.append(
                pltpu.make_async_remote_copy(
                    src_ref=src,
                    dst_ref=(before_ref, after_ref)[k].at[s],
                    send_sem=send_sems.at[base + s],
                    recv_sem=recv_sems.at[base + s],
                    device_id=(target, s),
                    device_id_type=MESH,
                )
            )
    local = [
        pltpu.make_async_copy(
            x_ref.at[:, :, pl.ds(pl.multiple_of(me * width, width), width)], dst, local_sems.at[0]
        ),
        pltpu.make_async_copy(cpk_ref.at[me], cols_ref.at[me], local_sems.at[1]),
    ]
    for cp in local:
        cp.start()
    for cp in local:
        cp.wait()
    for cp in recvs:
        cp.wait_recv()
    for cp in sends:
        cp.wait_send()


def from_lines_with_halo(x, cpk, last, first, n):
    comps, rows, around = x.shape
    n_ax = lax.axis_size("ax")
    shapes = [
        (comps, rows * n, around // n),
        cpk.shape,
        (n,) + last.shape[1:],
        (n,) + first.shape[1:],
    ]
    return pl.pallas_call(
        functools.partial(_from_lines_kernel, (n_ax, n)),
        out_shape=[jax.ShapeDtypeStruct(s, x.dtype) for s in shapes],
        in_specs=[pl.BlockSpec(memory_space=pltpu.VMEM)] * 4,
        out_specs=[pl.BlockSpec(memory_space=pltpu.VMEM)] * 4,
        scratch_shapes=[
            pltpu.SemaphoreType.DMA((4 * n,)),
            pltpu.SemaphoreType.DMA((4 * n,)),
            pltpu.SemaphoreType.DMA((2,)),
        ],
        compiler_params=pltpu.CompilerParams(collective_id=2, has_side_effects=True),
    )(x, cpk, last, first)


def dft_table(length):
    half = length // 2
    root = int(round(math.sqrt(length)))
    cols = jnp.concatenate([jnp.arange(half + 1), jnp.arange(1, half)])
    phase = jnp.where(jnp.arange(length) > half, 0.5 * math.pi, 0.0).astype(jnp.float32)
    step = 2.0 * math.pi / length
    coarse = step * ((root * jnp.arange(length // root)[:, None] * cols[None, :]) % length).astype(jnp.float32)
    fine = step * ((jnp.arange(root)[:, None] * cols[None, :]) % length).astype(jnp.float32) - phase
    table = jnp.cos(coarse)[:, None] * jnp.cos(fine)[None] - jnp.sin(coarse)[:, None] * jnp.sin(fine)[None]
    return table.reshape(length, length)


def paired_inverse(precond):
    length = precond.shape[2]
    half = length // 2
    low = precond[:, :, : half + 1]
    mirror = jnp.flip(precond[:, :, half + 1 :], axis=2)
    inner = jnp.concatenate([jnp.zeros_like(low[:, :, :1]), mirror, jnp.zeros_like(low[:, :, :1])], axis=2)
    paired = low + inner
    return jnp.concatenate([paired, paired[:, :, 1:half]], axis=2)


def with_halo(x, sides, width, wrap):
    for axis, dim in sides:
        size, length = (lax.axis_size(axis), x.shape[dim])
        up = [(i, (i + 1) % size) for i in range(size if wrap else size - 1)]
        down = [(j, i) for i, j in up]
        last = lax.slice_in_dim(x, length - width, length, axis=dim)
        first = lax.slice_in_dim(x, 0, width, axis=dim)
        before = lax.ppermute(last, axis, up)
        after = lax.ppermute(first, axis, down)
        x = jnp.concatenate([before, x, after], axis=dim)
    return x


def swap_channels(field):
    extent = field.shape
    folded = field.reshape((extent[0] // 2, 2) + extent[1:])
    return jnp.flip(folded, axis=1).reshape(extent)


def swap_radial(field):
    extent = field.shape
    folded = field.reshape(extent[0], extent[1] // 2, 2, extent[2])
    return jnp.flip(folded, axis=2).reshape(extent)


def apply_operator(field, stiffness):
    axial_pad = with_halo(field, (("ax", 0),), 1, False)
    sector_pad = with_halo(field, (("sec", 2),), 1, True)
    beside = axial_pad[2:] + axial_pad[:-2]
    beside = beside + sector_pad[:, :, 2:] + sector_pad[:, :, :-2]
    return (stiffness + 4.5) * field - beside - 0.5 * swap_radial(field)


def shards(load, disp, stiff, hole, section_class, class_table, precond):
    slab_count, comp_count, sector_width = disp.shape
    sector_count = lax.axis_size("sec")
    around_cells = sector_width * sector_count
    total_axial = slab_count * lax.axis_size("ax")
    position = lax.axis_index("ax") * slab_count + jnp.arange(slab_count)
    taper = 1.0 + 2.0 * position.astype(jnp.float32) / (total_axial - 1)
    one_hot = (section_class[:, None] == jnp.arange(class_table.shape[0])[None, :]).astype(
        jnp.float32
    )
    factors = jnp.dot(one_hot, class_table, precision=lax.Precision.HIGHEST)
    stiffness = stiff * (factors * taper[:, None])[:, :, None]
    solid = (1 - hole).astype(jnp.float32)[:, None, :]
    residual = solid * (load - apply_operator(disp, stiffness))
    residual_t = jnp.transpose(residual, (1, 0, 2))
    solid_t = jnp.transpose(solid, (1, 0, 2))
    lines, solid_lines = to_lines([residual_t, solid_t], sector_count)
    spectrum = jnp.dot(
        lines.reshape(-1, around_cells), dft_table(around_cells), precision=lax.Precision.HIGH
    ).reshape(lines.shape)
    mixed = jnp.sum(paired_inverse(precond)[:, :, None] * spectrum[None], axis=1)
    smoothed_lines = lax.dot_general(
        mixed.reshape(-1, around_cells),
        dft_table(around_cells),
        (((1,), (1,)), ((), ())),
        precision=lax.Precision.HIGH,
    ) / around_cells
    prec_lines = solid_lines * smoothed_lines.reshape(lines.shape)
    group_rows = lines.shape[1]
    lanes = -(-2 * group_rows // 128) * 128
    subl = -(-comp_count // 8) * 8
    edge_at = [(p * sector_width - 1) % around_cells for p in range(sector_count)]
    edge_at += [((p + 1) * sector_width) % around_cells for p in range(sector_count)]
    pick = (jnp.arange(around_cells)[None, :] == jnp.array(edge_at)[:, None]).astype(jnp.float32)
    edges = lax.dot_general(
        pick,
        prec_lines.reshape(-1, around_cells),
        (((1,), (1,)), ((), ())),
        precision=lax.Precision.HIGHEST,
    ).reshape(2, sector_count, comp_count, group_rows)
    cpk = jnp.pad(
        jnp.transpose(edges, (1, 2, 0, 3)).reshape(sector_count, comp_count, 2 * group_rows),
        ((0, 0), (0, subl - comp_count), (0, lanes - 2 * group_rows)),
    )

    def row_pack(row):
        split = jnp.transpose(row.reshape(comp_count, sector_count, sector_width), (1, 0, 2))
        return jnp.pad(split, ((0, 0), (0, subl - comp_count), (0, 0)))

    prec_t, halo_cols, before_rows, after_rows = from_lines_with_halo(
        prec_lines, cpk, row_pack(prec_lines[:, -1]), row_pack(prec_lines[:, 0]), sector_count
    )
    ax = lax.axis_index("ax")
    before_row = jnp.where(ax == 0, 0.0, before_rows[sector_count - 1, :comp_count])
    after_row = jnp.where(ax == lax.axis_size("ax") - 1, 0.0, after_rows[0, :comp_count])
    got_cols = jnp.transpose(halo_cols[:, :comp_count, : 2 * group_rows], (1, 0, 2))
    got_cols = got_cols.reshape(comp_count, sector_count, 2, group_rows)
    before_col = got_cols[:, :, 0].reshape(comp_count, slab_count)
    after_col = got_cols[:, :, 1].reshape(comp_count, slab_count)
    stiffness_t = jnp.transpose(stiffness, (1, 0, 2))
    halo_rows = jnp.pad(jnp.stack([before_row, after_row]), ((0, 0), (0, subl - comp_count), (0, 0)))
    halo_cols = jnp.stack([before_col, after_col])[..., None]
    cell_total = slab_count * lax.axis_size("ax") * comp_count * around_cells
    finished, image_t = image_and_totals(
        residual_t, prec_t, stiffness_t, solid_t[0], halo_rows, halo_cols, cell_total, 0
    )
    disp_new_t, residual_new_t = apply_step(
        finished, jnp.transpose(disp, (1, 0, 2)), prec_t, residual_t, image_t
    )
    return (
        jnp.transpose(disp_new_t, (1, 0, 2)),
        jnp.transpose(residual_new_t, (1, 0, 2)),
        finished[0, 1:4],
    )


def solution(mesh):
    in_specs = (
        P("ax", None, "sec"),
        P("ax", None, "sec"),
        P("ax", None, "sec"),
        P("ax", "sec"),
        P("ax"),
        P(),
        P(),
    )
    out_specs = (P("ax", None, "sec"), P("ax", None, "sec"), P())
    return jax.shard_map(shards, mesh=mesh, in_specs=in_specs, out_specs=out_specs, check_vma=False)
```

```python
import functools
import math

import jax
import jax.numpy as jnp
from jax import lax
from jax.experimental import pallas as pl
from jax.experimental.pallas import tpu as pltpu
from jax.sharding import PartitionSpec as P


MESH = pl.DeviceIdType.MESH


def _groups():
    me_ax = lax.axis_index("ax")
    me_sec = lax.axis_index("sec")
    x = me_ax % 4
    z = (me_ax // 4) % 8
    ylo = me_ax // 32
    core = me_sec % 2
    yhi = me_sec // 2

    def plane_peer(c):
        y = c % 4
        return ((y % 2) * 32 + z * 4 + (c // 4) % 4, (y // 2) * 2 + c // 16)

    return [
        (32, (core * 4 + x) * 4 + yhi * 2 + ylo, plane_peer),
        (8, z, lambda c: (me_ax - z * 4 + c * 4, me_sec)),
    ]


def _image_and_sums(r_ref, p_ref, s_ref, m_ref, hr_ref, hc_ref, img_ref):
    comps, rows, width = p_ref.shape
    row = lax.broadcasted_iota(jnp.int32, (rows, width), 0)
    lane = lax.broadcasted_iota(jnp.int32, (rows, width), 1)
    solid = m_ref[...]
    acc = [jnp.zeros((1, width), jnp.float32) for _ in range(5)]
    for q in range(comps):
        field = p_ref[q]
        up = jnp.where(row == 0, hr_ref[0, q : q + 1, :], pltpu.roll(field, 1, 0))
        down = jnp.where(row == rows - 1, hr_ref[1, q : q + 1, :], pltpu.roll(field, rows - 1, 0))
        left = jnp.where(lane == 0, hc_ref[0, q], pltpu.roll(field, 1, 1))
        right = jnp.where(lane == width - 1, hc_ref[1, q], pltpu.roll(field, width - 1, 1))
        beside = down + up + right + left
        image = solid * ((s_ref[q] + 4.5) * field - beside - 0.5 * p_ref[q ^ 1])
        img_ref[q] = image
        res = r_ref[q]
        for k, prod in enumerate((res * field, field * image, res * res, res * image, image * image)):
            acc[k] = acc[k] + jnp.sum(prod, axis=0, keepdims=True)
    lane8 = lax.broadcasted_iota(jnp.int32, (8, 128), 1)
    row8 = lax.broadcasted_iota(jnp.int32, (8, 128), 0)
    packed = jnp.zeros((8, 128), jnp.float32)
    for k, a in enumerate(acc):
        packed = jnp.where((row8 == 0) & (lane8 == k), jnp.sum(a), packed)
    return packed


def _finish(total, cell_total):
    lane = lax.broadcasted_iota(jnp.int32, total.shape, 1)
    row = lax.broadcasted_iota(jnp.int32, total.shape, 0)

    def pick(k):
        return jnp.sum(jnp.where((row == 0) & (lane == k), total, 0.0), keepdims=True)

    inner_rz = pick(0) / cell_total
    inner_zq = pick(1) / cell_total
    alpha = inner_rz / inner_zq
    square_new = (pick(2) - alpha * (2.0 * pick(3) - alpha * pick(4))) / cell_total
    out = jnp.zeros(total.shape, jnp.float32)
    for k, v in enumerate((alpha, inner_rz, inner_zq, square_new)):
        out = jnp.where((row == 0) & (lane == k), v, out)
    return out


def _ar_kernel(cell_total, r_ref, p_ref, s_ref, m_ref, hr_ref, hc_ref, o_ref, img_ref, recv_a, recv_b, own, send_sems, recv_sems):
    recvs = (recv_a, recv_b)
    groups = _groups()
    for r in recvs:
        r[...] = jnp.zeros_like(r)
    barrier = pltpu.get_barrier_semaphore()
    count = 0
    for n, mine, dev in groups:
        for d in range(1, n):
            pl.semaphore_signal(barrier, inc=1, device_id=dev((mine + d) % n), device_id_type=MESH)
            count += 1
    own[0] = _image_and_sums(r_ref, p_ref, s_ref, m_ref, hr_ref, hc_ref, img_ref)
    pl.semaphore_wait(barrier, count)
    base = 0
    for g, (n, mine, dev) in enumerate(groups):
        src = own.at[g]
        copies = []
        for d in range(1, n):
            cp = pltpu.make_async_remote_copy(
                src_ref=src,
                dst_ref=recvs[g].at[mine],
                send_sem=send_sems.at[base + d],
                recv_sem=recv_sems.at[base + d],
                device_id=dev((mine + d) % n),
                device_id_type=MESH,
            )
            cp.start()
            copies.append(cp)
        mine_val = src[...]
        for cp in copies:
            cp.wait_recv()
        total = None
        for c in range(n):
            v = jnp.where(mine == c, mine_val, recvs[g][c])
            total = v if total is None else total + v
        for cp in copies:
            cp.wait_send()
        base += n
        if g + 1 < len(groups):
            own[g + 1] = total
        else:
            finished = _finish(total, cell_total)
            o_ref[...] = finished


def image_and_totals(residual, prec, stiffness, solid, halo_rows, halo_cols, cell_total, cid):
    return pl.pallas_call(
        functools.partial(_ar_kernel, float(cell_total)),
        out_shape=[
            jax.ShapeDtypeStruct((8, 128), jnp.float32),
            jax.ShapeDtypeStruct(prec.shape, jnp.float32),
        ],
        in_specs=[pl.BlockSpec(memory_space=pltpu.VMEM)] * 6,
        out_specs=[pl.BlockSpec(memory_space=pltpu.VMEM)] * 2,
        scratch_shapes=[
            pltpu.VMEM((32, 8, 128), jnp.float32),
            pltpu.VMEM((8, 8, 128), jnp.float32),
            pltpu.VMEM((2, 8, 128), jnp.float32),
            pltpu.SemaphoreType.DMA((40,)),
            pltpu.SemaphoreType.DMA((40,)),
        ],
        compiler_params=pltpu.CompilerParams(collective_id=cid, has_side_effects=True),
    )(residual, prec, stiffness, solid, halo_rows, halo_cols)


def _update_kernel(f_ref, d_ref, p_ref, r_ref, i_ref, dn_ref, rn_ref):
    alpha = f_ref[0:1, 0:1]
    for q in range(d_ref.shape[0]):
        dn_ref[q] = d_ref[q] + alpha * p_ref[q]
        rn_ref[q] = r_ref[q] - alpha * i_ref[q]


def apply_step(finished, disp, prec, residual, image):
    comps, rows, width = prec.shape
    steps = 2 if comps % 2 == 0 else 1
    plane = pl.BlockSpec((comps // steps, rows, width), lambda q: (q, 0, 0))
    return pl.pallas_call(
        _update_kernel,
        grid=(steps,),
        out_shape=[jax.ShapeDtypeStruct(prec.shape, jnp.float32)] * 2,
        in_specs=[pl.BlockSpec((8, 128), lambda q: (0, 0))] + [plane] * 4,
        out_specs=[plane] * 2,
    )(finished, disp, prec, residual, image)


def _to_lines_kernel(n, count, *refs):
    x_refs, o_refs = refs[:count], refs[count : 2 * count]
    send_sems, recv_sems, local_sems = refs[2 * count :]
    me = lax.axis_index("sec")
    ax = lax.axis_index("ax")
    barrier = pltpu.get_barrier_semaphore()
    for d in range(1, n):
        pl.semaphore_signal(barrier, inc=1, device_id=(ax, (me + d) % n), device_id_type=MESH)
    pl.semaphore_wait(barrier, n - 1)
    copies, local = [], []
    for i, (x_ref, o_ref) in enumerate(zip(x_refs, o_refs)):
        rows, width = o_ref.shape[1], x_ref.shape[2]
        dst = o_ref.at[:, :, pl.ds(pl.multiple_of(me * width, width), width)]
        for d in range(1, n):
            peer = (me + d) % n
            cp = pltpu.make_async_remote_copy(
                src_ref=x_ref.at[:, pl.ds(pl.multiple_of(peer * rows, rows), rows), :],
                dst_ref=dst,
                send_sem=send_sems.at[i * n + d],
                recv_sem=recv_sems.at[i * n + d],
                device_id=(ax, peer),
                device_id_type=MESH,
            )
            cp.start()
            copies.append(cp)
        local.append(
            pltpu.make_async_copy(
                x_ref.at[:, pl.ds(pl.multiple_of(me * rows, rows), rows), :], dst, local_sems.at[i]
            )
        )
        local[-1].start()
    for cp in local:
        cp.wait()
    for cp in copies:
        cp.wait()


def to_lines(arrays, n):
    count = len(arrays)
    shapes = [(x.shape[0], x.shape[1] // n, x.shape[2] * n) for x in arrays]
    return pl.pallas_call(
        functools.partial(_to_lines_kernel, n, count),
        out_shape=[jax.ShapeDtypeStruct(s, x.dtype) for s, x in zip(shapes, arrays)],
        in_specs=[pl.BlockSpec(memory_space=pltpu.VMEM)] * count,
        out_specs=[pl.BlockSpec(memory_space=pltpu.VMEM)] * count,
        scratch_shapes=[
            pltpu.SemaphoreType.DMA((count * n,)),
            pltpu.SemaphoreType.DMA((count * n,)),
            pltpu.SemaphoreType.DMA((count,)),
        ],
        compiler_params=pltpu.CompilerParams(collective_id=1, has_side_effects=True),
    )(*arrays)


def _from_lines_kernel(sizes, x_ref, cpk_ref, last_ref, first_ref, o_ref, cols_ref, before_ref,
                       after_ref, send_sems, recv_sems, local_sems):
    n_ax, n = sizes
    me = lax.axis_index("sec")
    ax = lax.axis_index("ax")
    rows, width = x_ref.shape[1], o_ref.shape[2]
    up_ax, down_ax = (ax + 1) % n_ax, (ax + n_ax - 1) % n_ax
    peers = [(ax, (me + d) % n) for d in range(1, n)]
    peers += [(up_ax, s) for s in range(n)] + [(down_ax, s) for s in range(n)]
    barrier = pltpu.get_barrier_semaphore()
    for peer in peers:
        pl.semaphore_signal(barrier, inc=1, device_id=peer, device_id_type=MESH)
    pl.semaphore_wait(barrier, len(peers))
    dst = o_ref.at[:, pl.ds(pl.multiple_of(me * rows, rows), rows), :]
    sends, recvs = [], []
    for d in range(1, n):
        peer = (me + d) % n
        for k, (src, out) in enumerate(
            (
                (x_ref.at[:, :, pl.ds(pl.multiple_of(peer * width, width), width)], dst),
                (cpk_ref.at[peer], cols_ref.at[me]),
            )
        ):
            cp = pltpu.make_async_remote_copy(
                src_ref=src,
                dst_ref=out,
                send_sem=send_sems.at[k * n + d],
                recv_sem=recv_sems.at[k * n + d],
                device_id=(ax, peer),
                device_id_type=MESH,
            )
            cp.start()
            sends.append(cp)
        origin = (me + n - d) % n
        for k, (src, out) in enumerate(
            (
                (x_ref.at[:, :, pl.ds(0, width)], o_ref.at[:, pl.ds(pl.multiple_of(origin * rows, rows), rows), :]),
                (cpk_ref.at[0], cols_ref.at[origin]),
            )
        ):
            recvs.append(
                pltpu.make_async_remote_copy(
                    src_ref=src,
                    dst_ref=out,
                    send_sem=send_sems.at[k * n + d],
                    recv_sem=recv_sems.at[k * n + d],
                    device_id=(ax, origin),
                    device_id_type=MESH,
                )
            )
    for s in range(n):
        for k, (src, out, target) in enumerate(
            ((last_ref.at[s], before_ref.at[me], up_ax), (first_ref.at[s], after_ref.at[me], down_ax))
        ):
            base = (2 + k) * n
            cp = pltpu.make_async_remote_copy(
                src_ref=src,
                dst_ref=out,
                send_sem=send_sems.at[base + s],
                recv_sem=recv_sems.at[base + me],
                device_id=(target, s),
                device_id_type=MESH,
            )
            cp.start()
            sends.append(cp)
            recvs.append(
                pltpu.make_async_remote_copy(
                    src_ref=src,
                    dst_ref=(before_ref, after_ref)[k].at[s],
                    send_sem=send_sems.at[base + s],
                    recv_sem=recv_sems.at[base + s],
                    device_id=(target, s),
                    device_id_type=MESH,
                )
            )
    local = [
        pltpu.make_async_copy(
            x_ref.at[:, :, pl.ds(pl.multiple_of(me * width, width), width)], dst, local_sems.at[0]
        ),
        pltpu.make_async_copy(cpk_ref.at[me], cols_ref.at[me], local_sems.at[1]),
    ]
    for cp in local:
        cp.start()
    for cp in local:
        cp.wait()
    for cp in recvs:
        cp.wait_recv()
    for cp in sends:
        cp.wait_send()


def from_lines_with_halo(x, cpk, last, first, n):
    comps, rows, around = x.shape
    n_ax = lax.axis_size("ax")
    shapes = [
        (comps, rows * n, around // n),
        cpk.shape,
        (n,) + last.shape[1:],
        (n,) + first.shape[1:],
    ]
    return pl.pallas_call(
        functools.partial(_from_lines_kernel, (n_ax, n)),
        out_shape=[jax.ShapeDtypeStruct(s, x.dtype) for s in shapes],
        in_specs=[pl.BlockSpec(memory_space=pltpu.VMEM)] * 4,
        out_specs=[pl.BlockSpec(memory_space=pltpu.VMEM)] * 4,
        scratch_shapes=[
            pltpu.SemaphoreType.DMA((4 * n,)),
            pltpu.SemaphoreType.DMA((4 * n,)),
            pltpu.SemaphoreType.DMA((2,)),
        ],
        compiler_params=pltpu.CompilerParams(collective_id=2, has_side_effects=True),
    )(x, cpk, last, first)


def dft_table(length):
    half = length // 2
    root = int(round(math.sqrt(length)))
    cols = jnp.concatenate([jnp.arange(half + 1), jnp.arange(1, half)])
    phase = jnp.where(jnp.arange(length) > half, 0.5 * math.pi, 0.0).astype(jnp.float32)
    step = 2.0 * math.pi / length
    coarse = step * ((root * jnp.arange(length // root)[:, None] * cols[None, :]) % length).astype(jnp.float32)
    fine = step * ((jnp.arange(root)[:, None] * cols[None, :]) % length).astype(jnp.float32) - phase
    table = jnp.cos(coarse)[:, None] * jnp.cos(fine)[None] - jnp.sin(coarse)[:, None] * jnp.sin(fine)[None]
    return table.reshape(length, length)


def paired_inverse(precond):
    length = precond.shape[2]
    half = length // 2
    low = precond[:, :, : half + 1]
    mirror = jnp.flip(precond[:, :, half + 1 :], axis=2)
    inner = jnp.concatenate([jnp.zeros_like(low[:, :, :1]), mirror, jnp.zeros_like(low[:, :, :1])], axis=2)
    paired = low + inner
    return jnp.concatenate([paired, paired[:, :, 1:half]], axis=2)


def with_halo(x, sides, width, wrap):
    for axis, dim in sides:
        size, length = (lax.axis_size(axis), x.shape[dim])
        up = [(i, (i + 1) % size) for i in range(size if wrap else size - 1)]
        down = [(j, i) for i, j in up]
        last = lax.slice_in_dim(x, length - width, length, axis=dim)
        first = lax.slice_in_dim(x, 0, width, axis=dim)
        before = lax.ppermute(last, axis, up)
        after = lax.ppermute(first, axis, down)
        x = jnp.concatenate([before, x, after], axis=dim)
    return x


def swap_channels(field):
    extent = field.shape
    folded = field.reshape((extent[0] // 2, 2) + extent[1:])
    return jnp.flip(folded, axis=1).reshape(extent)


def swap_radial(field):
    extent = field.shape
    folded = field.reshape(extent[0], extent[1] // 2, 2, extent[2])
    return jnp.flip(folded, axis=2).reshape(extent)


def apply_operator(field, stiffness):
    axial_pad = with_halo(field, (("ax", 0),), 1, False)
    sector_pad = with_halo(field, (("sec", 2),), 1, True)
    beside = axial_pad[2:] + axial_pad[:-2]
    beside = beside + sector_pad[:, :, 2:] + sector_pad[:, :, :-2]
    return (stiffness + 4.5) * field - beside - 0.5 * swap_radial(field)


def shards(load, disp, stiff, hole, section_class, class_table, precond):
    slab_count, comp_count, sector_width = disp.shape
    sector_count = lax.axis_size("sec")
    around_cells = sector_width * sector_count
    total_axial = slab_count * lax.axis_size("ax")
    position = lax.axis_index("ax") * slab_count + jnp.arange(slab_count)
    taper = 1.0 + 2.0 * position.astype(jnp.float32) / (total_axial - 1)
    one_hot = (section_class[:, None] == jnp.arange(class_table.shape[0])[None, :]).astype(
        jnp.float32
    )
    factors = jnp.dot(one_hot, class_table, precision=lax.Precision.HIGHEST)
    stiffness = stiff * (factors * taper[:, None])[:, :, None]
    solid = (1 - hole).astype(jnp.float32)[:, None, :]
    residual = solid * (load - apply_operator(disp, stiffness))
    residual_t = jnp.transpose(residual, (1, 0, 2))
    solid_t = jnp.transpose(solid, (1, 0, 2))
    lines, solid_lines = to_lines([residual_t, solid_t], sector_count)
    spectrum = jnp.dot(
        lines.reshape(-1, around_cells), dft_table(around_cells), precision=lax.Precision.HIGH
    ).reshape(lines.shape)
    mixed = jnp.sum(paired_inverse(precond)[:, :, None] * spectrum[None], axis=1)
    smoothed_lines = lax.dot_general(
        mixed.reshape(-1, around_cells),
        dft_table(around_cells),
        (((1,), (1,)), ((), ())),
        precision=lax.Precision.HIGH,
    ) / around_cells
    prec_lines = solid_lines * smoothed_lines.reshape(lines.shape)
    group_rows = lines.shape[1]
    lanes = -(-2 * group_rows // 128) * 128
    subl = -(-comp_count // 8) * 8
    edge_at = [(p * sector_width - 1) % around_cells for p in range(sector_count)]
    edge_at += [((p + 1) * sector_width) % around_cells for p in range(sector_count)]
    pick = (jnp.arange(around_cells)[None, :] == jnp.array(edge_at)[:, None]).astype(jnp.float32)
    edges = lax.dot_general(
        pick,
        prec_lines.reshape(-1, around_cells),
        (((1,), (1,)), ((), ())),
        precision=lax.Precision.HIGHEST,
    ).reshape(2, sector_count, comp_count, group_rows)
    cpk = jnp.pad(
        jnp.transpose(edges, (1, 2, 0, 3)).reshape(sector_count, comp_count, 2 * group_rows),
        ((0, 0), (0, subl - comp_count), (0, lanes - 2 * group_rows)),
    )

    def row_pack(row):
        split = jnp.transpose(row.reshape(comp_count, sector_count, sector_width), (1, 0, 2))
        return jnp.pad(split, ((0, 0), (0, subl - comp_count), (0, 0)))

    prec_t, halo_cols, before_rows, after_rows = from_lines_with_halo(
        prec_lines, cpk, row_pack(prec_lines[:, -1]), row_pack(prec_lines[:, 0]), sector_count
    )
    ax = lax.axis_index("ax")
    before_row = jnp.where(ax == 0, 0.0, before_rows[sector_count - 1, :comp_count])
    after_row = jnp.where(ax == lax.axis_size("ax") - 1, 0.0, after_rows[0, :comp_count])
    got_cols = jnp.transpose(halo_cols[:, :comp_count, : 2 * group_rows], (1, 0, 2))
    got_cols = got_cols.reshape(comp_count, sector_count, 2, group_rows)
    before_col = got_cols[:, :, 0].reshape(comp_count, slab_count)
    after_col = got_cols[:, :, 1].reshape(comp_count, slab_count)
    stiffness_t = jnp.transpose(stiffness, (1, 0, 2))
    halo_rows = jnp.pad(jnp.stack([before_row, after_row]), ((0, 0), (0, subl - comp_count), (0, 0)))
    halo_cols = jnp.stack([before_col, after_col])[..., None]
    cell_total = slab_count * lax.axis_size("ax") * comp_count * around_cells
    finished, image_t = image_and_totals(
        residual_t, prec_t, stiffness_t, solid_t[0], halo_rows, halo_cols, cell_total, 0
    )
    disp_new_t, residual_new_t = apply_step(
        finished, jnp.transpose(disp, (1, 0, 2)), prec_t, residual_t, image_t
    )
    return (
        jnp.transpose(disp_new_t, (1, 0, 2)),
        jnp.transpose(residual_new_t, (1, 0, 2)),
        finished[0, 1:4],
    )


def solution(mesh):
    in_specs = (
        P("ax", None, "sec"),
        P("ax", None, "sec"),
        P("ax", None, "sec"),
        P("ax", "sec"),
        P("ax"),
        P(),
        P(),
    )
    out_specs = (P("ax", None, "sec"), P("ax", None, "sec"), P())
    return jax.shard_map(shards, mesh=mesh, in_specs=in_specs, out_specs=out_specs, check_vma=False)
```

```python
import functools
import math

import jax
import jax.numpy as jnp
from jax import lax
from jax.experimental import pallas as pl
from jax.experimental.pallas import tpu as pltpu
from jax.sharding import PartitionSpec as P


MESH = pl.DeviceIdType.MESH


def _groups():
    me_ax = lax.axis_index("ax")
    me_sec = lax.axis_index("sec")
    x = me_ax % 4
    z = (me_ax // 4) % 8
    ylo = me_ax // 32
    core = me_sec % 2
    yhi = me_sec // 2

    def plane_peer(c):
        y = c % 4
        return ((y % 2) * 32 + z * 4 + (c // 4) % 4, (y // 2) * 2 + c // 16)

    return [
        (32, (core * 4 + x) * 4 + yhi * 2 + ylo, plane_peer),
        (8, z, lambda c: (me_ax - z * 4 + c * 4, me_sec)),
    ]


def _image_and_sums(r_ref, p_ref, s_ref, m_ref, hr_ref, hc_ref, img_ref):
    comps, rows, width = p_ref.shape
    row = lax.broadcasted_iota(jnp.int32, (rows, width), 0)
    lane = lax.broadcasted_iota(jnp.int32, (rows, width), 1)
    solid = m_ref[...]
    acc = [jnp.zeros((1, width), jnp.float32) for _ in range(5)]
    for q in range(comps):
        field = p_ref[q]
        up = jnp.where(row == 0, hr_ref[0, q : q + 1, :], pltpu.roll(field, 1, 0))
        down = jnp.where(row == rows - 1, hr_ref[1, q : q + 1, :], pltpu.roll(field, rows - 1, 0))
        left = jnp.where(lane == 0, hc_ref[0, q], pltpu.roll(field, 1, 1))
        right = jnp.where(lane == width - 1, hc_ref[1, q], pltpu.roll(field, width - 1, 1))
        beside = down + up + right + left
        image = solid * ((s_ref[q] + 4.5) * field - beside - 0.5 * p_ref[q ^ 1])
        img_ref[q] = image
        res = r_ref[q]
        for k, prod in enumerate((res * field, field * image, res * res, res * image, image * image)):
            acc[k] = acc[k] + jnp.sum(prod, axis=0, keepdims=True)
    lane8 = lax.broadcasted_iota(jnp.int32, (8, 128), 1)
    row8 = lax.broadcasted_iota(jnp.int32, (8, 128), 0)
    packed = jnp.zeros((8, 128), jnp.float32)
    for k, a in enumerate(acc):
        packed = jnp.where((row8 == 0) & (lane8 == k), jnp.sum(a), packed)
    return packed


def _finish(total, cell_total):
    lane = lax.broadcasted_iota(jnp.int32, total.shape, 1)
    row = lax.broadcasted_iota(jnp.int32, total.shape, 0)

    def pick(k):
        return jnp.sum(jnp.where((row == 0) & (lane == k), total, 0.0), keepdims=True)

    inner_rz = pick(0) / cell_total
    inner_zq = pick(1) / cell_total
    alpha = inner_rz / inner_zq
    square_new = (pick(2) - alpha * (2.0 * pick(3) - alpha * pick(4))) / cell_total
    out = jnp.zeros(total.shape, jnp.float32)
    for k, v in enumerate((alpha, inner_rz, inner_zq, square_new)):
        out = jnp.where((row == 0) & (lane == k), v, out)
    return out


def _ar_kernel(cell_total, r_ref, p_ref, s_ref, m_ref, hr_ref, hc_ref, o_ref, img_ref, recv_a, recv_b, own, send_sems, recv_sems):
    recvs = (recv_a, recv_b)
    groups = _groups()
    for r in recvs:
        r[...] = jnp.zeros_like(r)
    barrier = pltpu.get_barrier_semaphore()
    count = 0
    for n, mine, dev in groups:
        for d in range(1, n):
            pl.semaphore_signal(barrier, inc=1, device_id=dev((mine + d) % n), device_id_type=MESH)
            count += 1
    own[0] = _image_and_sums(r_ref, p_ref, s_ref, m_ref, hr_ref, hc_ref, img_ref)
    pl.semaphore_wait(barrier, count)
    base = 0
    for g, (n, mine, dev) in enumerate(groups):
        src = own.at[g]
        copies = []
        for d in range(1, n):
            cp = pltpu.make_async_remote_copy(
                src_ref=src,
                dst_ref=recvs[g].at[mine],
                send_sem=send_sems.at[base + d],
                recv_sem=recv_sems.at[base + d],
                device_id=dev((mine + d) % n),
                device_id_type=MESH,
            )
            cp.start()
            copies.append(cp)
        mine_val = src[...]
        for cp in copies:
            cp.wait_recv()
        total = None
        for c in range(n):
            v = jnp.where(mine == c, mine_val, recvs[g][c])
            total = v if total is None else total + v
        for cp in copies:
            cp.wait_send()
        base += n
        if g + 1 < len(groups):
            own[g + 1] = total
        else:
            finished = _finish(total, cell_total)
            o_ref[...] = finished


def image_and_totals(residual, prec, stiffness, solid, halo_rows, halo_cols, cell_total, cid):
    return pl.pallas_call(
        functools.partial(_ar_kernel, float(cell_total)),
        out_shape=[
            jax.ShapeDtypeStruct((8, 128), jnp.float32),
            jax.ShapeDtypeStruct(prec.shape, jnp.float32),
        ],
        in_specs=[pl.BlockSpec(memory_space=pltpu.VMEM)] * 6,
        out_specs=[pl.BlockSpec(memory_space=pltpu.VMEM)] * 2,
        scratch_shapes=[
            pltpu.VMEM((32, 8, 128), jnp.float32),
            pltpu.VMEM((8, 8, 128), jnp.float32),
            pltpu.VMEM((2, 8, 128), jnp.float32),
            pltpu.SemaphoreType.DMA((40,)),
            pltpu.SemaphoreType.DMA((40,)),
        ],
        compiler_params=pltpu.CompilerParams(collective_id=cid, has_side_effects=True),
    )(residual, prec, stiffness, solid, halo_rows, halo_cols)


def _update_kernel(f_ref, d_ref, p_ref, r_ref, i_ref, dn_ref, rn_ref):
    alpha = f_ref[0:1, 0:1]
    for q in range(d_ref.shape[0]):
        dn_ref[q] = d_ref[q] + alpha * p_ref[q]
        rn_ref[q] = r_ref[q] - alpha * i_ref[q]


def apply_step(finished, disp, prec, residual, image):
    comps, rows, width = prec.shape
    steps = 2 if comps % 2 == 0 else 1
    plane = pl.BlockSpec((comps // steps, rows, width), lambda q: (q, 0, 0))
    return pl.pallas_call(
        _update_kernel,
        grid=(steps,),
        out_shape=[jax.ShapeDtypeStruct(prec.shape, jnp.float32)] * 2,
        in_specs=[pl.BlockSpec((8, 128), lambda q: (0, 0))] + [plane] * 4,
        out_specs=[plane] * 2,
    )(finished, disp, prec, residual, image)


def _to_lines_kernel(n, count, *refs):
    x_refs, o_refs = refs[:count], refs[count : 2 * count]
    send_sems, recv_sems, local_sems = refs[2 * count :]
    me = lax.axis_index("sec")
    ax = lax.axis_index("ax")
    barrier = pltpu.get_barrier_semaphore()
    for d in range(1, n):
        pl.semaphore_signal(barrier, inc=1, device_id=(ax, (me + d) % n), device_id_type=MESH)
    pl.semaphore_wait(barrier, n - 1)
    copies, local = [], []
    for i, (x_ref, o_ref) in enumerate(zip(x_refs, o_refs)):
        rows, width = o_ref.shape[1], x_ref.shape[2]
        dst = o_ref.at[:, :, pl.ds(pl.multiple_of(me * width, width), width)]
        for d in range(1, n):
            peer = (me + d) % n
            cp = pltpu.make_async_remote_copy(
                src_ref=x_ref.at[:, pl.ds(pl.multiple_of(peer * rows, rows), rows), :],
                dst_ref=dst,
                send_sem=send_sems.at[i * n + d],
                recv_sem=recv_sems.at[i * n + d],
                device_id=(ax, peer),
                device_id_type=MESH,
            )
            cp.start()
            copies.append(cp)
        local.append(
            pltpu.make_async_copy(
                x_ref.at[:, pl.ds(pl.multiple_of(me * rows, rows), rows), :], dst, local_sems.at[i]
            )
        )
        local[-1].start()
    for cp in local:
        cp.wait()
    for cp in copies:
        cp.wait()


def to_lines(arrays, n):
    count = len(arrays)
    shapes = [(x.shape[0], x.shape[1] // n, x.shape[2] * n) for x in arrays]
    return pl.pallas_call(
        functools.partial(_to_lines_kernel, n, count),
        out_shape=[jax.ShapeDtypeStruct(s, x.dtype) for s, x in zip(shapes, arrays)],
        in_specs=[pl.BlockSpec(memory_space=pltpu.VMEM)] * count,
        out_specs=[pl.BlockSpec(memory_space=pltpu.VMEM)] * count,
        scratch_shapes=[
            pltpu.SemaphoreType.DMA((count * n,)),
            pltpu.SemaphoreType.DMA((count * n,)),
            pltpu.SemaphoreType.DMA((count,)),
        ],
        compiler_params=pltpu.CompilerParams(collective_id=1, has_side_effects=True),
    )(*arrays)


def _from_lines_kernel(sizes, x_ref, cpk_ref, last_ref, first_ref, o_ref, cols_ref, before_ref,
                       after_ref, send_sems, recv_sems, local_sems):
    n_ax, n = sizes
    me = lax.axis_index("sec")
    ax = lax.axis_index("ax")
    rows, width = x_ref.shape[1], o_ref.shape[2]
    up_ax, down_ax = (ax + 1) % n_ax, (ax + n_ax - 1) % n_ax
    peers = [(ax, (me + d) % n) for d in range(1, n)]
    peers += [(up_ax, s) for s in range(n)] + [(down_ax, s) for s in range(n)]
    barrier = pltpu.get_barrier_semaphore()
    for peer in peers:
        pl.semaphore_signal(barrier, inc=1, device_id=peer, device_id_type=MESH)
    pl.semaphore_wait(barrier, len(peers))
    dst = o_ref.at[:, pl.ds(pl.multiple_of(me * rows, rows), rows), :]
    sends, recvs = [], []
    for d in range(1, n):
        peer = (me + d) % n
        for k, (src, out) in enumerate(
            (
                (x_ref.at[:, :, pl.ds(pl.multiple_of(peer * width, width), width)], dst),
                (cpk_ref.at[peer], cols_ref.at[me]),
            )
        ):
            cp = pltpu.make_async_remote_copy(
                src_ref=src,
                dst_ref=out,
                send_sem=send_sems.at[k * n + d],
                recv_sem=recv_sems.at[k * n + d],
                device_id=(ax, peer),
                device_id_type=MESH,
            )
            cp.start()
            sends.append(cp)
        origin = (me + n - d) % n
        for k, (src, out) in enumerate(
            (
                (x_ref.at[:, :, pl.ds(0, width)], o_ref.at[:, pl.ds(pl.multiple_of(origin * rows, rows), rows), :]),
                (cpk_ref.at[0], cols_ref.at[origin]),
            )
        ):
            recvs.append(
                pltpu.make_async_remote_copy(
                    src_ref=src,
                    dst_ref=out,
                    send_sem=send_sems.at[k * n + d],
                    recv_sem=recv_sems.at[k * n + d],
                    device_id=(ax, origin),
                    device_id_type=MESH,
                )
            )
    for s in range(n):
        for k, (src, out, target) in enumerate(
            ((last_ref.at[s], before_ref.at[me], up_ax), (first_ref.at[s], after_ref.at[me], down_ax))
        ):
            base = (2 + k) * n
            cp = pltpu.make_async_remote_copy(
                src_ref=src,
                dst_ref=out,
                send_sem=send_sems.at[base + s],
                recv_sem=recv_sems.at[base + me],
                device_id=(target, s),
                device_id_type=MESH,
            )
            cp.start()
            sends.append(cp)
            recvs.append(
                pltpu.make_async_remote_copy(
                    src_ref=src,
                    dst_ref=(before_ref, after_ref)[k].at[s],
                    send_sem=send_sems.at[base + s],
                    recv_sem=recv_sems.at[base + s],
                    device_id=(target, s),
                    device_id_type=MESH,
                )
            )
    local = [
        pltpu.make_async_copy(
            x_ref.at[:, :, pl.ds(pl.multiple_of(me * width, width), width)], dst, local_sems.at[0]
        ),
        pltpu.make_async_copy(cpk_ref.at[me], cols_ref.at[me], local_sems.at[1]),
    ]
    for cp in local:
        cp.start()
    for cp in local:
        cp.wait()
    for cp in recvs:
        cp.wait_recv()
    for cp in sends:
        cp.wait_send()


def from_lines_with_halo(x, cpk, last, first, n):
    comps, rows, around = x.shape
    n_ax = lax.axis_size("ax")
    shapes = [
        (comps, rows * n, around // n),
        cpk.shape,
        (n,) + last.shape[1:],
        (n,) + first.shape[1:],
    ]
    return pl.pallas_call(
        functools.partial(_from_lines_kernel, (n_ax, n)),
        out_shape=[jax.ShapeDtypeStruct(s, x.dtype) for s in shapes],
        in_specs=[pl.BlockSpec(memory_space=pltpu.VMEM)] * 4,
        out_specs=[pl.BlockSpec(memory_space=pltpu.VMEM)] * 4,
        scratch_shapes=[
            pltpu.SemaphoreType.DMA((4 * n,)),
            pltpu.SemaphoreType.DMA((4 * n,)),
            pltpu.SemaphoreType.DMA((2,)),
        ],
        compiler_params=pltpu.CompilerParams(collective_id=2, has_side_effects=True),
    )(x, cpk, last, first)


def dft_table(length):
    half = length // 2
    root = int(round(math.sqrt(length)))
    cols = jnp.concatenate([jnp.arange(half + 1), jnp.arange(1, half)])
    phase = jnp.where(jnp.arange(length) > half, 0.5 * math.pi, 0.0).astype(jnp.float32)
    step = 2.0 * math.pi / length
    coarse = step * ((root * jnp.arange(length // root)[:, None] * cols[None, :]) % length).astype(jnp.float32)
    fine = step * ((jnp.arange(root)[:, None] * cols[None, :]) % length).astype(jnp.float32) - phase
    table = jnp.cos(coarse)[:, None] * jnp.cos(fine)[None] - jnp.sin(coarse)[:, None] * jnp.sin(fine)[None]
    return table.reshape(length, length)


def paired_inverse(precond):
    length = precond.shape[2]
    half = length // 2
    low = precond[:, :, : half + 1]
    mirror = jnp.flip(precond[:, :, half + 1 :], axis=2)
    inner = jnp.concatenate([jnp.zeros_like(low[:, :, :1]), mirror, jnp.zeros_like(low[:, :, :1])], axis=2)
    paired = low + inner
    return jnp.concatenate([paired, paired[:, :, 1:half]], axis=2)


def with_halo(x, sides, width, wrap):
    for axis, dim in sides:
        size, length = (lax.axis_size(axis), x.shape[dim])
        up = [(i, (i + 1) % size) for i in range(size if wrap else size - 1)]
        down = [(j, i) for i, j in up]
        last = lax.slice_in_dim(x, length - width, length, axis=dim)
        first = lax.slice_in_dim(x, 0, width, axis=dim)
        before = lax.ppermute(last, axis, up)
        after = lax.ppermute(first, axis, down)
        x = jnp.concatenate([before, x, after], axis=dim)
    return x


def swap_channels(field):
    extent = field.shape
    folded = field.reshape((extent[0] // 2, 2) + extent[1:])
    return jnp.flip(folded, axis=1).reshape(extent)


def swap_radial(field):
    extent = field.shape
    folded = field.reshape(extent[0], extent[1] // 2, 2, extent[2])
    return jnp.flip(folded, axis=2).reshape(extent)


def apply_operator(field, stiffness):
    axial_pad = with_halo(field, (("ax", 0),), 1, False)
    sector_pad = with_halo(field, (("sec", 2),), 1, True)
    beside = axial_pad[2:] + axial_pad[:-2]
    beside = beside + sector_pad[:, :, 2:] + sector_pad[:, :, :-2]
    return (stiffness + 4.5) * field - beside - 0.5 * swap_radial(field)


def shards(load, disp, stiff, hole, section_class, class_table, precond):
    slab_count, comp_count, sector_width = disp.shape
    sector_count = lax.axis_size("sec")
    around_cells = sector_width * sector_count
    total_axial = slab_count * lax.axis_size("ax")
    position = lax.axis_index("ax") * slab_count + jnp.arange(slab_count)
    taper = 1.0 + 2.0 * position.astype(jnp.float32) / (total_axial - 1)
    one_hot = (section_class[:, None] == jnp.arange(class_table.shape[0])[None, :]).astype(
        jnp.float32
    )
    factors = jnp.dot(one_hot, class_table, precision=lax.Precision.HIGHEST)
    stiffness = stiff * (factors * taper[:, None])[:, :, None]
    solid = (1 - hole).astype(jnp.float32)[:, None, :]
    residual = solid * (load - apply_operator(disp, stiffness))
    residual_t = jnp.transpose(residual, (1, 0, 2))
    solid_t = jnp.transpose(solid, (1, 0, 2))
    lines, solid_lines = to_lines([residual_t, solid_t], sector_count)
    spectrum = jnp.dot(
        lines.reshape(-1, around_cells), dft_table(around_cells), precision=lax.Precision.HIGH
    ).reshape(lines.shape)
    mixed = jnp.sum(paired_inverse(precond)[:, :, None] * spectrum[None], axis=1)
    smoothed_lines = lax.dot_general(
        mixed.reshape(-1, around_cells),
        dft_table(around_cells),
        (((1,), (1,)), ((), ())),
        precision=lax.Precision.HIGH,
    ) / around_cells
    prec_lines = solid_lines * smoothed_lines.reshape(lines.shape)
    group_rows = lines.shape[1]
    subl = -(-comp_count // 8) * 8
    edge_at = [(p * sector_width - 1) % around_cells for p in range(sector_count)]
    edge_at += [((p + 1) * sector_width) % around_cells for p in range(sector_count)]
    pick = (jnp.arange(around_cells)[None, :] == jnp.array(edge_at)[:, None]).astype(jnp.float32)
    edges = lax.dot_general(
        pick,
        prec_lines.reshape(-1, around_cells),
        (((1,), (1,)), ((), ())),
        precision=lax.Precision.HIGHEST,
    ).reshape(2, sector_count, comp_count, group_rows)
    cpk = jnp.transpose(edges, (1, 2, 0, 3)).reshape(sector_count, comp_count, 2 * group_rows)

    def row_pack(row):
        return jnp.transpose(row.reshape(comp_count, sector_count, sector_width), (1, 0, 2))

    prec_t, halo_cols, before_rows, after_rows = from_lines_with_halo(
        prec_lines, cpk, row_pack(prec_lines[:, -1]), row_pack(prec_lines[:, 0]), sector_count
    )
    ax = lax.axis_index("ax")
    before_row = jnp.where(ax == 0, 0.0, before_rows[sector_count - 1, :comp_count])
    after_row = jnp.where(ax == lax.axis_size("ax") - 1, 0.0, after_rows[0, :comp_count])
    got_cols = jnp.transpose(halo_cols[:, :comp_count, : 2 * group_rows], (1, 0, 2))
    got_cols = got_cols.reshape(comp_count, sector_count, 2, group_rows)
    before_col = got_cols[:, :, 0].reshape(comp_count, slab_count)
    after_col = got_cols[:, :, 1].reshape(comp_count, slab_count)
    stiffness_t = jnp.transpose(stiffness, (1, 0, 2))
    halo_rows = jnp.pad(jnp.stack([before_row, after_row]), ((0, 0), (0, subl - comp_count), (0, 0)))
    halo_cols = jnp.stack([before_col, after_col])[..., None]
    cell_total = slab_count * lax.axis_size("ax") * comp_count * around_cells
    finished, image_t = image_and_totals(
        residual_t, prec_t, stiffness_t, solid_t[0], halo_rows, halo_cols, cell_total, 0
    )
    disp_new_t, residual_new_t = apply_step(
        finished, jnp.transpose(disp, (1, 0, 2)), prec_t, residual_t, image_t
    )
    return (
        jnp.transpose(disp_new_t, (1, 0, 2)),
        jnp.transpose(residual_new_t, (1, 0, 2)),
        finished[0, 1:4],
    )


def solution(mesh):
    in_specs = (
        P("ax", None, "sec"),
        P("ax", None, "sec"),
        P("ax", None, "sec"),
        P("ax", "sec"),
        P("ax"),
        P(),
        P(),
    )
    out_specs = (P("ax", None, "sec"), P("ax", None, "sec"), P())
    return jax.shard_map(shards, mesh=mesh, in_specs=in_specs, out_specs=out_specs, check_vma=False)
```

```python
import functools
import math

import jax
import jax.numpy as jnp
from jax import lax
from jax.experimental import pallas as pl
from jax.experimental.pallas import tpu as pltpu
from jax.sharding import PartitionSpec as P


MESH = pl.DeviceIdType.MESH


def _groups():
    me_ax = lax.axis_index("ax")
    me_sec = lax.axis_index("sec")
    x = me_ax % 4
    z = (me_ax // 4) % 8
    ylo = me_ax // 32
    core = me_sec % 2
    yhi = me_sec // 2

    def plane_peer(c):
        y = c % 4
        return ((y % 2) * 32 + z * 4 + (c // 4) % 4, (y // 2) * 2 + c // 16)

    return [
        (32, (core * 4 + x) * 4 + yhi * 2 + ylo, plane_peer),
        (8, z, lambda c: (me_ax - z * 4 + c * 4, me_sec)),
    ]


def _image_and_sums(r_ref, p_ref, s_ref, m_ref, hr_ref, hc_ref, img_ref):
    comps, rows, width = p_ref.shape
    row = lax.broadcasted_iota(jnp.int32, (rows, width), 0)
    lane = lax.broadcasted_iota(jnp.int32, (rows, width), 1)
    solid = m_ref[...]
    acc = [jnp.zeros((1, width), jnp.float32) for _ in range(5)]
    for q in range(comps):
        field = p_ref[q]
        up = jnp.where(row == 0, hr_ref[0, q : q + 1, :], pltpu.roll(field, 1, 0))
        down = jnp.where(row == rows - 1, hr_ref[1, q : q + 1, :], pltpu.roll(field, rows - 1, 0))
        left = jnp.where(lane == 0, hc_ref[0, q], pltpu.roll(field, 1, 1))
        right = jnp.where(lane == width - 1, hc_ref[1, q], pltpu.roll(field, width - 1, 1))
        beside = down + up + right + left
        image = solid * ((s_ref[q] + 4.5) * field - beside - 0.5 * p_ref[q ^ 1])
        img_ref[q] = image
        res = r_ref[q]
        for k, prod in enumerate((res * field, field * image, res * res, res * image, image * image)):
            acc[k] = acc[k] + jnp.sum(prod, axis=0, keepdims=True)
    lane8 = lax.broadcasted_iota(jnp.int32, (8, 128), 1)
    row8 = lax.broadcasted_iota(jnp.int32, (8, 128), 0)
    packed = jnp.zeros((8, 128), jnp.float32)
    for k, a in enumerate(acc):
        packed = jnp.where((row8 == 0) & (lane8 == k), jnp.sum(a), packed)
    return packed


def _finish(total, cell_total):
    lane = lax.broadcasted_iota(jnp.int32, total.shape, 1)
    row = lax.broadcasted_iota(jnp.int32, total.shape, 0)

    def pick(k):
        return jnp.sum(jnp.where((row == 0) & (lane == k), total, 0.0), keepdims=True)

    inner_rz = pick(0) / cell_total
    inner_zq = pick(1) / cell_total
    alpha = inner_rz / inner_zq
    square_new = (pick(2) - alpha * (2.0 * pick(3) - alpha * pick(4))) / cell_total
    out = jnp.zeros(total.shape, jnp.float32)
    for k, v in enumerate((alpha, inner_rz, inner_zq, square_new)):
        out = jnp.where((row == 0) & (lane == k), v, out)
    return out


def _ar_kernel(cell_total, r_ref, p_ref, s_ref, m_ref, hr_ref, hc_ref, o_ref, img_ref, recv_a, recv_b, own, send_sems, recv_sems):
    recvs = (recv_a, recv_b)
    groups = _groups()
    for r in recvs:
        r[...] = jnp.zeros_like(r)
    barrier = pltpu.get_barrier_semaphore()
    count = 0
    for n, mine, dev in groups:
        for d in range(1, n):
            pl.semaphore_signal(barrier, inc=1, device_id=dev((mine + d) % n), device_id_type=MESH)
            count += 1
    own[0] = _image_and_sums(r_ref, p_ref, s_ref, m_ref, hr_ref, hc_ref, img_ref)
    pl.semaphore_wait(barrier, count)
    base = 0
    for g, (n, mine, dev) in enumerate(groups):
        src = own.at[g]
        copies = []
        for d in range(1, n):
            cp = pltpu.make_async_remote_copy(
                src_ref=src,
                dst_ref=recvs[g].at[mine],
                send_sem=send_sems.at[base + d],
                recv_sem=recv_sems.at[base + d],
                device_id=dev((mine + d) % n),
                device_id_type=MESH,
            )
            cp.start()
            copies.append(cp)
        mine_val = src[...]
        for cp in copies:
            cp.wait_recv()
        total = None
        for c in range(n):
            v = jnp.where(mine == c, mine_val, recvs[g][c])
            total = v if total is None else total + v
        for cp in copies:
            cp.wait_send()
        base += n
        if g + 1 < len(groups):
            own[g + 1] = total
        else:
            finished = _finish(total, cell_total)
            o_ref[...] = finished


def image_and_totals(residual, prec, stiffness, solid, halo_rows, halo_cols, cell_total, cid):
    return pl.pallas_call(
        functools.partial(_ar_kernel, float(cell_total)),
        out_shape=[
            jax.ShapeDtypeStruct((8, 128), jnp.float32),
            jax.ShapeDtypeStruct(prec.shape, jnp.float32),
        ],
        in_specs=[pl.BlockSpec(memory_space=pltpu.VMEM)] * 6,
        out_specs=[pl.BlockSpec(memory_space=pltpu.VMEM)] * 2,
        scratch_shapes=[
            pltpu.VMEM((32, 8, 128), jnp.float32),
            pltpu.VMEM((8, 8, 128), jnp.float32),
            pltpu.VMEM((2, 8, 128), jnp.float32),
            pltpu.SemaphoreType.DMA((40,)),
            pltpu.SemaphoreType.DMA((40,)),
        ],
        compiler_params=pltpu.CompilerParams(collective_id=cid, has_side_effects=True),
    )(residual, prec, stiffness, solid, halo_rows, halo_cols)


def _update_kernel(f_ref, d_ref, p_ref, r_ref, i_ref, dn_ref, rn_ref):
    alpha = f_ref[0:1, 0:1]
    for q in range(d_ref.shape[0]):
        dn_ref[q] = d_ref[q] + alpha * p_ref[q]
        rn_ref[q] = r_ref[q] - alpha * i_ref[q]


def apply_step(finished, disp, prec, residual, image):
    comps, rows, width = prec.shape
    steps = 2 if comps % 2 == 0 else 1
    plane = pl.BlockSpec((comps // steps, rows, width), lambda q: (q, 0, 0))
    return pl.pallas_call(
        _update_kernel,
        grid=(steps,),
        out_shape=[jax.ShapeDtypeStruct(prec.shape, jnp.float32)] * 2,
        in_specs=[pl.BlockSpec((8, 128), lambda q: (0, 0))] + [plane] * 4,
        out_specs=[plane] * 2,
    )(finished, disp, prec, residual, image)


def _to_lines_kernel(n, count, *refs):
    x_refs, o_refs = refs[:count], refs[count : 2 * count]
    send_sems, recv_sems, local_sems = refs[2 * count :]
    me = lax.axis_index("sec")
    ax = lax.axis_index("ax")
    barrier = pltpu.get_barrier_semaphore()
    for d in range(1, n):
        pl.semaphore_signal(barrier, inc=1, device_id=(ax, (me + d) % n), device_id_type=MESH)
    pl.semaphore_wait(barrier, n - 1)
    copies, local = [], []
    for i, (x_ref, o_ref) in enumerate(zip(x_refs, o_refs)):
        rows, width = o_ref.shape[1], x_ref.shape[2]
        dst = o_ref.at[:, :, pl.ds(pl.multiple_of(me * width, width), width)]
        for d in range(1, n):
            peer = (me + d) % n
            cp = pltpu.make_async_remote_copy(
                src_ref=x_ref.at[:, pl.ds(pl.multiple_of(peer * rows, rows), rows), :],
                dst_ref=dst,
                send_sem=send_sems.at[i * n + d],
                recv_sem=recv_sems.at[i * n + d],
                device_id=(ax, peer),
                device_id_type=MESH,
            )
            cp.start()
            copies.append(cp)
        local.append(
            pltpu.make_async_copy(
                x_ref.at[:, pl.ds(pl.multiple_of(me * rows, rows), rows), :], dst, local_sems.at[i]
            )
        )
        local[-1].start()
    for cp in local:
        cp.wait()
    for cp in copies:
        cp.wait()


def to_lines(arrays, n):
    count = len(arrays)
    shapes = [(x.shape[0], x.shape[1] // n, x.shape[2] * n) for x in arrays]
    return pl.pallas_call(
        functools.partial(_to_lines_kernel, n, count),
        out_shape=[jax.ShapeDtypeStruct(s, x.dtype) for s, x in zip(shapes, arrays)],
        in_specs=[pl.BlockSpec(memory_space=pltpu.VMEM)] * count,
        out_specs=[pl.BlockSpec(memory_space=pltpu.VMEM)] * count,
        scratch_shapes=[
            pltpu.SemaphoreType.DMA((count * n,)),
            pltpu.SemaphoreType.DMA((count * n,)),
            pltpu.SemaphoreType.DMA((count,)),
        ],
        compiler_params=pltpu.CompilerParams(collective_id=1, has_side_effects=True),
    )(*arrays)


def _from_lines_kernel(sizes, x_ref, cpk_ref, last_ref, first_ref, o_ref, cols_ref, before_ref,
                       after_ref, send_sems, recv_sems, local_sems):
    n_ax, n = sizes
    me = lax.axis_index("sec")
    ax = lax.axis_index("ax")
    rows, width = x_ref.shape[1], o_ref.shape[2]
    up_ax, down_ax = (ax + 1) % n_ax, (ax + n_ax - 1) % n_ax
    peers = [(ax, (me + d) % n) for d in range(1, n)]
    peers += [(up_ax, s) for s in range(n)] + [(down_ax, s) for s in range(n)]
    barrier = pltpu.get_barrier_semaphore()
    for peer in peers:
        pl.semaphore_signal(barrier, inc=1, device_id=peer, device_id_type=MESH)
    pl.semaphore_wait(barrier, len(peers))
    dst = o_ref.at[:, pl.ds(pl.multiple_of(me * rows, rows), rows), :]
    sends, recvs = [], []
    for d in range(1, n):
        peer = (me + d) % n
        for k, (src, out) in enumerate(
            (
                (x_ref.at[:, :, pl.ds(pl.multiple_of(peer * width, width), width)], dst),
                (cpk_ref.at[peer], cols_ref.at[me]),
            )
        ):
            cp = pltpu.make_async_remote_copy(
                src_ref=src,
                dst_ref=out,
                send_sem=send_sems.at[k * n + d],
                recv_sem=recv_sems.at[k * n + d],
                device_id=(ax, peer),
                device_id_type=MESH,
            )
            cp.start()
            sends.append(cp)
        origin = (me + n - d) % n
        for k, (src, out) in enumerate(
            (
                (x_ref.at[:, :, pl.ds(0, width)], o_ref.at[:, pl.ds(pl.multiple_of(origin * rows, rows), rows), :]),
                (cpk_ref.at[0], cols_ref.at[origin]),
            )
        ):
            recvs.append(
                pltpu.make_async_remote_copy(
                    src_ref=src,
                    dst_ref=out,
                    send_sem=send_sems.at[k * n + d],
                    recv_sem=recv_sems.at[k * n + d],
                    device_id=(ax, origin),
                    device_id_type=MESH,
                )
            )
    for s in range(n):
        for k, (src, out, target) in enumerate(
            ((last_ref.at[s], before_ref.at[me], up_ax), (first_ref.at[s], after_ref.at[me], down_ax))
        ):
            base = (2 + k) * n
            cp = pltpu.make_async_remote_copy(
                src_ref=src,
                dst_ref=out,
                send_sem=send_sems.at[base + s],
                recv_sem=recv_sems.at[base + me],
                device_id=(target, s),
                device_id_type=MESH,
            )
            cp.start()
            sends.append(cp)
            recvs.append(
                pltpu.make_async_remote_copy(
                    src_ref=src,
                    dst_ref=(before_ref, after_ref)[k].at[s],
                    send_sem=send_sems.at[base + s],
                    recv_sem=recv_sems.at[base + s],
                    device_id=(target, s),
                    device_id_type=MESH,
                )
            )
    local = [
        pltpu.make_async_copy(
            x_ref.at[:, :, pl.ds(pl.multiple_of(me * width, width), width)], dst, local_sems.at[0]
        ),
        pltpu.make_async_copy(cpk_ref.at[me], cols_ref.at[me], local_sems.at[1]),
    ]
    for cp in local:
        cp.start()
    for cp in local:
        cp.wait()
    for cp in recvs:
        cp.wait_recv()
    for cp in sends:
        cp.wait_send()


def from_lines_with_halo(x, cpk, last, first, n):
    comps, rows, around = x.shape
    n_ax = lax.axis_size("ax")
    shapes = [
        (comps, rows * n, around // n),
        cpk.shape,
        (n,) + last.shape[1:],
        (n,) + first.shape[1:],
    ]
    return pl.pallas_call(
        functools.partial(_from_lines_kernel, (n_ax, n)),
        out_shape=[jax.ShapeDtypeStruct(s, x.dtype) for s in shapes],
        in_specs=[pl.BlockSpec(memory_space=pltpu.VMEM)] * 4,
        out_specs=[pl.BlockSpec(memory_space=pltpu.VMEM)] * 4,
        scratch_shapes=[
            pltpu.SemaphoreType.DMA((4 * n,)),
            pltpu.SemaphoreType.DMA((4 * n,)),
            pltpu.SemaphoreType.DMA((2,)),
        ],
        compiler_params=pltpu.CompilerParams(collective_id=2, has_side_effects=True),
    )(x, cpk, last, first)


def dft_table(length):
    half = length // 2
    root = int(round(math.sqrt(length)))
    cols = jnp.concatenate([jnp.arange(half + 1), jnp.arange(1, half)])
    phase = jnp.where(jnp.arange(length) > half, 0.5 * math.pi, 0.0).astype(jnp.float32)
    step = 2.0 * math.pi / length
    coarse = step * ((root * jnp.arange(length // root)[:, None] * cols[None, :]) % length).astype(jnp.float32)
    fine = step * ((jnp.arange(root)[:, None] * cols[None, :]) % length).astype(jnp.float32) - phase
    table = jnp.cos(coarse)[:, None] * jnp.cos(fine)[None] - jnp.sin(coarse)[:, None] * jnp.sin(fine)[None]
    return table.reshape(length, length)


def paired_inverse(precond):
    length = precond.shape[2]
    half = length // 2
    col = lax.broadcasted_iota(jnp.int32, precond.shape, 2)
    mirror = jnp.flip(jnp.roll(precond, -1, axis=2), axis=2)
    low = jnp.where(col <= half, precond, jnp.roll(precond, half, axis=2))
    inner = (col >= 1) & (col < half)
    high = jnp.where(col <= half, jnp.where(inner, mirror, 0.0), jnp.roll(mirror, half, axis=2))
    return low + high


def with_halo(x, sides, width, wrap):
    for axis, dim in sides:
        size, length = (lax.axis_size(axis), x.shape[dim])
        up = [(i, (i + 1) % size) for i in range(size if wrap else size - 1)]
        down = [(j, i) for i, j in up]
        last = lax.slice_in_dim(x, length - width, length, axis=dim)
        first = lax.slice_in_dim(x, 0, width, axis=dim)
        before = lax.ppermute(last, axis, up)
        after = lax.ppermute(first, axis, down)
        x = jnp.concatenate([before, x, after], axis=dim)
    return x


def swap_channels(field):
    extent = field.shape
    folded = field.reshape((extent[0] // 2, 2) + extent[1:])
    return jnp.flip(folded, axis=1).reshape(extent)


def swap_radial(field):
    extent = field.shape
    folded = field.reshape(extent[0], extent[1] // 2, 2, extent[2])
    return jnp.flip(folded, axis=2).reshape(extent)


def apply_operator(field, stiffness):
    axial_pad = with_halo(field, (("ax", 0),), 1, False)
    sector_pad = with_halo(field, (("sec", 2),), 1, True)
    beside = axial_pad[2:] + axial_pad[:-2]
    beside = beside + sector_pad[:, :, 2:] + sector_pad[:, :, :-2]
    return (stiffness + 4.5) * field - beside - 0.5 * swap_radial(field)


def shards(load, disp, stiff, hole, section_class, class_table, precond):
    slab_count, comp_count, sector_width = disp.shape
    sector_count = lax.axis_size("sec")
    around_cells = sector_width * sector_count
    total_axial = slab_count * lax.axis_size("ax")
    position = lax.axis_index("ax") * slab_count + jnp.arange(slab_count)
    taper = 1.0 + 2.0 * position.astype(jnp.float32) / (total_axial - 1)
    one_hot = (section_class[:, None] == jnp.arange(class_table.shape[0])[None, :]).astype(
        jnp.float32
    )
    factors = jnp.dot(one_hot, class_table, precision=lax.Precision.HIGHEST)
    stiffness = stiff * (factors * taper[:, None])[:, :, None]
    solid = (1 - hole).astype(jnp.float32)[:, None, :]
    residual = solid * (load - apply_operator(disp, stiffness))
    residual_t = jnp.transpose(residual, (1, 0, 2))
    solid_t = jnp.transpose(solid, (1, 0, 2))
    lines, solid_lines = to_lines([residual_t, solid_t], sector_count)
    spectrum = jnp.dot(
        lines.reshape(-1, around_cells), dft_table(around_cells), precision=lax.Precision.HIGH
    ).reshape(lines.shape)
    mixed = jnp.sum(paired_inverse(precond)[:, :, None] * spectrum[None], axis=1)
    smoothed_lines = lax.dot_general(
        mixed.reshape(-1, around_cells),
        dft_table(around_cells),
        (((1,), (1,)), ((), ())),
        precision=lax.Precision.HIGH,
    ) / around_cells
    prec_lines = solid_lines * smoothed_lines.reshape(lines.shape)
    group_rows = lines.shape[1]
    subl = -(-comp_count // 8) * 8
    edge_at = [(p * sector_width - 1) % around_cells for p in range(sector_count)]
    edge_at += [((p + 1) * sector_width) % around_cells for p in range(sector_count)]
    pick = (jnp.arange(around_cells)[None, :] == jnp.array(edge_at)[:, None]).astype(jnp.float32)
    edges = lax.dot_general(
        pick,
        prec_lines.reshape(-1, around_cells),
        (((1,), (1,)), ((), ())),
        precision=lax.Precision.HIGHEST,
    ).reshape(2, sector_count, comp_count, group_rows)
    cpk = jnp.transpose(edges, (1, 2, 0, 3)).reshape(sector_count, comp_count, 2 * group_rows)

    def row_pack(row):
        return jnp.transpose(row.reshape(comp_count, sector_count, sector_width), (1, 0, 2))

    prec_t, halo_cols, before_rows, after_rows = from_lines_with_halo(
        prec_lines, cpk, row_pack(prec_lines[:, -1]), row_pack(prec_lines[:, 0]), sector_count
    )
    ax = lax.axis_index("ax")
    before_row = jnp.where(ax == 0, 0.0, before_rows[sector_count - 1, :comp_count])
    after_row = jnp.where(ax == lax.axis_size("ax") - 1, 0.0, after_rows[0, :comp_count])
    got_cols = jnp.transpose(halo_cols[:, :comp_count, : 2 * group_rows], (1, 0, 2))
    got_cols = got_cols.reshape(comp_count, sector_count, 2, group_rows)
    before_col = got_cols[:, :, 0].reshape(comp_count, slab_count)
    after_col = got_cols[:, :, 1].reshape(comp_count, slab_count)
    stiffness_t = jnp.transpose(stiffness, (1, 0, 2))
    halo_rows = jnp.pad(jnp.stack([before_row, after_row]), ((0, 0), (0, subl - comp_count), (0, 0)))
    halo_cols = jnp.stack([before_col, after_col])[..., None]
    cell_total = slab_count * lax.axis_size("ax") * comp_count * around_cells
    finished, image_t = image_and_totals(
        residual_t, prec_t, stiffness_t, solid_t[0], halo_rows, halo_cols, cell_total, 0
    )
    disp_new_t, residual_new_t = apply_step(
        finished, jnp.transpose(disp, (1, 0, 2)), prec_t, residual_t, image_t
    )
    return (
        jnp.transpose(disp_new_t, (1, 0, 2)),
        jnp.transpose(residual_new_t, (1, 0, 2)),
        finished[0, 1:4],
    )


def solution(mesh):
    in_specs = (
        P("ax", None, "sec"),
        P("ax", None, "sec"),
        P("ax", None, "sec"),
        P("ax", "sec"),
        P("ax"),
        P(),
        P(),
    )
    out_specs = (P("ax", None, "sec"), P("ax", None, "sec"), P())
    return jax.shard_map(shards, mesh=mesh, in_specs=in_specs, out_specs=out_specs, check_vma=False)
```

```python
import functools
import math

import jax
import jax.numpy as jnp
from jax import lax
from jax.experimental import pallas as pl
from jax.experimental.pallas import tpu as pltpu
from jax.sharding import PartitionSpec as P


MESH = pl.DeviceIdType.MESH


def _groups():
    me_ax = lax.axis_index("ax")
    me_sec = lax.axis_index("sec")
    x = me_ax % 4
    z = (me_ax // 4) % 8
    ylo = me_ax // 32
    core = me_sec % 2
    yhi = me_sec // 2

    def plane_peer(c):
        y = c % 4
        return ((y % 2) * 32 + z * 4 + (c // 4) % 4, (y // 2) * 2 + c // 16)

    return [
        (32, (core * 4 + x) * 4 + yhi * 2 + ylo, plane_peer),
        (8, z, lambda c: (me_ax - z * 4 + c * 4, me_sec)),
    ]


def _image_and_sums(r_ref, p_ref, s_ref, m_ref, hr_ref, hc_ref, img_ref):
    comps, rows, width = p_ref.shape
    row = lax.broadcasted_iota(jnp.int32, (rows, width), 0)
    lane = lax.broadcasted_iota(jnp.int32, (rows, width), 1)
    solid = m_ref[...]
    acc = [jnp.zeros((1, width), jnp.float32) for _ in range(5)]
    for q in range(comps):
        field = p_ref[q]
        up = jnp.where(row == 0, hr_ref[0, q : q + 1, :], pltpu.roll(field, 1, 0))
        down = jnp.where(row == rows - 1, hr_ref[1, q : q + 1, :], pltpu.roll(field, rows - 1, 0))
        left = jnp.where(lane == 0, hc_ref[0, q], pltpu.roll(field, 1, 1))
        right = jnp.where(lane == width - 1, hc_ref[1, q], pltpu.roll(field, width - 1, 1))
        beside = down + up + right + left
        image = solid * ((s_ref[q] + 4.5) * field - beside - 0.5 * p_ref[q ^ 1])
        img_ref[q] = image
        res = r_ref[q]
        for k, prod in enumerate((res * field, field * image, res * res, res * image, image * image)):
            acc[k] = acc[k] + jnp.sum(prod, axis=0, keepdims=True)
    lane8 = lax.broadcasted_iota(jnp.int32, (8, 128), 1)
    row8 = lax.broadcasted_iota(jnp.int32, (8, 128), 0)
    packed = jnp.zeros((8, 128), jnp.float32)
    for k, a in enumerate(acc):
        packed = jnp.where((row8 == 0) & (lane8 == k), jnp.sum(a), packed)
    return packed


def _finish(total, cell_total):
    lane = lax.broadcasted_iota(jnp.int32, total.shape, 1)
    row = lax.broadcasted_iota(jnp.int32, total.shape, 0)

    def pick(k):
        return jnp.sum(jnp.where((row == 0) & (lane == k), total, 0.0), keepdims=True)

    inner_rz = pick(0) / cell_total
    inner_zq = pick(1) / cell_total
    alpha = inner_rz / inner_zq
    square_new = (pick(2) - alpha * (2.0 * pick(3) - alpha * pick(4))) / cell_total
    out = jnp.zeros(total.shape, jnp.float32)
    for k, v in enumerate((alpha, inner_rz, inner_zq, square_new)):
        out = jnp.where((row == 0) & (lane == k), v, out)
    return out


def _ar_kernel(cell_total, r_ref, p_ref, s_ref, m_ref, hr_ref, hc_ref, o_ref, img_ref, recv_a, recv_b, own, send_sems, recv_sems):
    recvs = (recv_a, recv_b)
    groups = _groups()
    for r in recvs:
        r[...] = jnp.zeros_like(r)
    barrier = pltpu.get_barrier_semaphore()
    count = 0
    for n, mine, dev in groups:
        for d in range(1, n):
            pl.semaphore_signal(barrier, inc=1, device_id=dev((mine + d) % n), device_id_type=MESH)
            count += 1
    own[0] = _image_and_sums(r_ref, p_ref, s_ref, m_ref, hr_ref, hc_ref, img_ref)
    pl.semaphore_wait(barrier, count)
    base = 0
    for g, (n, mine, dev) in enumerate(groups):
        src = own.at[g]
        copies = []
        for d in range(1, n):
            cp = pltpu.make_async_remote_copy(
                src_ref=src,
                dst_ref=recvs[g].at[mine],
                send_sem=send_sems.at[base + d],
                recv_sem=recv_sems.at[base + d],
                device_id=dev((mine + d) % n),
                device_id_type=MESH,
            )
            cp.start()
            copies.append(cp)
        mine_val = src[...]
        for cp in copies:
            cp.wait_recv()
        total = None
        for c in range(n):
            v = jnp.where(mine == c, mine_val, recvs[g][c])
            total = v if total is None else total + v
        for cp in copies:
            cp.wait_send()
        base += n
        if g + 1 < len(groups):
            own[g + 1] = total
        else:
            finished = _finish(total, cell_total)
            o_ref[...] = finished


def image_and_totals(residual, prec, stiffness, solid, halo_rows, halo_cols, cell_total, cid):
    return pl.pallas_call(
        functools.partial(_ar_kernel, float(cell_total)),
        out_shape=[
            jax.ShapeDtypeStruct((8, 128), jnp.float32),
            jax.ShapeDtypeStruct(prec.shape, jnp.float32),
        ],
        in_specs=[pl.BlockSpec(memory_space=pltpu.VMEM)] * 6,
        out_specs=[pl.BlockSpec(memory_space=pltpu.VMEM)] * 2,
        scratch_shapes=[
            pltpu.VMEM((32, 8, 128), jnp.float32),
            pltpu.VMEM((8, 8, 128), jnp.float32),
            pltpu.VMEM((2, 8, 128), jnp.float32),
            pltpu.SemaphoreType.DMA((40,)),
            pltpu.SemaphoreType.DMA((40,)),
        ],
        compiler_params=pltpu.CompilerParams(collective_id=cid, has_side_effects=True),
    )(residual, prec, stiffness, solid, halo_rows, halo_cols)


def _update_kernel(f_ref, d_ref, p_ref, r_ref, i_ref, dn_ref, rn_ref):
    alpha = f_ref[0:1, 0:1]
    for q in range(d_ref.shape[0]):
        dn_ref[q] = d_ref[q] + alpha * p_ref[q]
        rn_ref[q] = r_ref[q] - alpha * i_ref[q]


def apply_step(finished, disp, prec, residual, image):
    comps, rows, width = prec.shape
    steps = 2 if comps % 2 == 0 else 1
    plane = pl.BlockSpec((comps // steps, rows, width), lambda q: (q, 0, 0))
    return pl.pallas_call(
        _update_kernel,
        grid=(steps,),
        out_shape=[jax.ShapeDtypeStruct(prec.shape, jnp.float32)] * 2,
        in_specs=[pl.BlockSpec((8, 128), lambda q: (0, 0))] + [plane] * 4,
        out_specs=[plane] * 2,
    )(finished, disp, prec, residual, image)


def _to_lines_kernel(n, count, *refs):
    x_refs, o_refs = refs[:count], refs[count : 2 * count]
    send_sems, recv_sems, local_sems = refs[2 * count :]
    me = lax.axis_index("sec")
    ax = lax.axis_index("ax")
    barrier = pltpu.get_barrier_semaphore()
    for d in range(1, n):
        pl.semaphore_signal(barrier, inc=1, device_id=(ax, (me + d) % n), device_id_type=MESH)
    pl.semaphore_wait(barrier, n - 1)
    copies, local = [], []
    for i, (x_ref, o_ref) in enumerate(zip(x_refs, o_refs)):
        rows, width = o_ref.shape[1], x_ref.shape[2]
        dst = o_ref.at[:, :, pl.ds(pl.multiple_of(me * width, width), width)]
        for d in range(1, n):
            peer = (me + d) % n
            cp = pltpu.make_async_remote_copy(
                src_ref=x_ref.at[:, pl.ds(pl.multiple_of(peer * rows, rows), rows), :],
                dst_ref=dst,
                send_sem=send_sems.at[i * n + d],
                recv_sem=recv_sems.at[i * n + d],
                device_id=(ax, peer),
                device_id_type=MESH,
            )
            cp.start()
            copies.append(cp)
        local.append(
            pltpu.make_async_copy(
                x_ref.at[:, pl.ds(pl.multiple_of(me * rows, rows), rows), :], dst, local_sems.at[i]
            )
        )
        local[-1].start()
    for cp in local:
        cp.wait()
    for cp in copies:
        cp.wait()


def to_lines(arrays, n):
    count = len(arrays)
    shapes = [(x.shape[0], x.shape[1] // n, x.shape[2] * n) for x in arrays]
    return pl.pallas_call(
        functools.partial(_to_lines_kernel, n, count),
        out_shape=[jax.ShapeDtypeStruct(s, x.dtype) for s, x in zip(shapes, arrays)],
        in_specs=[pl.BlockSpec(memory_space=pltpu.VMEM)] * count,
        out_specs=[pl.BlockSpec(memory_space=pltpu.VMEM)] * count,
        scratch_shapes=[
            pltpu.SemaphoreType.DMA((count * n,)),
            pltpu.SemaphoreType.DMA((count * n,)),
            pltpu.SemaphoreType.DMA((count,)),
        ],
        compiler_params=pltpu.CompilerParams(collective_id=1, has_side_effects=True),
    )(*arrays)


def _from_lines_kernel(sizes, x_ref, cpk_ref, last_ref, first_ref, o_ref, cols_ref, before_ref,
                       after_ref, send_sems, recv_sems, local_sems):
    n_ax, n = sizes
    me = lax.axis_index("sec")
    ax = lax.axis_index("ax")
    rows, width = x_ref.shape[1], o_ref.shape[2]
    up_ax, down_ax = (ax + 1) % n_ax, (ax + n_ax - 1) % n_ax
    peers = [(ax, (me + d) % n) for d in range(1, n)]
    peers += [(up_ax, s) for s in range(n)] + [(down_ax, s) for s in range(n)]
    barrier = pltpu.get_barrier_semaphore()
    for peer in peers:
        pl.semaphore_signal(barrier, inc=1, device_id=peer, device_id_type=MESH)
    pl.semaphore_wait(barrier, len(peers))
    dst = o_ref.at[:, pl.ds(pl.multiple_of(me * rows, rows), rows), :]
    sends, recvs = [], []
    for d in range(1, n):
        peer = (me + d) % n
        for k, (src, out) in enumerate(
            (
                (x_ref.at[:, :, pl.ds(pl.multiple_of(peer * width, width), width)], dst),
                (cpk_ref.at[peer], cols_ref.at[me]),
            )
        ):
            cp = pltpu.make_async_remote_copy(
                src_ref=src,
                dst_ref=out,
                send_sem=send_sems.at[k * n + d],
                recv_sem=recv_sems.at[k * n + d],
                device_id=(ax, peer),
                device_id_type=MESH,
            )
            cp.start()
            sends.append(cp)
        origin = (me + n - d) % n
        for k, (src, out) in enumerate(
            (
                (x_ref.at[:, :, pl.ds(0, width)], o_ref.at[:, pl.ds(pl.multiple_of(origin * rows, rows), rows), :]),
                (cpk_ref.at[0], cols_ref.at[origin]),
            )
        ):
            recvs.append(
                pltpu.make_async_remote_copy(
                    src_ref=src,
                    dst_ref=out,
                    send_sem=send_sems.at[k * n + d],
                    recv_sem=recv_sems.at[k * n + d],
                    device_id=(ax, origin),
                    device_id_type=MESH,
                )
            )
    for s in range(n):
        for k, (src, out, target) in enumerate(
            ((last_ref.at[s], before_ref.at[me], up_ax), (first_ref.at[s], after_ref.at[me], down_ax))
        ):
            base = (2 + k) * n
            cp = pltpu.make_async_remote_copy(
                src_ref=src,
                dst_ref=out,
                send_sem=send_sems.at[base + s],
                recv_sem=recv_sems.at[base + me],
                device_id=(target, s),
                device_id_type=MESH,
            )
            cp.start()
            sends.append(cp)
            recvs.append(
                pltpu.make_async_remote_copy(
                    src_ref=src,
                    dst_ref=(before_ref, after_ref)[k].at[s],
                    send_sem=send_sems.at[base + s],
                    recv_sem=recv_sems.at[base + s],
                    device_id=(target, s),
                    device_id_type=MESH,
                )
            )
    local = [
        pltpu.make_async_copy(
            x_ref.at[:, :, pl.ds(pl.multiple_of(me * width, width), width)], dst, local_sems.at[0]
        ),
        pltpu.make_async_copy(cpk_ref.at[me], cols_ref.at[me], local_sems.at[1]),
    ]
    for cp in local:
        cp.start()
    for cp in local:
        cp.wait()
    for cp in recvs:
        cp.wait_recv()
    for cp in sends:
        cp.wait_send()


def from_lines_with_halo(x, cpk, last, first, n):
    comps, rows, around = x.shape
    n_ax = lax.axis_size("ax")
    shapes = [
        (comps, rows * n, around // n),
        cpk.shape,
        (n,) + last.shape[1:],
        (n,) + first.shape[1:],
    ]
    return pl.pallas_call(
        functools.partial(_from_lines_kernel, (n_ax, n)),
        out_shape=[jax.ShapeDtypeStruct(s, x.dtype) for s in shapes],
        in_specs=[pl.BlockSpec(memory_space=pltpu.VMEM)] * 4,
        out_specs=[pl.BlockSpec(memory_space=pltpu.VMEM)] * 4,
        scratch_shapes=[
            pltpu.SemaphoreType.DMA((4 * n,)),
            pltpu.SemaphoreType.DMA((4 * n,)),
            pltpu.SemaphoreType.DMA((2,)),
        ],
        compiler_params=pltpu.CompilerParams(collective_id=2, has_side_effects=True),
    )(x, cpk, last, first)


def dft_table(length):
    half = length // 2
    root = int(round(math.sqrt(length)))
    cols = jnp.concatenate([jnp.arange(half + 1), jnp.arange(1, half)])
    phase = jnp.where(jnp.arange(length) > half, 0.5 * math.pi, 0.0).astype(jnp.float32)
    step = 2.0 * math.pi / length
    coarse = step * ((root * jnp.arange(length // root)[:, None] * cols[None, :]) % length).astype(jnp.float32)
    fine = step * ((jnp.arange(root)[:, None] * cols[None, :]) % length).astype(jnp.float32) - phase
    table = jnp.cos(coarse)[:, None] * jnp.cos(fine)[None] - jnp.sin(coarse)[:, None] * jnp.sin(fine)[None]
    return table.reshape(length, length)


def paired_inverse(precond):
    length = precond.shape[2]
    half = length // 2
    low = precond[:, :, : half + 1]
    mirror = jnp.flip(precond[:, :, half + 1 :], axis=2)
    inner = jnp.concatenate([jnp.zeros_like(low[:, :, :1]), mirror, jnp.zeros_like(low[:, :, :1])], axis=2)
    paired = low + inner
    return jnp.concatenate([paired, paired[:, :, 1:half]], axis=2)


def with_halo(x, sides, width, wrap):
    for axis, dim in sides:
        size, length = (lax.axis_size(axis), x.shape[dim])
        up = [(i, (i + 1) % size) for i in range(size if wrap else size - 1)]
        down = [(j, i) for i, j in up]
        last = lax.slice_in_dim(x, length - width, length, axis=dim)
        first = lax.slice_in_dim(x, 0, width, axis=dim)
        before = lax.ppermute(last, axis, up)
        after = lax.ppermute(first, axis, down)
        x = jnp.concatenate([before, x, after], axis=dim)
    return x


def swap_channels(field):
    extent = field.shape
    folded = field.reshape((extent[0] // 2, 2) + extent[1:])
    return jnp.flip(folded, axis=1).reshape(extent)


def swap_radial(field):
    extent = field.shape
    folded = field.reshape(extent[0], extent[1] // 2, 2, extent[2])
    return jnp.flip(folded, axis=2).reshape(extent)


def apply_operator(field, stiffness):
    axial_pad = with_halo(field, (("ax", 0),), 1, False)
    sector_pad = with_halo(field, (("sec", 2),), 1, True)
    beside = axial_pad[2:] + axial_pad[:-2]
    beside = beside + sector_pad[:, :, 2:] + sector_pad[:, :, :-2]
    return (stiffness + 4.5) * field - beside - 0.5 * swap_radial(field)


def shards(load, disp, stiff, hole, section_class, class_table, precond):
    slab_count, comp_count, sector_width = disp.shape
    sector_count = lax.axis_size("sec")
    around_cells = sector_width * sector_count
    total_axial = slab_count * lax.axis_size("ax")
    position = lax.axis_index("ax") * slab_count + jnp.arange(slab_count)
    taper = 1.0 + 2.0 * position.astype(jnp.float32) / (total_axial - 1)
    one_hot = (section_class[:, None] == jnp.arange(class_table.shape[0])[None, :]).astype(
        jnp.float32
    )
    factors = jnp.dot(one_hot, class_table, precision=lax.Precision.HIGHEST)
    stiffness = stiff * (factors * taper[:, None])[:, :, None]
    solid = (1 - hole).astype(jnp.float32)[:, None, :]
    residual = solid * (load - apply_operator(disp, stiffness))
    residual_t = jnp.transpose(residual, (1, 0, 2))
    solid_t = jnp.transpose(solid, (1, 0, 2))
    lines, solid_lines = to_lines([residual_t, solid_t], sector_count)
    spectrum = lax.optimization_barrier(
        jnp.dot(
            lax.optimization_barrier(lines.reshape(-1, around_cells)),
            dft_table(around_cells),
            precision=lax.Precision.HIGH,
        )
    ).reshape(lines.shape)
    mixed = jnp.sum(paired_inverse(precond)[:, :, None] * spectrum[None], axis=1)
    smoothed_lines = lax.dot_general(
        mixed.reshape(-1, around_cells),
        dft_table(around_cells),
        (((1,), (1,)), ((), ())),
        precision=lax.Precision.HIGH,
    ) / around_cells
    prec_lines = solid_lines * smoothed_lines.reshape(lines.shape)
    group_rows = lines.shape[1]
    subl = -(-comp_count // 8) * 8
    edge_at = [(p * sector_width - 1) % around_cells for p in range(sector_count)]
    edge_at += [((p + 1) * sector_width) % around_cells for p in range(sector_count)]
    pick = (jnp.arange(around_cells)[None, :] == jnp.array(edge_at)[:, None]).astype(jnp.float32)
    edges = lax.dot_general(
        pick,
        prec_lines.reshape(-1, around_cells),
        (((1,), (1,)), ((), ())),
        precision=lax.Precision.HIGHEST,
    ).reshape(2, sector_count, comp_count, group_rows)
    cpk = jnp.transpose(edges, (1, 2, 0, 3)).reshape(sector_count, comp_count, 2 * group_rows)

    def row_pack(row):
        return jnp.transpose(row.reshape(comp_count, sector_count, sector_width), (1, 0, 2))

    prec_t, halo_cols, before_rows, after_rows = from_lines_with_halo(
        prec_lines, cpk, row_pack(prec_lines[:, -1]), row_pack(prec_lines[:, 0]), sector_count
    )
    ax = lax.axis_index("ax")
    before_row = jnp.where(ax == 0, 0.0, before_rows[sector_count - 1, :comp_count])
    after_row = jnp.where(ax == lax.axis_size("ax") - 1, 0.0, after_rows[0, :comp_count])
    got_cols = jnp.transpose(halo_cols[:, :comp_count, : 2 * group_rows], (1, 0, 2))
    got_cols = got_cols.reshape(comp_count, sector_count, 2, group_rows)
    before_col = got_cols[:, :, 0].reshape(comp_count, slab_count)
    after_col = got_cols[:, :, 1].reshape(comp_count, slab_count)
    stiffness_t = jnp.transpose(stiffness, (1, 0, 2))
    halo_rows = jnp.pad(jnp.stack([before_row, after_row]), ((0, 0), (0, subl - comp_count), (0, 0)))
    halo_cols = jnp.stack([before_col, after_col])[..., None]
    cell_total = slab_count * lax.axis_size("ax") * comp_count * around_cells
    finished, image_t = image_and_totals(
        residual_t, prec_t, stiffness_t, solid_t[0], halo_rows, halo_cols, cell_total, 0
    )
    disp_new_t, residual_new_t = apply_step(
        finished, jnp.transpose(disp, (1, 0, 2)), prec_t, residual_t, image_t
    )
    return (
        jnp.transpose(disp_new_t, (1, 0, 2)),
        jnp.transpose(residual_new_t, (1, 0, 2)),
        finished[0, 1:4],
    )


def solution(mesh):
    in_specs = (
        P("ax", None, "sec"),
        P("ax", None, "sec"),
        P("ax", None, "sec"),
        P("ax", "sec"),
        P("ax"),
        P(),
        P(),
    )
    out_specs = (P("ax", None, "sec"), P("ax", None, "sec"), P())
    return jax.shard_map(shards, mesh=mesh, in_specs=in_specs, out_specs=out_specs, check_vma=False)
```

```python
import functools
import math

import jax
import jax.numpy as jnp
from jax import lax
from jax.experimental import pallas as pl
from jax.experimental.pallas import tpu as pltpu
from jax.sharding import PartitionSpec as P


MESH = pl.DeviceIdType.MESH


def _groups():
    me_ax = lax.axis_index("ax")
    me_sec = lax.axis_index("sec")
    x = me_ax % 4
    z = (me_ax // 4) % 8
    ylo = me_ax // 32
    core = me_sec % 2
    yhi = me_sec // 2

    def plane_peer(c):
        y = c % 4
        return ((y % 2) * 32 + z * 4 + (c // 4) % 4, (y // 2) * 2 + c // 16)

    return [
        (32, (core * 4 + x) * 4 + yhi * 2 + ylo, plane_peer),
        (8, z, lambda c: (me_ax - z * 4 + c * 4, me_sec)),
    ]


def _image_and_sums(r_ref, p_ref, s_ref, m_ref, hr_ref, hc_ref, img_ref):
    comps, rows, width = p_ref.shape
    row = lax.broadcasted_iota(jnp.int32, (rows, width), 0)
    lane = lax.broadcasted_iota(jnp.int32, (rows, width), 1)
    solid = m_ref[...]
    acc = [jnp.zeros((1, width), jnp.float32) for _ in range(5)]
    for q in range(comps):
        field = p_ref[q]
        up = jnp.where(row == 0, hr_ref[0, q : q + 1, :], pltpu.roll(field, 1, 0))
        down = jnp.where(row == rows - 1, hr_ref[1, q : q + 1, :], pltpu.roll(field, rows - 1, 0))
        left = jnp.where(lane == 0, hc_ref[0, q], pltpu.roll(field, 1, 1))
        right = jnp.where(lane == width - 1, hc_ref[1, q], pltpu.roll(field, width - 1, 1))
        beside = down + up + right + left
        image = solid * ((s_ref[q] + 4.5) * field - beside - 0.5 * p_ref[q ^ 1])
        img_ref[q] = image
        res = r_ref[q]
        for k, prod in enumerate((res * field, field * image, res * res, res * image, image * image)):
            acc[k] = acc[k] + jnp.sum(prod, axis=0, keepdims=True)
    lane8 = lax.broadcasted_iota(jnp.int32, (8, 128), 1)
    row8 = lax.broadcasted_iota(jnp.int32, (8, 128), 0)
    packed = jnp.zeros((8, 128), jnp.float32)
    for k, a in enumerate(acc):
        packed = jnp.where((row8 == 0) & (lane8 == k), jnp.sum(a), packed)
    return packed


def _finish(total, cell_total):
    lane = lax.broadcasted_iota(jnp.int32, total.shape, 1)
    row = lax.broadcasted_iota(jnp.int32, total.shape, 0)

    def pick(k):
        return jnp.sum(jnp.where((row == 0) & (lane == k), total, 0.0), keepdims=True)

    inner_rz = pick(0) / cell_total
    inner_zq = pick(1) / cell_total
    alpha = inner_rz / inner_zq
    square_new = (pick(2) - alpha * (2.0 * pick(3) - alpha * pick(4))) / cell_total
    out = jnp.zeros(total.shape, jnp.float32)
    for k, v in enumerate((alpha, inner_rz, inner_zq, square_new)):
        out = jnp.where((row == 0) & (lane == k), v, out)
    return out


def _ar_kernel(cell_total, r_ref, p_ref, s_ref, m_ref, hr_ref, hc_ref, o_ref, img_ref, recv_a, recv_b, own, send_sems, recv_sems):
    recvs = (recv_a, recv_b)
    groups = _groups()
    for r in recvs:
        r[...] = jnp.zeros_like(r)
    barrier = pltpu.get_barrier_semaphore()
    count = 0
    for n, mine, dev in groups:
        for d in range(1, n):
            pl.semaphore_signal(barrier, inc=1, device_id=dev((mine + d) % n), device_id_type=MESH)
            count += 1
    own[0] = _image_and_sums(r_ref, p_ref, s_ref, m_ref, hr_ref, hc_ref, img_ref)
    pl.semaphore_wait(barrier, count)
    base = 0
    for g, (n, mine, dev) in enumerate(groups):
        src = own.at[g]
        copies = []
        for d in range(1, n):
            cp = pltpu.make_async_remote_copy(
                src_ref=src,
                dst_ref=recvs[g].at[mine],
                send_sem=send_sems.at[base + d],
                recv_sem=recv_sems.at[base + d],
                device_id=dev((mine + d) % n),
                device_id_type=MESH,
            )
            cp.start()
            copies.append(cp)
        mine_val = src[...]
        for cp in copies:
            cp.wait_recv()
        total = None
        for c in range(n):
            v = jnp.where(mine == c, mine_val, recvs[g][c])
            total = v if total is None else total + v
        for cp in copies:
            cp.wait_send()
        base += n
        if g + 1 < len(groups):
            own[g + 1] = total
        else:
            finished = _finish(total, cell_total)
            o_ref[...] = finished


def image_and_totals(residual, prec, stiffness, solid, halo_rows, halo_cols, cell_total, cid):
    return pl.pallas_call(
        functools.partial(_ar_kernel, float(cell_total)),
        out_shape=[
            jax.ShapeDtypeStruct((8, 128), jnp.float32),
            jax.ShapeDtypeStruct(prec.shape, jnp.float32),
        ],
        in_specs=[pl.BlockSpec(memory_space=pltpu.VMEM)] * 6,
        out_specs=[pl.BlockSpec(memory_space=pltpu.VMEM)] * 2,
        scratch_shapes=[
            pltpu.VMEM((32, 8, 128), jnp.float32),
            pltpu.VMEM((8, 8, 128), jnp.float32),
            pltpu.VMEM((2, 8, 128), jnp.float32),
            pltpu.SemaphoreType.DMA((40,)),
            pltpu.SemaphoreType.DMA((40,)),
        ],
        compiler_params=pltpu.CompilerParams(collective_id=cid, has_side_effects=True),
    )(residual, prec, stiffness, solid, halo_rows, halo_cols)


def _update_kernel(f_ref, d_ref, p_ref, r_ref, i_ref, dn_ref, rn_ref):
    alpha = f_ref[0:1, 0:1]
    for q in range(d_ref.shape[0]):
        dn_ref[q] = d_ref[q] + alpha * p_ref[q]
        rn_ref[q] = r_ref[q] - alpha * i_ref[q]


def apply_step(finished, disp, prec, residual, image):
    comps, rows, width = prec.shape
    steps = 2 if comps % 2 == 0 else 1
    plane = pl.BlockSpec((comps // steps, rows, width), lambda q: (q, 0, 0))
    return pl.pallas_call(
        _update_kernel,
        grid=(steps,),
        out_shape=[jax.ShapeDtypeStruct(prec.shape, jnp.float32)] * 2,
        in_specs=[pl.BlockSpec((8, 128), lambda q: (0, 0))] + [plane] * 4,
        out_specs=[plane] * 2,
    )(finished, disp, prec, residual, image)


def _to_lines_kernel(n, count, *refs):
    x_refs, o_refs = refs[:count], refs[count : 2 * count]
    send_sems, recv_sems, local_sems = refs[2 * count :]
    me = lax.axis_index("sec")
    ax = lax.axis_index("ax")
    barrier = pltpu.get_barrier_semaphore()
    for d in range(1, n):
        pl.semaphore_signal(barrier, inc=1, device_id=(ax, (me + d) % n), device_id_type=MESH)
    pl.semaphore_wait(barrier, n - 1)
    copies, local = [], []
    for i, (x_ref, o_ref) in enumerate(zip(x_refs, o_refs)):
        rows, width = o_ref.shape[1], x_ref.shape[2]
        dst = o_ref.at[:, :, pl.ds(pl.multiple_of(me * width, width), width)]
        for d in range(1, n):
            peer = (me + d) % n
            cp = pltpu.make_async_remote_copy(
                src_ref=x_ref.at[:, pl.ds(pl.multiple_of(peer * rows, rows), rows), :],
                dst_ref=dst,
                send_sem=send_sems.at[i * n + d],
                recv_sem=recv_sems.at[i * n + d],
                device_id=(ax, peer),
                device_id_type=MESH,
            )
            cp.start()
            copies.append(cp)
        local.append(
            pltpu.make_async_copy(
                x_ref.at[:, pl.ds(pl.multiple_of(me * rows, rows), rows), :], dst, local_sems.at[i]
            )
        )
        local[-1].start()
    for cp in local:
        cp.wait()
    for cp in copies:
        cp.wait()


def to_lines(arrays, n):
    count = len(arrays)
    shapes = [(x.shape[0], x.shape[1] // n, x.shape[2] * n) for x in arrays]
    return pl.pallas_call(
        functools.partial(_to_lines_kernel, n, count),
        out_shape=[jax.ShapeDtypeStruct(s, x.dtype) for s, x in zip(shapes, arrays)],
        in_specs=[pl.BlockSpec(memory_space=pltpu.VMEM)] * count,
        out_specs=[pl.BlockSpec(memory_space=pltpu.VMEM)] * count,
        scratch_shapes=[
            pltpu.SemaphoreType.DMA((count * n,)),
            pltpu.SemaphoreType.DMA((count * n,)),
            pltpu.SemaphoreType.DMA((count,)),
        ],
        compiler_params=pltpu.CompilerParams(collective_id=1, has_side_effects=True),
    )(*arrays)


def _from_lines_kernel(sizes, x_ref, cpk_ref, last_ref, first_ref, o_ref, cols_ref, before_ref,
                       after_ref, send_sems, recv_sems, local_sems):
    n_ax, n = sizes
    me = lax.axis_index("sec")
    ax = lax.axis_index("ax")
    rows, width = x_ref.shape[1], o_ref.shape[2]
    up_ax, down_ax = (ax + 1) % n_ax, (ax + n_ax - 1) % n_ax
    peers = [(ax, (me + d) % n) for d in range(1, n)]
    peers += [(up_ax, s) for s in range(n)] + [(down_ax, s) for s in range(n)]
    barrier = pltpu.get_barrier_semaphore()
    for peer in peers:
        pl.semaphore_signal(barrier, inc=1, device_id=peer, device_id_type=MESH)
    pl.semaphore_wait(barrier, len(peers))
    dst = o_ref.at[:, pl.ds(pl.multiple_of(me * rows, rows), rows), :]
    sends, recvs = [], []
    for d in range(1, n):
        peer = (me + d) % n
        for k, (src, out) in enumerate(
            (
                (x_ref.at[:, :, pl.ds(pl.multiple_of(peer * width, width), width)], dst),
                (cpk_ref.at[peer], cols_ref.at[me]),
            )
        ):
            cp = pltpu.make_async_remote_copy(
                src_ref=src,
                dst_ref=out,
                send_sem=send_sems.at[k * n + d],
                recv_sem=recv_sems.at[k * n + d],
                device_id=(ax, peer),
                device_id_type=MESH,
            )
            cp.start()
            sends.append(cp)
        origin = (me + n - d) % n
        for k, (src, out) in enumerate(
            (
                (x_ref.at[:, :, pl.ds(0, width)], o_ref.at[:, pl.ds(pl.multiple_of(origin * rows, rows), rows), :]),
                (cpk_ref.at[0], cols_ref.at[origin]),
            )
        ):
            recvs.append(
                pltpu.make_async_remote_copy(
                    src_ref=src,
                    dst_ref=out,
                    send_sem=send_sems.at[k * n + d],
                    recv_sem=recv_sems.at[k * n + d],
                    device_id=(ax, origin),
                    device_id_type=MESH,
                )
            )
    for s in range(n):
        for k, (src, out, target) in enumerate(
            ((last_ref.at[s], before_ref.at[me], up_ax), (first_ref.at[s], after_ref.at[me], down_ax))
        ):
            base = (2 + k) * n
            cp = pltpu.make_async_remote_copy(
                src_ref=src,
                dst_ref=out,
                send_sem=send_sems.at[base + s],
                recv_sem=recv_sems.at[base + me],
                device_id=(target, s),
                device_id_type=MESH,
            )
            cp.start()
            sends.append(cp)
            recvs.append(
                pltpu.make_async_remote_copy(
                    src_ref=src,
                    dst_ref=(before_ref, after_ref)[k].at[s],
                    send_sem=send_sems.at[base + s],
                    recv_sem=recv_sems.at[base + s],
                    device_id=(target, s),
                    device_id_type=MESH,
                )
            )
    local = [
        pltpu.make_async_copy(
            x_ref.at[:, :, pl.ds(pl.multiple_of(me * width, width), width)], dst, local_sems.at[0]
        ),
        pltpu.make_async_copy(cpk_ref.at[me], cols_ref.at[me], local_sems.at[1]),
    ]
    for cp in local:
        cp.start()
    for cp in local:
        cp.wait()
    for cp in recvs:
        cp.wait_recv()
    for cp in sends:
        cp.wait_send()


def from_lines_with_halo(x, cpk, last, first, n):
    comps, rows, around = x.shape
    n_ax = lax.axis_size("ax")
    shapes = [
        (comps, rows * n, around // n),
        cpk.shape,
        (n,) + last.shape[1:],
        (n,) + first.shape[1:],
    ]
    return pl.pallas_call(
        functools.partial(_from_lines_kernel, (n_ax, n)),
        out_shape=[jax.ShapeDtypeStruct(s, x.dtype) for s in shapes],
        in_specs=[pl.BlockSpec(memory_space=pltpu.VMEM)] * 4,
        out_specs=[pl.BlockSpec(memory_space=pltpu.VMEM)] * 4,
        scratch_shapes=[
            pltpu.SemaphoreType.DMA((4 * n,)),
            pltpu.SemaphoreType.DMA((4 * n,)),
            pltpu.SemaphoreType.DMA((2,)),
        ],
        compiler_params=pltpu.CompilerParams(collective_id=2, has_side_effects=True),
    )(x, cpk, last, first)


def cas_table(length):
    root = int(round(math.sqrt(length)))
    index = jnp.arange(length)
    step = 2.0 * math.pi / length
    coarse = step * ((root * jnp.arange(length // root)[:, None] * index[None, :]) % length).astype(jnp.float32)
    fine = step * ((jnp.arange(root)[:, None] * index[None, :]) % length).astype(jnp.float32) - 0.25 * math.pi
    scale = math.sqrt(2.0)
    table = jnp.cos(coarse)[:, None] * (scale * jnp.cos(fine))[None] - jnp.sin(coarse)[:, None] * (
        scale * jnp.sin(fine)
    )[None]
    return table.reshape(length, length)


def paired_inverse(precond):
    mirror = jnp.flip(jnp.roll(precond, -1, axis=2), axis=2)
    return 0.5 * (precond + mirror)


def with_halo(x, sides, width, wrap):
    for axis, dim in sides:
        size, length = (lax.axis_size(axis), x.shape[dim])
        up = [(i, (i + 1) % size) for i in range(size if wrap else size - 1)]
        down = [(j, i) for i, j in up]
        last = lax.slice_in_dim(x, length - width, length, axis=dim)
        first = lax.slice_in_dim(x, 0, width, axis=dim)
        before = lax.ppermute(last, axis, up)
        after = lax.ppermute(first, axis, down)
        x = jnp.concatenate([before, x, after], axis=dim)
    return x


def swap_channels(field):
    extent = field.shape
    folded = field.reshape((extent[0] // 2, 2) + extent[1:])
    return jnp.flip(folded, axis=1).reshape(extent)


def swap_radial(field):
    extent = field.shape
    folded = field.reshape(extent[0], extent[1] // 2, 2, extent[2])
    return jnp.flip(folded, axis=2).reshape(extent)


def apply_operator(field, stiffness):
    axial_pad = with_halo(field, (("ax", 0),), 1, False)
    sector_pad = with_halo(field, (("sec", 2),), 1, True)
    beside = axial_pad[2:] + axial_pad[:-2]
    beside = beside + sector_pad[:, :, 2:] + sector_pad[:, :, :-2]
    return (stiffness + 4.5) * field - beside - 0.5 * swap_radial(field)


def shards(load, disp, stiff, hole, section_class, class_table, precond):
    slab_count, comp_count, sector_width = disp.shape
    sector_count = lax.axis_size("sec")
    around_cells = sector_width * sector_count
    total_axial = slab_count * lax.axis_size("ax")
    position = lax.axis_index("ax") * slab_count + jnp.arange(slab_count)
    taper = 1.0 + 2.0 * position.astype(jnp.float32) / (total_axial - 1)
    one_hot = (section_class[:, None] == jnp.arange(class_table.shape[0])[None, :]).astype(
        jnp.float32
    )
    factors = jnp.dot(one_hot, class_table, precision=lax.Precision.HIGHEST)
    stiffness = stiff * (factors * taper[:, None])[:, :, None]
    solid = (1 - hole).astype(jnp.float32)[:, None, :]
    residual = solid * (load - apply_operator(disp, stiffness))
    residual_t = jnp.transpose(residual, (1, 0, 2))
    solid_t = jnp.transpose(solid, (1, 0, 2))
    lines, solid_lines = to_lines([residual_t, solid_t], sector_count)
    table = cas_table(around_cells)
    spectrum = lax.optimization_barrier(
        lax.dot_general(
            lax.optimization_barrier(lines.reshape(-1, around_cells)),
            table,
            (((1,), (1,)), ((), ())),
            precision=lax.Precision.HIGH,
        )
    ).reshape(lines.shape)
    mixed = jnp.sum(paired_inverse(precond)[:, :, None] * spectrum[None], axis=1)
    smoothed_lines = lax.dot_general(
        mixed.reshape(-1, around_cells),
        table,
        (((1,), (1,)), ((), ())),
        precision=lax.Precision.HIGH,
    ) / around_cells
    prec_lines = solid_lines * smoothed_lines.reshape(lines.shape)
    group_rows = lines.shape[1]
    subl = -(-comp_count // 8) * 8
    edge_at = [(p * sector_width - 1) % around_cells for p in range(sector_count)]
    edge_at += [((p + 1) * sector_width) % around_cells for p in range(sector_count)]
    pick = (jnp.arange(around_cells)[None, :] == jnp.array(edge_at)[:, None]).astype(jnp.float32)
    edges = lax.dot_general(
        pick,
        prec_lines.reshape(-1, around_cells),
        (((1,), (1,)), ((), ())),
        precision=lax.Precision.HIGHEST,
    ).reshape(2, sector_count, comp_count, group_rows)
    cpk = jnp.transpose(edges, (1, 2, 0, 3)).reshape(sector_count, comp_count, 2 * group_rows)

    def row_pack(row):
        return jnp.transpose(row.reshape(comp_count, sector_count, sector_width), (1, 0, 2))

    prec_t, halo_cols, before_rows, after_rows = from_lines_with_halo(
        prec_lines, cpk, row_pack(prec_lines[:, -1]), row_pack(prec_lines[:, 0]), sector_count
    )
    ax = lax.axis_index("ax")
    before_row = jnp.where(ax == 0, 0.0, before_rows[sector_count - 1, :comp_count])
    after_row = jnp.where(ax == lax.axis_size("ax") - 1, 0.0, after_rows[0, :comp_count])
    got_cols = jnp.transpose(halo_cols[:, :comp_count, : 2 * group_rows], (1, 0, 2))
    got_cols = got_cols.reshape(comp_count, sector_count, 2, group_rows)
    before_col = got_cols[:, :, 0].reshape(comp_count, slab_count)
    after_col = got_cols[:, :, 1].reshape(comp_count, slab_count)
    stiffness_t = jnp.transpose(stiffness, (1, 0, 2))
    halo_rows = jnp.pad(jnp.stack([before_row, after_row]), ((0, 0), (0, subl - comp_count), (0, 0)))
    halo_cols = jnp.stack([before_col, after_col])[..., None]
    cell_total = slab_count * lax.axis_size("ax") * comp_count * around_cells
    finished, image_t = image_and_totals(
        residual_t, prec_t, stiffness_t, solid_t[0], halo_rows, halo_cols, cell_total, 0
    )
    disp_new_t, residual_new_t = apply_step(
        finished, jnp.transpose(disp, (1, 0, 2)), prec_t, residual_t, image_t
    )
    return (
        jnp.transpose(disp_new_t, (1, 0, 2)),
        jnp.transpose(residual_new_t, (1, 0, 2)),
        finished[0, 1:4],
    )


def solution(mesh):
    in_specs = (
        P("ax", None, "sec"),
        P("ax", None, "sec"),
        P("ax", None, "sec"),
        P("ax", "sec"),
        P("ax"),
        P(),
        P(),
    )
    out_specs = (P("ax", None, "sec"), P("ax", None, "sec"), P())
    return jax.shard_map(shards, mesh=mesh, in_specs=in_specs, out_specs=out_specs, check_vma=False)
```

```python
import functools
import math

import jax
import jax.numpy as jnp
from jax import lax
from jax.experimental import pallas as pl
from jax.experimental.pallas import tpu as pltpu
from jax.sharding import PartitionSpec as P


MESH = pl.DeviceIdType.MESH


def _groups():
    me_ax = lax.axis_index("ax")
    me_sec = lax.axis_index("sec")
    x = me_ax % 4
    z = (me_ax // 4) % 8
    ylo = me_ax // 32
    core = me_sec % 2
    yhi = me_sec // 2

    def plane_peer(c):
        y = c % 4
        return ((y % 2) * 32 + z * 4 + (c // 4) % 4, (y // 2) * 2 + c // 16)

    return [
        (32, (core * 4 + x) * 4 + yhi * 2 + ylo, plane_peer),
        (8, z, lambda c: (me_ax - z * 4 + c * 4, me_sec)),
    ]


def _image_and_sums(r_ref, p_ref, s_ref, m_ref, br_ref, ar_ref, hc_ref, img_ref):
    comps, rows, width = p_ref.shape
    ax = lax.axis_index("ax")
    first_slab = ax == 0
    last_slab = ax == lax.axis_size("ax") - 1

    def before_row(q):
        return jnp.where(first_slab, 0.0, br_ref[br_ref.shape[0] - 1, q : q + 1, :])

    def after_row(q):
        return jnp.where(last_slab, 0.0, ar_ref[0, q : q + 1, :])

    row = lax.broadcasted_iota(jnp.int32, (rows, width), 0)
    lane = lax.broadcasted_iota(jnp.int32, (rows, width), 1)
    solid = m_ref[...]
    acc = [jnp.zeros((1, width), jnp.float32) for _ in range(5)]
    for q in range(comps):
        field = p_ref[q]
        up = jnp.where(row == 0, before_row(q), pltpu.roll(field, 1, 0))
        down = jnp.where(row == rows - 1, after_row(q), pltpu.roll(field, rows - 1, 0))
        left = jnp.where(lane == 0, hc_ref[0, q], pltpu.roll(field, 1, 1))
        right = jnp.where(lane == width - 1, hc_ref[1, q], pltpu.roll(field, width - 1, 1))
        beside = down + up + right + left
        image = solid * ((s_ref[q] + 4.5) * field - beside - 0.5 * p_ref[q ^ 1])
        img_ref[q] = image
        res = r_ref[q]
        for k, prod in enumerate((res * field, field * image, res * res, res * image, image * image)):
            acc[k] = acc[k] + jnp.sum(prod, axis=0, keepdims=True)
    lane8 = lax.broadcasted_iota(jnp.int32, (8, 128), 1)
    row8 = lax.broadcasted_iota(jnp.int32, (8, 128), 0)
    packed = jnp.zeros((8, 128), jnp.float32)
    for k, a in enumerate(acc):
        packed = jnp.where((row8 == 0) & (lane8 == k), jnp.sum(a), packed)
    return packed


def _finish(total, cell_total):
    lane = lax.broadcasted_iota(jnp.int32, total.shape, 1)
    row = lax.broadcasted_iota(jnp.int32, total.shape, 0)

    def pick(k):
        return jnp.sum(jnp.where((row == 0) & (lane == k), total, 0.0), keepdims=True)

    inner_rz = pick(0) / cell_total
    inner_zq = pick(1) / cell_total
    alpha = inner_rz / inner_zq
    square_new = (pick(2) - alpha * (2.0 * pick(3) - alpha * pick(4))) / cell_total
    out = jnp.zeros(total.shape, jnp.float32)
    for k, v in enumerate((alpha, inner_rz, inner_zq, square_new)):
        out = jnp.where((row == 0) & (lane == k), v, out)
    return out


def _ar_kernel(cell_total, r_ref, p_ref, s_ref, m_ref, br_ref, ar_ref, hc_ref, o_ref, img_ref, recv_a, recv_b, own, send_sems, recv_sems):
    recvs = (recv_a, recv_b)
    groups = _groups()
    for r in recvs:
        r[...] = jnp.zeros_like(r)
    barrier = pltpu.get_barrier_semaphore()
    count = 0
    for n, mine, dev in groups:
        for d in range(1, n):
            pl.semaphore_signal(barrier, inc=1, device_id=dev((mine + d) % n), device_id_type=MESH)
            count += 1
    own[0] = _image_and_sums(r_ref, p_ref, s_ref, m_ref, br_ref, ar_ref, hc_ref, img_ref)
    pl.semaphore_wait(barrier, count)
    base = 0
    for g, (n, mine, dev) in enumerate(groups):
        src = own.at[g]
        copies = []
        for d in range(1, n):
            cp = pltpu.make_async_remote_copy(
                src_ref=src,
                dst_ref=recvs[g].at[mine],
                send_sem=send_sems.at[base + d],
                recv_sem=recv_sems.at[base + d],
                device_id=dev((mine + d) % n),
                device_id_type=MESH,
            )
            cp.start()
            copies.append(cp)
        mine_val = src[...]
        for cp in copies:
            cp.wait_recv()
        total = None
        for c in range(n):
            v = jnp.where(mine == c, mine_val, recvs[g][c])
            total = v if total is None else total + v
        for cp in copies:
            cp.wait_send()
        base += n
        if g + 1 < len(groups):
            own[g + 1] = total
        else:
            finished = _finish(total, cell_total)
            o_ref[...] = finished


def image_and_totals(residual, prec, stiffness, solid, before_rows, after_rows, halo_cols, cell_total, cid):
    return pl.pallas_call(
        functools.partial(_ar_kernel, float(cell_total)),
        out_shape=[
            jax.ShapeDtypeStruct((8, 128), jnp.float32),
            jax.ShapeDtypeStruct(prec.shape, jnp.float32),
        ],
        in_specs=[pl.BlockSpec(memory_space=pltpu.VMEM)] * 7,
        out_specs=[pl.BlockSpec(memory_space=pltpu.VMEM)] * 2,
        scratch_shapes=[
            pltpu.VMEM((32, 8, 128), jnp.float32),
            pltpu.VMEM((8, 8, 128), jnp.float32),
            pltpu.VMEM((2, 8, 128), jnp.float32),
            pltpu.SemaphoreType.DMA((40,)),
            pltpu.SemaphoreType.DMA((40,)),
        ],
        compiler_params=pltpu.CompilerParams(collective_id=cid, has_side_effects=True),
    )(residual, prec, stiffness, solid, before_rows, after_rows, halo_cols)


def _update_kernel(f_ref, d_ref, p_ref, r_ref, i_ref, dn_ref, rn_ref):
    alpha = f_ref[0:1, 0:1]
    for q in range(d_ref.shape[0]):
        dn_ref[q] = d_ref[q] + alpha * p_ref[q]
        rn_ref[q] = r_ref[q] - alpha * i_ref[q]


def apply_step(finished, disp, prec, residual, image):
    comps, rows, width = prec.shape
    steps = 2 if comps % 2 == 0 else 1
    plane = pl.BlockSpec((comps // steps, rows, width), lambda q: (q, 0, 0))
    return pl.pallas_call(
        _update_kernel,
        grid=(steps,),
        out_shape=[jax.ShapeDtypeStruct(prec.shape, jnp.float32)] * 2,
        in_specs=[pl.BlockSpec((8, 128), lambda q: (0, 0))] + [plane] * 4,
        out_specs=[plane] * 2,
    )(finished, disp, prec, residual, image)


def _to_lines_kernel(n, count, *refs):
    x_refs, o_refs = refs[:count], refs[count : 2 * count]
    send_sems, recv_sems, local_sems = refs[2 * count :]
    me = lax.axis_index("sec")
    ax = lax.axis_index("ax")
    barrier = pltpu.get_barrier_semaphore()
    for d in range(1, n):
        pl.semaphore_signal(barrier, inc=1, device_id=(ax, (me + d) % n), device_id_type=MESH)
    pl.semaphore_wait(barrier, n - 1)
    copies, local = [], []
    for i, (x_ref, o_ref) in enumerate(zip(x_refs, o_refs)):
        rows, width = o_ref.shape[1], x_ref.shape[2]
        dst = o_ref.at[:, :, pl.ds(pl.multiple_of(me * width, width), width)]
        for d in range(1, n):
            peer = (me + d) % n
            cp = pltpu.make_async_remote_copy(
                src_ref=x_ref.at[:, pl.ds(pl.multiple_of(peer * rows, rows), rows), :],
                dst_ref=dst,
                send_sem=send_sems.at[i * n + d],
                recv_sem=recv_sems.at[i * n + d],
                device_id=(ax, peer),
                device_id_type=MESH,
            )
            cp.start()
            copies.append(cp)
        local.append(
            pltpu.make_async_copy(
                x_ref.at[:, pl.ds(pl.multiple_of(me * rows, rows), rows), :], dst, local_sems.at[i]
            )
        )
        local[-1].start()
    for cp in local:
        cp.wait()
    for cp in copies:
        cp.wait()


def to_lines(arrays, n):
    count = len(arrays)
    shapes = [(x.shape[0], x.shape[1] // n, x.shape[2] * n) for x in arrays]
    return pl.pallas_call(
        functools.partial(_to_lines_kernel, n, count),
        out_shape=[jax.ShapeDtypeStruct(s, x.dtype) for s, x in zip(shapes, arrays)],
        in_specs=[pl.BlockSpec(memory_space=pltpu.VMEM)] * count,
        out_specs=[pl.BlockSpec(memory_space=pltpu.VMEM)] * count,
        scratch_shapes=[
            pltpu.SemaphoreType.DMA((count * n,)),
            pltpu.SemaphoreType.DMA((count * n,)),
            pltpu.SemaphoreType.DMA((count,)),
        ],
        compiler_params=pltpu.CompilerParams(collective_id=1, has_side_effects=True),
    )(*arrays)


def _from_lines_kernel(sizes, x_ref, cpk_ref, last_ref, first_ref, o_ref, cols_ref, before_ref,
                       after_ref, send_sems, recv_sems, local_sems):
    n_ax, n = sizes
    me = lax.axis_index("sec")
    ax = lax.axis_index("ax")
    rows, width = x_ref.shape[1], o_ref.shape[2]
    up_ax, down_ax = (ax + 1) % n_ax, (ax + n_ax - 1) % n_ax
    peers = [(ax, (me + d) % n) for d in range(1, n)]
    peers += [(up_ax, s) for s in range(n)] + [(down_ax, s) for s in range(n)]
    barrier = pltpu.get_barrier_semaphore()
    for peer in peers:
        pl.semaphore_signal(barrier, inc=1, device_id=peer, device_id_type=MESH)
    pl.semaphore_wait(barrier, len(peers))
    dst = o_ref.at[:, pl.ds(pl.multiple_of(me * rows, rows), rows), :]
    sends, recvs = [], []
    for d in range(1, n):
        peer = (me + d) % n
        for k, (src, out) in enumerate(
            (
                (x_ref.at[:, :, pl.ds(pl.multiple_of(peer * width, width), width)], dst),
                (cpk_ref.at[peer], cols_ref.at[me]),
            )
        ):
            cp = pltpu.make_async_remote_copy(
                src_ref=src,
                dst_ref=out,
                send_sem=send_sems.at[k * n + d],
                recv_sem=recv_sems.at[k * n + d],
                device_id=(ax, peer),
                device_id_type=MESH,
            )
            cp.start()
            sends.append(cp)
        origin = (me + n - d) % n
        for k, (src, out) in enumerate(
            (
                (x_ref.at[:, :, pl.ds(0, width)], o_ref.at[:, pl.ds(pl.multiple_of(origin * rows, rows), rows), :]),
                (cpk_ref.at[0], cols_ref.at[origin]),
            )
        ):
            recvs.append(
                pltpu.make_async_remote_copy(
                    src_ref=src,
                    dst_ref=out,
                    send_sem=send_sems.at[k * n + d],
                    recv_sem=recv_sems.at[k * n + d],
                    device_id=(ax, origin),
                    device_id_type=MESH,
                )
            )
    for s in range(n):
        for k, (src, out, target) in enumerate(
            ((last_ref.at[s], before_ref.at[me], up_ax), (first_ref.at[s], after_ref.at[me], down_ax))
        ):
            base = (2 + k) * n
            cp = pltpu.make_async_remote_copy(
                src_ref=src,
                dst_ref=out,
                send_sem=send_sems.at[base + s],
                recv_sem=recv_sems.at[base + me],
                device_id=(target, s),
                device_id_type=MESH,
            )
            cp.start()
            sends.append(cp)
            recvs.append(
                pltpu.make_async_remote_copy(
                    src_ref=src,
                    dst_ref=(before_ref, after_ref)[k].at[s],
                    send_sem=send_sems.at[base + s],
                    recv_sem=recv_sems.at[base + s],
                    device_id=(target, s),
                    device_id_type=MESH,
                )
            )
    local = [
        pltpu.make_async_copy(
            x_ref.at[:, :, pl.ds(pl.multiple_of(me * width, width), width)], dst, local_sems.at[0]
        ),
        pltpu.make_async_copy(cpk_ref.at[me], cols_ref.at[me], local_sems.at[1]),
    ]
    for cp in local:
        cp.start()
    for cp in local:
        cp.wait()
    for cp in recvs:
        cp.wait_recv()
    for cp in sends:
        cp.wait_send()


def from_lines_with_halo(x, cpk, last, first, n):
    comps, rows, around = x.shape
    n_ax = lax.axis_size("ax")
    shapes = [
        (comps, rows * n, around // n),
        cpk.shape,
        (n,) + last.shape[1:],
        (n,) + first.shape[1:],
    ]
    return pl.pallas_call(
        functools.partial(_from_lines_kernel, (n_ax, n)),
        out_shape=[jax.ShapeDtypeStruct(s, x.dtype) for s in shapes],
        in_specs=[pl.BlockSpec(memory_space=pltpu.VMEM)] * 4,
        out_specs=[pl.BlockSpec(memory_space=pltpu.VMEM)] * 4,
        scratch_shapes=[
            pltpu.SemaphoreType.DMA((4 * n,)),
            pltpu.SemaphoreType.DMA((4 * n,)),
            pltpu.SemaphoreType.DMA((2,)),
        ],
        compiler_params=pltpu.CompilerParams(collective_id=2, has_side_effects=True),
    )(x, cpk, last, first)


def dft_table(length):
    half = length // 2
    root = int(round(math.sqrt(length)))
    cols = jnp.concatenate([jnp.arange(half + 1), jnp.arange(1, half)])
    phase = jnp.where(jnp.arange(length) > half, 0.5 * math.pi, 0.0).astype(jnp.float32)
    step = 2.0 * math.pi / length
    coarse = step * ((root * jnp.arange(length // root)[:, None] * cols[None, :]) % length).astype(jnp.float32)
    fine = step * ((jnp.arange(root)[:, None] * cols[None, :]) % length).astype(jnp.float32) - phase
    table = jnp.cos(coarse)[:, None] * jnp.cos(fine)[None] - jnp.sin(coarse)[:, None] * jnp.sin(fine)[None]
    return table.reshape(length, length)


def paired_inverse(precond):
    length = precond.shape[2]
    half = length // 2
    low = precond[:, :, : half + 1]
    mirror = jnp.flip(precond[:, :, half + 1 :], axis=2)
    inner = jnp.concatenate([jnp.zeros_like(low[:, :, :1]), mirror, jnp.zeros_like(low[:, :, :1])], axis=2)
    paired = low + inner
    return jnp.concatenate([paired, paired[:, :, 1:half]], axis=2)


def with_halo(x, sides, width, wrap):
    for axis, dim in sides:
        size, length = (lax.axis_size(axis), x.shape[dim])
        up = [(i, (i + 1) % size) for i in range(size if wrap else size - 1)]
        down = [(j, i) for i, j in up]
        last = lax.slice_in_dim(x, length - width, length, axis=dim)
        first = lax.slice_in_dim(x, 0, width, axis=dim)
        before = lax.ppermute(last, axis, up)
        after = lax.ppermute(first, axis, down)
        x = jnp.concatenate([before, x, after], axis=dim)
    return x


def swap_channels(field):
    extent = field.shape
    folded = field.reshape((extent[0] // 2, 2) + extent[1:])
    return jnp.flip(folded, axis=1).reshape(extent)


def swap_radial(field):
    extent = field.shape
    folded = field.reshape(extent[0], extent[1] // 2, 2, extent[2])
    return jnp.flip(folded, axis=2).reshape(extent)


def apply_operator(field, stiffness):
    axial_pad = with_halo(field, (("ax", 0),), 1, False)
    sector_pad = with_halo(field, (("sec", 2),), 1, True)
    beside = axial_pad[2:] + axial_pad[:-2]
    beside = beside + sector_pad[:, :, 2:] + sector_pad[:, :, :-2]
    return (stiffness + 4.5) * field - beside - 0.5 * swap_radial(field)


def shards(load, disp, stiff, hole, section_class, class_table, precond):
    slab_count, comp_count, sector_width = disp.shape
    sector_count = lax.axis_size("sec")
    around_cells = sector_width * sector_count
    total_axial = slab_count * lax.axis_size("ax")
    position = lax.axis_index("ax") * slab_count + jnp.arange(slab_count)
    taper = 1.0 + 2.0 * position.astype(jnp.float32) / (total_axial - 1)
    one_hot = (section_class[:, None] == jnp.arange(class_table.shape[0])[None, :]).astype(
        jnp.float32
    )
    factors = jnp.dot(one_hot, class_table, precision=lax.Precision.HIGHEST)
    stiffness = stiff * (factors * taper[:, None])[:, :, None]
    solid = (1 - hole).astype(jnp.float32)[:, None, :]
    residual = solid * (load - apply_operator(disp, stiffness))
    residual_t = jnp.transpose(residual, (1, 0, 2))
    solid_t = jnp.transpose(solid, (1, 0, 2))
    lines, solid_lines = to_lines([residual_t, solid_t], sector_count)
    spectrum = lax.optimization_barrier(
        jnp.dot(
            lax.optimization_barrier(lines.reshape(-1, around_cells)),
            dft_table(around_cells),
            precision=lax.Precision.HIGH,
        )
    ).reshape(lines.shape)
    mixed = jnp.sum(paired_inverse(precond)[:, :, None] * spectrum[None], axis=1)
    smoothed_lines = lax.dot_general(
        mixed.reshape(-1, around_cells),
        dft_table(around_cells),
        (((1,), (1,)), ((), ())),
        precision=lax.Precision.HIGH,
    ) / around_cells
    prec_lines = solid_lines * smoothed_lines.reshape(lines.shape)
    group_rows = lines.shape[1]
    edge_at = [(p * sector_width - 1) % around_cells for p in range(sector_count)]
    edge_at += [((p + 1) * sector_width) % around_cells for p in range(sector_count)]
    pick = (jnp.arange(around_cells)[None, :] == jnp.array(edge_at)[:, None]).astype(jnp.float32)
    edges = lax.dot_general(
        pick,
        prec_lines.reshape(-1, around_cells),
        (((1,), (1,)), ((), ())),
        precision=lax.Precision.HIGHEST,
    ).reshape(2, sector_count, comp_count, group_rows)
    cpk = jnp.transpose(edges, (1, 2, 0, 3)).reshape(sector_count, comp_count, 2 * group_rows)

    def row_pack(row):
        return jnp.transpose(row.reshape(comp_count, sector_count, sector_width), (1, 0, 2))

    prec_t, halo_cols, before_rows, after_rows = from_lines_with_halo(
        prec_lines, cpk, row_pack(prec_lines[:, -1]), row_pack(prec_lines[:, 0]), sector_count
    )
    got_cols = jnp.transpose(halo_cols[:, :comp_count, : 2 * group_rows], (1, 0, 2))
    got_cols = got_cols.reshape(comp_count, sector_count, 2, group_rows)
    before_col = got_cols[:, :, 0].reshape(comp_count, slab_count)
    after_col = got_cols[:, :, 1].reshape(comp_count, slab_count)
    stiffness_t = jnp.transpose(stiffness, (1, 0, 2))
    halo_cols = jnp.stack([before_col, after_col])[..., None]
    cell_total = slab_count * lax.axis_size("ax") * comp_count * around_cells
    finished, image_t = image_and_totals(
        residual_t, prec_t, stiffness_t, solid_t[0], before_rows, after_rows, halo_cols, cell_total, 0
    )
    disp_new_t, residual_new_t = apply_step(
        finished, jnp.transpose(disp, (1, 0, 2)), prec_t, residual_t, image_t
    )
    return (
        jnp.transpose(disp_new_t, (1, 0, 2)),
        jnp.transpose(residual_new_t, (1, 0, 2)),
        finished[0, 1:4],
    )


def solution(mesh):
    in_specs = (
        P("ax", None, "sec"),
        P("ax", None, "sec"),
        P("ax", None, "sec"),
        P("ax", "sec"),
        P("ax"),
        P(),
        P(),
    )
    out_specs = (P("ax", None, "sec"), P("ax", None, "sec"), P())
    return jax.shard_map(shards, mesh=mesh, in_specs=in_specs, out_specs=out_specs, check_vma=False)
```

```python
import functools
import math

import jax
import jax.numpy as jnp
from jax import lax
from jax.experimental import pallas as pl
from jax.experimental.pallas import tpu as pltpu
from jax.sharding import PartitionSpec as P


MESH = pl.DeviceIdType.MESH


def _groups():
    me_ax = lax.axis_index("ax")
    me_sec = lax.axis_index("sec")
    x = me_ax % 4
    z = (me_ax // 4) % 8
    ylo = me_ax // 32
    core = me_sec % 2
    yhi = me_sec // 2

    def plane_peer(c):
        y = c % 4
        return ((y % 2) * 32 + z * 4 + (c // 4) % 4, (y // 2) * 2 + c // 16)

    return [
        (32, (core * 4 + x) * 4 + yhi * 2 + ylo, plane_peer),
        (8, z, lambda c: (me_ax - z * 4 + c * 4, me_sec)),
    ]


def _image_and_sums(r_ref, p_ref, s_ref, m_ref, br_ref, ar_ref, hc_ref, img_ref):
    comps, rows, width = p_ref.shape
    ax = lax.axis_index("ax")
    first_slab = ax == 0
    last_slab = ax == lax.axis_size("ax") - 1

    def before_row(q):
        return jnp.where(first_slab, 0.0, br_ref[br_ref.shape[0] - 1, q : q + 1, :])

    def after_row(q):
        return jnp.where(last_slab, 0.0, ar_ref[0, q : q + 1, :])

    flipped = [hc_ref[g].T for g in range(hc_ref.shape[0])]
    part = rows // len(flipped)

    def column(w, q):
        pieces = [t[w * part : (w + 1) * part, q : q + 1] for t in flipped]
        return jnp.broadcast_to(jnp.concatenate(pieces, axis=0), (rows, width))

    row = lax.broadcasted_iota(jnp.int32, (rows, width), 0)
    lane = lax.broadcasted_iota(jnp.int32, (rows, width), 1)
    solid = m_ref[...]
    acc = [jnp.zeros((1, width), jnp.float32) for _ in range(5)]
    for q in range(comps):
        field = p_ref[q]
        up = jnp.where(row == 0, before_row(q), pltpu.roll(field, 1, 0))
        down = jnp.where(row == rows - 1, after_row(q), pltpu.roll(field, rows - 1, 0))
        left = jnp.where(lane == 0, column(0, q), pltpu.roll(field, 1, 1))
        right = jnp.where(lane == width - 1, column(1, q), pltpu.roll(field, width - 1, 1))
        beside = down + up + right + left
        image = solid * ((s_ref[q] + 4.5) * field - beside - 0.5 * p_ref[q ^ 1])
        img_ref[q] = image
        res = r_ref[q]
        for k, prod in enumerate((res * field, field * image, res * res, res * image, image * image)):
            acc[k] = acc[k] + jnp.sum(prod, axis=0, keepdims=True)
    lane8 = lax.broadcasted_iota(jnp.int32, (8, 128), 1)
    row8 = lax.broadcasted_iota(jnp.int32, (8, 128), 0)
    packed = jnp.zeros((8, 128), jnp.float32)
    for k, a in enumerate(acc):
        packed = jnp.where((row8 == 0) & (lane8 == k), jnp.sum(a), packed)
    return packed


def _finish(total, cell_total):
    lane = lax.broadcasted_iota(jnp.int32, total.shape, 1)
    row = lax.broadcasted_iota(jnp.int32, total.shape, 0)

    def pick(k):
        return jnp.sum(jnp.where((row == 0) & (lane == k), total, 0.0), keepdims=True)

    inner_rz = pick(0) / cell_total
    inner_zq = pick(1) / cell_total
    alpha = inner_rz / inner_zq
    square_new = (pick(2) - alpha * (2.0 * pick(3) - alpha * pick(4))) / cell_total
    out = jnp.zeros(total.shape, jnp.float32)
    for k, v in enumerate((alpha, inner_rz, inner_zq, square_new)):
        out = jnp.where((row == 0) & (lane == k), v, out)
    return out


def _ar_kernel(cell_total, r_ref, p_ref, s_ref, m_ref, br_ref, ar_ref, hc_ref, o_ref, img_ref, recv_a, recv_b, own, send_sems, recv_sems):
    recvs = (recv_a, recv_b)
    groups = _groups()
    for r in recvs:
        r[...] = jnp.zeros_like(r)
    barrier = pltpu.get_barrier_semaphore()
    count = 0
    for n, mine, dev in groups:
        for d in range(1, n):
            pl.semaphore_signal(barrier, inc=1, device_id=dev((mine + d) % n), device_id_type=MESH)
            count += 1
    own[0] = _image_and_sums(r_ref, p_ref, s_ref, m_ref, br_ref, ar_ref, hc_ref, img_ref)
    pl.semaphore_wait(barrier, count)
    base = 0
    for g, (n, mine, dev) in enumerate(groups):
        src = own.at[g]
        copies = []
        for d in range(1, n):
            cp = pltpu.make_async_remote_copy(
                src_ref=src,
                dst_ref=recvs[g].at[mine],
                send_sem=send_sems.at[base + d],
                recv_sem=recv_sems.at[base + d],
                device_id=dev((mine + d) % n),
                device_id_type=MESH,
            )
            cp.start()
            copies.append(cp)
        mine_val = src[...]
        for cp in copies:
            cp.wait_recv()
        total = None
        for c in range(n):
            v = jnp.where(mine == c, mine_val, recvs[g][c])
            total = v if total is None else total + v
        for cp in copies:
            cp.wait_send()
        base += n
        if g + 1 < len(groups):
            own[g + 1] = total
        else:
            finished = _finish(total, cell_total)
            o_ref[...] = finished


def image_and_totals(residual, prec, stiffness, solid, before_rows, after_rows, halo_cols, cell_total, cid):
    return pl.pallas_call(
        functools.partial(_ar_kernel, float(cell_total)),
        out_shape=[
            jax.ShapeDtypeStruct((8, 128), jnp.float32),
            jax.ShapeDtypeStruct(prec.shape, jnp.float32),
        ],
        in_specs=[pl.BlockSpec(memory_space=pltpu.VMEM)] * 7,
        out_specs=[pl.BlockSpec(memory_space=pltpu.VMEM)] * 2,
        scratch_shapes=[
            pltpu.VMEM((32, 8, 128), jnp.float32),
            pltpu.VMEM((8, 8, 128), jnp.float32),
            pltpu.VMEM((2, 8, 128), jnp.float32),
            pltpu.SemaphoreType.DMA((40,)),
            pltpu.SemaphoreType.DMA((40,)),
        ],
        compiler_params=pltpu.CompilerParams(collective_id=cid, has_side_effects=True),
    )(residual, prec, stiffness, solid, before_rows, after_rows, halo_cols)


def _update_kernel(f_ref, d_ref, p_ref, r_ref, i_ref, dn_ref, rn_ref):
    alpha = f_ref[0:1, 0:1]
    for q in range(d_ref.shape[0]):
        dn_ref[q] = d_ref[q] + alpha * p_ref[q]
        rn_ref[q] = r_ref[q] - alpha * i_ref[q]


def apply_step(finished, disp, prec, residual, image):
    comps, rows, width = prec.shape
    steps = 2 if comps % 2 == 0 else 1
    plane = pl.BlockSpec((comps // steps, rows, width), lambda q: (q, 0, 0))
    return pl.pallas_call(
        _update_kernel,
        grid=(steps,),
        out_shape=[jax.ShapeDtypeStruct(prec.shape, jnp.float32)] * 2,
        in_specs=[pl.BlockSpec((8, 128), lambda q: (0, 0))] + [plane] * 4,
        out_specs=[plane] * 2,
    )(finished, disp, prec, residual, image)


def _to_lines_kernel(n, count, *refs):
    x_refs, o_refs = refs[:count], refs[count : 2 * count]
    send_sems, recv_sems, local_sems = refs[2 * count :]
    me = lax.axis_index("sec")
    ax = lax.axis_index("ax")
    barrier = pltpu.get_barrier_semaphore()
    for d in range(1, n):
        pl.semaphore_signal(barrier, inc=1, device_id=(ax, (me + d) % n), device_id_type=MESH)
    pl.semaphore_wait(barrier, n - 1)
    copies, local = [], []
    for i, (x_ref, o_ref) in enumerate(zip(x_refs, o_refs)):
        rows, width = o_ref.shape[1], x_ref.shape[2]
        dst = o_ref.at[:, :, pl.ds(pl.multiple_of(me * width, width), width)]
        for d in range(1, n):
            peer = (me + d) % n
            cp = pltpu.make_async_remote_copy(
                src_ref=x_ref.at[:, pl.ds(pl.multiple_of(peer * rows, rows), rows), :],
                dst_ref=dst,
                send_sem=send_sems.at[i * n + d],
                recv_sem=recv_sems.at[i * n + d],
                device_id=(ax, peer),
                device_id_type=MESH,
            )
            cp.start()
            copies.append(cp)
        local.append(
            pltpu.make_async_copy(
                x_ref.at[:, pl.ds(pl.multiple_of(me * rows, rows), rows), :], dst, local_sems.at[i]
            )
        )
        local[-1].start()
    for cp in local:
        cp.wait()
    for cp in copies:
        cp.wait()


def to_lines(arrays, n):
    count = len(arrays)
    shapes = [(x.shape[0], x.shape[1] // n, x.shape[2] * n) for x in arrays]
    return pl.pallas_call(
        functools.partial(_to_lines_kernel, n, count),
        out_shape=[jax.ShapeDtypeStruct(s, x.dtype) for s, x in zip(shapes, arrays)],
        in_specs=[pl.BlockSpec(memory_space=pltpu.VMEM)] * count,
        out_specs=[pl.BlockSpec(memory_space=pltpu.VMEM)] * count,
        scratch_shapes=[
            pltpu.SemaphoreType.DMA((count * n,)),
            pltpu.SemaphoreType.DMA((count * n,)),
            pltpu.SemaphoreType.DMA((count,)),
        ],
        compiler_params=pltpu.CompilerParams(collective_id=1, has_side_effects=True),
    )(*arrays)


def _from_lines_kernel(sizes, x_ref, cpk_ref, last_ref, first_ref, o_ref, cols_ref, before_ref,
                       after_ref, send_sems, recv_sems, local_sems):
    n_ax, n = sizes
    me = lax.axis_index("sec")
    ax = lax.axis_index("ax")
    rows, width = x_ref.shape[1], o_ref.shape[2]
    up_ax, down_ax = (ax + 1) % n_ax, (ax + n_ax - 1) % n_ax
    peers = [(ax, (me + d) % n) for d in range(1, n)]
    peers += [(up_ax, s) for s in range(n)] + [(down_ax, s) for s in range(n)]
    barrier = pltpu.get_barrier_semaphore()
    for peer in peers:
        pl.semaphore_signal(barrier, inc=1, device_id=peer, device_id_type=MESH)
    pl.semaphore_wait(barrier, len(peers))
    dst = o_ref.at[:, pl.ds(pl.multiple_of(me * rows, rows), rows), :]
    sends, recvs = [], []
    for d in range(1, n):
        peer = (me + d) % n
        for k, (src, out) in enumerate(
            (
                (x_ref.at[:, :, pl.ds(pl.multiple_of(peer * width, width), width)], dst),
                (cpk_ref.at[peer], cols_ref.at[me]),
            )
        ):
            cp = pltpu.make_async_remote_copy(
                src_ref=src,
                dst_ref=out,
                send_sem=send_sems.at[k * n + d],
                recv_sem=recv_sems.at[k * n + d],
                device_id=(ax, peer),
                device_id_type=MESH,
            )
            cp.start()
            sends.append(cp)
        origin = (me + n - d) % n
        for k, (src, out) in enumerate(
            (
                (x_ref.at[:, :, pl.ds(0, width)], o_ref.at[:, pl.ds(pl.multiple_of(origin * rows, rows), rows), :]),
                (cpk_ref.at[0], cols_ref.at[origin]),
            )
        ):
            recvs.append(
                pltpu.make_async_remote_copy(
                    src_ref=src,
                    dst_ref=out,
                    send_sem=send_sems.at[k * n + d],
                    recv_sem=recv_sems.at[k * n + d],
                    device_id=(ax, origin),
                    device_id_type=MESH,
                )
            )
    for s in range(n):
        for k, (src, out, target) in enumerate(
            ((last_ref.at[s], before_ref.at[me], up_ax), (first_ref.at[s], after_ref.at[me], down_ax))
        ):
            base = (2 + k) * n
            cp = pltpu.make_async_remote_copy(
                src_ref=src,
                dst_ref=out,
                send_sem=send_sems.at[base + s],
                recv_sem=recv_sems.at[base + me],
                device_id=(target, s),
                device_id_type=MESH,
            )
            cp.start()
            sends.append(cp)
            recvs.append(
                pltpu.make_async_remote_copy(
                    src_ref=src,
                    dst_ref=(before_ref, after_ref)[k].at[s],
                    send_sem=send_sems.at[base + s],
                    recv_sem=recv_sems.at[base + s],
                    device_id=(target, s),
                    device_id_type=MESH,
                )
            )
    local = [
        pltpu.make_async_copy(
            x_ref.at[:, :, pl.ds(pl.multiple_of(me * width, width), width)], dst, local_sems.at[0]
        ),
        pltpu.make_async_copy(cpk_ref.at[me], cols_ref.at[me], local_sems.at[1]),
    ]
    for cp in local:
        cp.start()
    for cp in local:
        cp.wait()
    for cp in recvs:
        cp.wait_recv()
    for cp in sends:
        cp.wait_send()


def from_lines_with_halo(x, cpk, last, first, n):
    comps, rows, around = x.shape
    n_ax = lax.axis_size("ax")
    shapes = [
        (comps, rows * n, around // n),
        cpk.shape,
        (n,) + last.shape[1:],
        (n,) + first.shape[1:],
    ]
    return pl.pallas_call(
        functools.partial(_from_lines_kernel, (n_ax, n)),
        out_shape=[jax.ShapeDtypeStruct(s, x.dtype) for s in shapes],
        in_specs=[pl.BlockSpec(memory_space=pltpu.VMEM)] * 4,
        out_specs=[pl.BlockSpec(memory_space=pltpu.VMEM)] * 4,
        scratch_shapes=[
            pltpu.SemaphoreType.DMA((4 * n,)),
            pltpu.SemaphoreType.DMA((4 * n,)),
            pltpu.SemaphoreType.DMA((2,)),
        ],
        compiler_params=pltpu.CompilerParams(collective_id=2, has_side_effects=True),
    )(x, cpk, last, first)


def dft_table(length):
    half = length // 2
    root = int(round(math.sqrt(length)))
    cols = jnp.concatenate([jnp.arange(half + 1), jnp.arange(1, half)])
    phase = jnp.where(jnp.arange(length) > half, 0.5 * math.pi, 0.0).astype(jnp.float32)
    step = 2.0 * math.pi / length
    coarse = step * ((root * jnp.arange(length // root)[:, None] * cols[None, :]) % length).astype(jnp.float32)
    fine = step * ((jnp.arange(root)[:, None] * cols[None, :]) % length).astype(jnp.float32) - phase
    table = jnp.cos(coarse)[:, None] * jnp.cos(fine)[None] - jnp.sin(coarse)[:, None] * jnp.sin(fine)[None]
    return table.reshape(length, length)


def paired_inverse(precond):
    length = precond.shape[2]
    half = length // 2
    low = precond[:, :, : half + 1]
    mirror = jnp.flip(precond[:, :, half + 1 :], axis=2)
    inner = jnp.concatenate([jnp.zeros_like(low[:, :, :1]), mirror, jnp.zeros_like(low[:, :, :1])], axis=2)
    paired = low + inner
    return jnp.concatenate([paired, paired[:, :, 1:half]], axis=2)


def with_halo(x, sides, width, wrap):
    for axis, dim in sides:
        size, length = (lax.axis_size(axis), x.shape[dim])
        up = [(i, (i + 1) % size) for i in range(size if wrap else size - 1)]
        down = [(j, i) for i, j in up]
        last = lax.slice_in_dim(x, length - width, length, axis=dim)
        first = lax.slice_in_dim(x, 0, width, axis=dim)
        before = lax.ppermute(last, axis, up)
        after = lax.ppermute(first, axis, down)
        x = jnp.concatenate([before, x, after], axis=dim)
    return x


def swap_channels(field):
    extent = field.shape
    folded = field.reshape((extent[0] // 2, 2) + extent[1:])
    return jnp.flip(folded, axis=1).reshape(extent)


def swap_radial(field):
    extent = field.shape
    folded = field.reshape(extent[0], extent[1] // 2, 2, extent[2])
    return jnp.flip(folded, axis=2).reshape(extent)


def apply_operator(field, stiffness):
    axial_pad = with_halo(field, (("ax", 0),), 1, False)
    sector_pad = with_halo(field, (("sec", 2),), 1, True)
    beside = axial_pad[2:] + axial_pad[:-2]
    beside = beside + sector_pad[:, :, 2:] + sector_pad[:, :, :-2]
    return (stiffness + 4.5) * field - beside - 0.5 * swap_radial(field)


def shards(load, disp, stiff, hole, section_class, class_table, precond):
    slab_count, comp_count, sector_width = disp.shape
    sector_count = lax.axis_size("sec")
    around_cells = sector_width * sector_count
    total_axial = slab_count * lax.axis_size("ax")
    position = lax.axis_index("ax") * slab_count + jnp.arange(slab_count)
    taper = 1.0 + 2.0 * position.astype(jnp.float32) / (total_axial - 1)
    one_hot = (section_class[:, None] == jnp.arange(class_table.shape[0])[None, :]).astype(
        jnp.float32
    )
    factors = jnp.dot(one_hot, class_table, precision=lax.Precision.HIGHEST)
    stiffness = stiff * (factors * taper[:, None])[:, :, None]
    solid = (1 - hole).astype(jnp.float32)[:, None, :]
    residual = solid * (load - apply_operator(disp, stiffness))
    residual_t = jnp.transpose(residual, (1, 0, 2))
    solid_t = jnp.transpose(solid, (1, 0, 2))
    lines, solid_lines = to_lines([residual_t, solid_t], sector_count)
    spectrum = lax.optimization_barrier(
        jnp.dot(
            lax.optimization_barrier(lines.reshape(-1, around_cells)),
            dft_table(around_cells),
            precision=lax.Precision.HIGH,
        )
    ).reshape(lines.shape)
    mixed = jnp.sum(paired_inverse(precond)[:, :, None] * spectrum[None], axis=1)
    smoothed_lines = lax.dot_general(
        mixed.reshape(-1, around_cells),
        dft_table(around_cells),
        (((1,), (1,)), ((), ())),
        precision=lax.Precision.HIGH,
    ) / around_cells
    prec_lines = solid_lines * smoothed_lines.reshape(lines.shape)
    group_rows = lines.shape[1]
    edge_at = [(p * sector_width - 1) % around_cells for p in range(sector_count)]
    edge_at += [((p + 1) * sector_width) % around_cells for p in range(sector_count)]
    pick = (jnp.arange(around_cells)[None, :] == jnp.array(edge_at)[:, None]).astype(jnp.float32)
    edges = lax.dot_general(
        pick,
        prec_lines.reshape(-1, around_cells),
        (((1,), (1,)), ((), ())),
        precision=lax.Precision.HIGHEST,
    ).reshape(2, sector_count, comp_count, group_rows)
    cpk = jnp.pad(
        jnp.transpose(edges, (1, 2, 0, 3)).reshape(sector_count, comp_count, 2 * group_rows),
        ((0, 0), (0, -(-comp_count // 8) * 8 - comp_count), (0, -(-2 * group_rows // 128) * 128 - 2 * group_rows)),
    )

    def row_pack(row):
        return jnp.transpose(row.reshape(comp_count, sector_count, sector_width), (1, 0, 2))

    prec_t, halo_cols, before_rows, after_rows = from_lines_with_halo(
        prec_lines, cpk, row_pack(prec_lines[:, -1]), row_pack(prec_lines[:, 0]), sector_count
    )
    stiffness_t = jnp.transpose(stiffness, (1, 0, 2))
    cell_total = slab_count * lax.axis_size("ax") * comp_count * around_cells
    finished, image_t = image_and_totals(
        residual_t, prec_t, stiffness_t, solid_t[0], before_rows, after_rows, halo_cols, cell_total, 0
    )
    disp_new_t, residual_new_t = apply_step(
        finished, jnp.transpose(disp, (1, 0, 2)), prec_t, residual_t, image_t
    )
    return (
        jnp.transpose(disp_new_t, (1, 0, 2)),
        jnp.transpose(residual_new_t, (1, 0, 2)),
        finished[0, 1:4],
    )


def solution(mesh):
    in_specs = (
        P("ax", None, "sec"),
        P("ax", None, "sec"),
        P("ax", None, "sec"),
        P("ax", "sec"),
        P("ax"),
        P(),
        P(),
    )
    out_specs = (P("ax", None, "sec"), P("ax", None, "sec"), P())
    return jax.shard_map(shards, mesh=mesh, in_specs=in_specs, out_specs=out_specs, check_vma=False)
```

```python
import functools
import math

import jax
import jax.numpy as jnp
from jax import lax
from jax.experimental import pallas as pl
from jax.experimental.pallas import tpu as pltpu
from jax.sharding import PartitionSpec as P


MESH = pl.DeviceIdType.MESH


def _groups():
    me_ax = lax.axis_index("ax")
    me_sec = lax.axis_index("sec")
    x = me_ax % 4
    z = (me_ax // 4) % 8
    ylo = me_ax // 32
    core = me_sec % 2
    yhi = me_sec // 2

    def plane_peer(c):
        y = c % 4
        return ((y % 2) * 32 + z * 4 + (c // 4) % 4, (y // 2) * 2 + c // 16)

    return [
        (32, (core * 4 + x) * 4 + yhi * 2 + ylo, plane_peer),
        (8, z, lambda c: (me_ax - z * 4 + c * 4, me_sec)),
    ]


def _image_and_sums(r_ref, p_ref, s_ref, m_ref, br_ref, ar_ref, hc_ref, img_ref):
    comps, rows, width = p_ref.shape
    ax = lax.axis_index("ax")
    first_slab = ax == 0
    last_slab = ax == lax.axis_size("ax") - 1

    def before_row(q):
        return jnp.where(first_slab, 0.0, br_ref[br_ref.shape[0] - 1, q : q + 1, :])

    def after_row(q):
        return jnp.where(last_slab, 0.0, ar_ref[0, q : q + 1, :])

    flipped = [hc_ref[g].T for g in range(hc_ref.shape[0])]
    part = rows // len(flipped)

    def column(w, q):
        pieces = [t[w * part : (w + 1) * part, q : q + 1] for t in flipped]
        return jnp.broadcast_to(jnp.concatenate(pieces, axis=0), (rows, width))

    row = lax.broadcasted_iota(jnp.int32, (rows, width), 0)
    lane = lax.broadcasted_iota(jnp.int32, (rows, width), 1)
    solid = m_ref[...]
    acc = [jnp.zeros((1, width), jnp.float32) for _ in range(5)]
    for q in range(comps):
        field = p_ref[q]
        up = jnp.where(row == 0, before_row(q), pltpu.roll(field, 1, 0))
        down = jnp.where(row == rows - 1, after_row(q), pltpu.roll(field, rows - 1, 0))
        left = jnp.where(lane == 0, column(0, q), pltpu.roll(field, 1, 1))
        right = jnp.where(lane == width - 1, column(1, q), pltpu.roll(field, width - 1, 1))
        beside = down + up + right + left
        image = solid * ((s_ref[q] + 4.5) * field - beside - 0.5 * p_ref[q ^ 1])
        img_ref[q] = image
        res = r_ref[q]
        for k, prod in enumerate((res * field, field * image, res * res, res * image, image * image)):
            acc[k] = acc[k] + jnp.sum(prod, axis=0, keepdims=True)
    lane8 = lax.broadcasted_iota(jnp.int32, (8, 128), 1)
    row8 = lax.broadcasted_iota(jnp.int32, (8, 128), 0)
    packed = jnp.zeros((8, 128), jnp.float32)
    for k, a in enumerate(acc):
        packed = jnp.where((row8 == 0) & (lane8 == k), jnp.sum(a), packed)
    return packed


def _finish(total, cell_total):
    lane = lax.broadcasted_iota(jnp.int32, total.shape, 1)
    row = lax.broadcasted_iota(jnp.int32, total.shape, 0)

    def pick(k):
        return jnp.sum(jnp.where((row == 0) & (lane == k), total, 0.0), keepdims=True)

    inner_rz = pick(0) / cell_total
    inner_zq = pick(1) / cell_total
    alpha = inner_rz / inner_zq
    square_new = (pick(2) - alpha * (2.0 * pick(3) - alpha * pick(4))) / cell_total
    out = jnp.zeros(total.shape, jnp.float32)
    for k, v in enumerate((alpha, inner_rz, inner_zq, square_new)):
        out = jnp.where((row == 0) & (lane == k), v, out)
    return out


def _ar_kernel(cell_total, r_ref, p_ref, s_ref, m_ref, br_ref, ar_ref, hc_ref, o_ref, img_ref, recv_a, recv_b, own, send_sems, recv_sems):
    recvs = (recv_a, recv_b)
    groups = _groups()
    for r in recvs:
        r[...] = jnp.zeros_like(r)
    barrier = pltpu.get_barrier_semaphore()
    count = 0
    for n, mine, dev in groups:
        for d in range(1, n):
            pl.semaphore_signal(barrier, inc=1, device_id=dev((mine + d) % n), device_id_type=MESH)
            count += 1
    own[0] = _image_and_sums(r_ref, p_ref, s_ref, m_ref, br_ref, ar_ref, hc_ref, img_ref)
    pl.semaphore_wait(barrier, count)
    base = 0
    for g, (n, mine, dev) in enumerate(groups):
        src = own.at[g]
        copies = []
        for d in range(1, n):
            cp = pltpu.make_async_remote_copy(
                src_ref=src,
                dst_ref=recvs[g].at[mine],
                send_sem=send_sems.at[base + d],
                recv_sem=recv_sems.at[base + d],
                device_id=dev((mine + d) % n),
                device_id_type=MESH,
            )
            cp.start()
            copies.append(cp)
        mine_val = src[...]
        for cp in copies:
            cp.wait_recv()
        total = None
        for c in range(n):
            v = jnp.where(mine == c, mine_val, recvs[g][c])
            total = v if total is None else total + v
        for cp in copies:
            cp.wait_send()
        base += n
        if g + 1 < len(groups):
            own[g + 1] = total
        else:
            finished = _finish(total, cell_total)
            o_ref[...] = finished


def image_and_totals(residual, prec, stiffness, solid, before_rows, after_rows, halo_cols, cell_total, cid):
    return pl.pallas_call(
        functools.partial(_ar_kernel, float(cell_total)),
        out_shape=[
            jax.ShapeDtypeStruct((8, 128), jnp.float32),
            jax.ShapeDtypeStruct(prec.shape, jnp.float32),
        ],
        in_specs=[pl.BlockSpec(memory_space=pltpu.VMEM)] * 7,
        out_specs=[pl.BlockSpec(memory_space=pltpu.VMEM)] * 2,
        scratch_shapes=[
            pltpu.VMEM((32, 8, 128), jnp.float32),
            pltpu.VMEM((8, 8, 128), jnp.float32),
            pltpu.VMEM((2, 8, 128), jnp.float32),
            pltpu.SemaphoreType.DMA((40,)),
            pltpu.SemaphoreType.DMA((40,)),
        ],
        compiler_params=pltpu.CompilerParams(collective_id=cid, has_side_effects=True),
    )(residual, prec, stiffness, solid, before_rows, after_rows, halo_cols)


def _update_kernel(f_ref, d_ref, p_ref, r_ref, i_ref, dn_ref, rn_ref):
    alpha = f_ref[0:1, 0:1]
    for q in range(d_ref.shape[0]):
        dn_ref[q] = d_ref[q] + alpha * p_ref[q]
        rn_ref[q] = r_ref[q] - alpha * i_ref[q]


def apply_step(finished, disp, prec, residual, image):
    comps, rows, width = prec.shape
    steps = 3 if comps % 3 == 0 else 1
    plane = pl.BlockSpec((comps // steps, rows, width), lambda q: (q, 0, 0))
    return pl.pallas_call(
        _update_kernel,
        grid=(steps,),
        out_shape=[jax.ShapeDtypeStruct(prec.shape, jnp.float32)] * 2,
        in_specs=[pl.BlockSpec((8, 128), lambda q: (0, 0))] + [plane] * 4,
        out_specs=[plane] * 2,
    )(finished, disp, prec, residual, image)


def _to_lines_kernel(n, count, *refs):
    x_refs, o_refs = refs[:count], refs[count : 2 * count]
    send_sems, recv_sems, local_sems = refs[2 * count :]
    me = lax.axis_index("sec")
    ax = lax.axis_index("ax")
    barrier = pltpu.get_barrier_semaphore()
    for d in range(1, n):
        pl.semaphore_signal(barrier, inc=1, device_id=(ax, (me + d) % n), device_id_type=MESH)
    pl.semaphore_wait(barrier, n - 1)
    copies, local = [], []
    for i, (x_ref, o_ref) in enumerate(zip(x_refs, o_refs)):
        rows, width = o_ref.shape[1], x_ref.shape[2]
        dst = o_ref.at[:, :, pl.ds(pl.multiple_of(me * width, width), width)]
        for d in range(1, n):
            peer = (me + d) % n
            cp = pltpu.make_async_remote_copy(
                src_ref=x_ref.at[:, pl.ds(pl.multiple_of(peer * rows, rows), rows), :],
                dst_ref=dst,
                send_sem=send_sems.at[i * n + d],
                recv_sem=recv_sems.at[i * n + d],
                device_id=(ax, peer),
                device_id_type=MESH,
            )
            cp.start()
            copies.append(cp)
        local.append(
            pltpu.make_async_copy(
                x_ref.at[:, pl.ds(pl.multiple_of(me * rows, rows), rows), :], dst, local_sems.at[i]
            )
        )
        local[-1].start()
    for cp in local:
        cp.wait()
    for cp in copies:
        cp.wait()


def to_lines(arrays, n):
    count = len(arrays)
    shapes = [(x.shape[0], x.shape[1] // n, x.shape[2] * n) for x in arrays]
    return pl.pallas_call(
        functools.partial(_to_lines_kernel, n, count),
        out_shape=[jax.ShapeDtypeStruct(s, x.dtype) for s, x in zip(shapes, arrays)],
        in_specs=[pl.BlockSpec(memory_space=pltpu.VMEM)] * count,
        out_specs=[pl.BlockSpec(memory_space=pltpu.VMEM)] * count,
        scratch_shapes=[
            pltpu.SemaphoreType.DMA((count * n,)),
            pltpu.SemaphoreType.DMA((count * n,)),
            pltpu.SemaphoreType.DMA((count,)),
        ],
        compiler_params=pltpu.CompilerParams(collective_id=1, has_side_effects=True),
    )(*arrays)


def _from_lines_kernel(sizes, x_ref, cpk_ref, last_ref, first_ref, o_ref, cols_ref, before_ref,
                       after_ref, send_sems, recv_sems, local_sems):
    n_ax, n = sizes
    me = lax.axis_index("sec")
    ax = lax.axis_index("ax")
    rows, width = x_ref.shape[1], o_ref.shape[2]
    up_ax, down_ax = (ax + 1) % n_ax, (ax + n_ax - 1) % n_ax
    peers = [(ax, (me + d) % n) for d in range(1, n)]
    peers += [(up_ax, s) for s in range(n)] + [(down_ax, s) for s in range(n)]
    barrier = pltpu.get_barrier_semaphore()
    for peer in peers:
        pl.semaphore_signal(barrier, inc=1, device_id=peer, device_id_type=MESH)
    pl.semaphore_wait(barrier, len(peers))
    dst = o_ref.at[:, pl.ds(pl.multiple_of(me * rows, rows), rows), :]
    sends, recvs = [], []
    for d in range(1, n):
        peer = (me + d) % n
        for k, (src, out) in enumerate(
            (
                (x_ref.at[:, :, pl.ds(pl.multiple_of(peer * width, width), width)], dst),
                (cpk_ref.at[peer], cols_ref.at[me]),
            )
        ):
            cp = pltpu.make_async_remote_copy(
                src_ref=src,
                dst_ref=out,
                send_sem=send_sems.at[k * n + d],
                recv_sem=recv_sems.at[k * n + d],
                device_id=(ax, peer),
                device_id_type=MESH,
            )
            cp.start()
            sends.append(cp)
        origin = (me + n - d) % n
        for k, (src, out) in enumerate(
            (
                (x_ref.at[:, :, pl.ds(0, width)], o_ref.at[:, pl.ds(pl.multiple_of(origin * rows, rows), rows), :]),
                (cpk_ref.at[0], cols_ref.at[origin]),
            )
        ):
            recvs.append(
                pltpu.make_async_remote_copy(
                    src_ref=src,
                    dst_ref=out,
                    send_sem=send_sems.at[k * n + d],
                    recv_sem=recv_sems.at[k * n + d],
                    device_id=(ax, origin),
                    device_id_type=MESH,
                )
            )
    for s in range(n):
        for k, (src, out, target) in enumerate(
            ((last_ref.at[s], before_ref.at[me], up_ax), (first_ref.at[s], after_ref.at[me], down_ax))
        ):
            base = (2 + k) * n
            cp = pltpu.make_async_remote_copy(
                src_ref=src,
                dst_ref=out,
                send_sem=send_sems.at[base + s],
                recv_sem=recv_sems.at[base + me],
                device_id=(target, s),
                device_id_type=MESH,
            )
            cp.start()
            sends.append(cp)
            recvs.append(
                pltpu.make_async_remote_copy(
                    src_ref=src,
                    dst_ref=(before_ref, after_ref)[k].at[s],
                    send_sem=send_sems.at[base + s],
                    recv_sem=recv_sems.at[base + s],
                    device_id=(target, s),
                    device_id_type=MESH,
                )
            )
    local = [
        pltpu.make_async_copy(
            x_ref.at[:, :, pl.ds(pl.multiple_of(me * width, width), width)], dst, local_sems.at[0]
        ),
        pltpu.make_async_copy(cpk_ref.at[me], cols_ref.at[me], local_sems.at[1]),
    ]
    for cp in local:
        cp.start()
    for cp in local:
        cp.wait()
    for cp in recvs:
        cp.wait_recv()
    for cp in sends:
        cp.wait_send()


def from_lines_with_halo(x, cpk, last, first, n):
    comps, rows, around = x.shape
    n_ax = lax.axis_size("ax")
    shapes = [
        (comps, rows * n, around // n),
        cpk.shape,
        (n,) + last.shape[1:],
        (n,) + first.shape[1:],
    ]
    return pl.pallas_call(
        functools.partial(_from_lines_kernel, (n_ax, n)),
        out_shape=[jax.ShapeDtypeStruct(s, x.dtype) for s in shapes],
        in_specs=[pl.BlockSpec(memory_space=pltpu.VMEM)] * 4,
        out_specs=[pl.BlockSpec(memory_space=pltpu.VMEM)] * 4,
        scratch_shapes=[
            pltpu.SemaphoreType.DMA((4 * n,)),
            pltpu.SemaphoreType.DMA((4 * n,)),
            pltpu.SemaphoreType.DMA((2,)),
        ],
        compiler_params=pltpu.CompilerParams(collective_id=2, has_side_effects=True),
    )(x, cpk, last, first)


def dft_table(length):
    half = length // 2
    root = int(round(math.sqrt(length)))
    cols = jnp.concatenate([jnp.arange(half + 1), jnp.arange(1, half)])
    phase = jnp.where(jnp.arange(length) > half, 0.5 * math.pi, 0.0).astype(jnp.float32)
    step = 2.0 * math.pi / length
    coarse = step * ((root * jnp.arange(length // root)[:, None] * cols[None, :]) % length).astype(jnp.float32)
    fine = step * ((jnp.arange(root)[:, None] * cols[None, :]) % length).astype(jnp.float32) - phase
    table = jnp.cos(coarse)[:, None] * jnp.cos(fine)[None] - jnp.sin(coarse)[:, None] * jnp.sin(fine)[None]
    return table.reshape(length, length)


def paired_inverse(precond):
    length = precond.shape[2]
    half = length // 2
    low = precond[:, :, : half + 1]
    mirror = jnp.flip(precond[:, :, half + 1 :], axis=2)
    inner = jnp.concatenate([jnp.zeros_like(low[:, :, :1]), mirror, jnp.zeros_like(low[:, :, :1])], axis=2)
    paired = low + inner
    return jnp.concatenate([paired, paired[:, :, 1:half]], axis=2)


def with_halo(x, sides, width, wrap):
    for axis, dim in sides:
        size, length = (lax.axis_size(axis), x.shape[dim])
        up = [(i, (i + 1) % size) for i in range(size if wrap else size - 1)]
        down = [(j, i) for i, j in up]
        last = lax.slice_in_dim(x, length - width, length, axis=dim)
        first = lax.slice_in_dim(x, 0, width, axis=dim)
        before = lax.ppermute(last, axis, up)
        after = lax.ppermute(first, axis, down)
        x = jnp.concatenate([before, x, after], axis=dim)
    return x


def swap_channels(field):
    extent = field.shape
    folded = field.reshape((extent[0] // 2, 2) + extent[1:])
    return jnp.flip(folded, axis=1).reshape(extent)


def swap_radial(field):
    extent = field.shape
    folded = field.reshape(extent[0], extent[1] // 2, 2, extent[2])
    return jnp.flip(folded, axis=2).reshape(extent)


def apply_operator(field, stiffness):
    axial_pad = with_halo(field, (("ax", 0),), 1, False)
    sector_pad = with_halo(field, (("sec", 2),), 1, True)
    beside = axial_pad[2:] + axial_pad[:-2]
    beside = beside + sector_pad[:, :, 2:] + sector_pad[:, :, :-2]
    return (stiffness + 4.5) * field - beside - 0.5 * swap_radial(field)


def shards(load, disp, stiff, hole, section_class, class_table, precond):
    slab_count, comp_count, sector_width = disp.shape
    sector_count = lax.axis_size("sec")
    around_cells = sector_width * sector_count
    total_axial = slab_count * lax.axis_size("ax")
    position = lax.axis_index("ax") * slab_count + jnp.arange(slab_count)
    taper = 1.0 + 2.0 * position.astype(jnp.float32) / (total_axial - 1)
    one_hot = (section_class[:, None] == jnp.arange(class_table.shape[0])[None, :]).astype(
        jnp.float32
    )
    factors = jnp.dot(one_hot, class_table, precision=lax.Precision.HIGHEST)
    stiffness = stiff * (factors * taper[:, None])[:, :, None]
    solid = (1 - hole).astype(jnp.float32)[:, None, :]
    residual = solid * (load - apply_operator(disp, stiffness))
    residual_t = jnp.transpose(residual, (1, 0, 2))
    solid_t = jnp.transpose(solid, (1, 0, 2))
    lines, solid_lines = to_lines([residual_t, solid_t], sector_count)
    spectrum = lax.optimization_barrier(
        jnp.dot(
            lax.optimization_barrier(lines.reshape(-1, around_cells)),
            dft_table(around_cells),
            precision=lax.Precision.HIGH,
        )
    ).reshape(lines.shape)
    mixed = jnp.sum(paired_inverse(precond)[:, :, None] * spectrum[None], axis=1)
    smoothed_lines = lax.dot_general(
        mixed.reshape(-1, around_cells),
        dft_table(around_cells),
        (((1,), (1,)), ((), ())),
        precision=lax.Precision.HIGH,
    ) / around_cells
    prec_lines = solid_lines * smoothed_lines.reshape(lines.shape)
    group_rows = lines.shape[1]
    edge_at = [(p * sector_width - 1) % around_cells for p in range(sector_count)]
    edge_at += [((p + 1) * sector_width) % around_cells for p in range(sector_count)]
    pick = (jnp.arange(around_cells)[None, :] == jnp.array(edge_at)[:, None]).astype(jnp.float32)
    edges = lax.dot_general(
        pick,
        prec_lines.reshape(-1, around_cells),
        (((1,), (1,)), ((), ())),
        precision=lax.Precision.HIGHEST,
    ).reshape(2, sector_count, comp_count, group_rows)
    cpk = jnp.pad(
        jnp.transpose(edges, (1, 2, 0, 3)).reshape(sector_count, comp_count, 2 * group_rows),
        ((0, 0), (0, -(-comp_count // 8) * 8 - comp_count), (0, -(-2 * group_rows // 128) * 128 - 2 * group_rows)),
    )

    def row_pack(row):
        return jnp.transpose(row.reshape(comp_count, sector_count, sector_width), (1, 0, 2))

    prec_t, halo_cols, before_rows, after_rows = from_lines_with_halo(
        prec_lines, cpk, row_pack(prec_lines[:, -1]), row_pack(prec_lines[:, 0]), sector_count
    )
    stiffness_t = jnp.transpose(stiffness, (1, 0, 2))
    cell_total = slab_count * lax.axis_size("ax") * comp_count * around_cells
    finished, image_t = image_and_totals(
        residual_t, prec_t, stiffness_t, solid_t[0], before_rows, after_rows, halo_cols, cell_total, 0
    )
    disp_new_t, residual_new_t = apply_step(
        finished, jnp.transpose(disp, (1, 0, 2)), prec_t, residual_t, image_t
    )
    return (
        jnp.transpose(disp_new_t, (1, 0, 2)),
        jnp.transpose(residual_new_t, (1, 0, 2)),
        finished[0, 1:4],
    )


def solution(mesh):
    in_specs = (
        P("ax", None, "sec"),
        P("ax", None, "sec"),
        P("ax", None, "sec"),
        P("ax", "sec"),
        P("ax"),
        P(),
        P(),
    )
    out_specs = (P("ax", None, "sec"), P("ax", None, "sec"), P())
    return jax.shard_map(shards, mesh=mesh, in_specs=in_specs, out_specs=out_specs, check_vma=False)
```

```python
import functools
import math

import jax
import jax.numpy as jnp
from jax import lax
from jax.experimental import pallas as pl
from jax.experimental.pallas import tpu as pltpu
from jax.sharding import PartitionSpec as P


MESH = pl.DeviceIdType.MESH


def _groups():
    me_ax = lax.axis_index("ax")
    me_sec = lax.axis_index("sec")
    x = me_ax % 4
    z = (me_ax // 4) % 8
    ylo = me_ax // 32
    core = me_sec % 2
    yhi = me_sec // 2

    def plane_peer(c):
        y = c % 4
        return ((y % 2) * 32 + z * 4 + (c // 4) % 4, (y // 2) * 2 + c // 16)

    return [
        (32, (core * 4 + x) * 4 + yhi * 2 + ylo, plane_peer),
        (8, z, lambda c: (me_ax - z * 4 + c * 4, me_sec)),
    ]


def _image_and_sums(r_ref, p_ref, s_ref, m_ref, br_ref, ar_ref, hc_ref, img_ref):
    comps, rows, width = p_ref.shape
    ax = lax.axis_index("ax")
    first_slab = ax == 0
    last_slab = ax == lax.axis_size("ax") - 1

    def before_row(q):
        return jnp.where(first_slab, 0.0, br_ref[br_ref.shape[0] - 1, q : q + 1, :])

    def after_row(q):
        return jnp.where(last_slab, 0.0, ar_ref[0, q : q + 1, :])

    flipped = [hc_ref[g].T for g in range(hc_ref.shape[0])]
    part = rows // len(flipped)

    def column(w, q):
        pieces = [t[w * part : (w + 1) * part, q : q + 1] for t in flipped]
        return jnp.broadcast_to(jnp.concatenate(pieces, axis=0), (rows, width))

    row = lax.broadcasted_iota(jnp.int32, (rows, width), 0)
    lane = lax.broadcasted_iota(jnp.int32, (rows, width), 1)
    solid = m_ref[...]
    acc = [jnp.zeros((1, width), jnp.float32) for _ in range(5)]
    for q in range(comps):
        field = p_ref[q]
        up = jnp.where(row == 0, before_row(q), pltpu.roll(field, 1, 0))
        down = jnp.where(row == rows - 1, after_row(q), pltpu.roll(field, rows - 1, 0))
        left = jnp.where(lane == 0, column(0, q), pltpu.roll(field, 1, 1))
        right = jnp.where(lane == width - 1, column(1, q), pltpu.roll(field, width - 1, 1))
        beside = down + up + right + left
        image = solid * ((s_ref[q] + 4.5) * field - beside - 0.5 * p_ref[q ^ 1])
        img_ref[q] = image
        res = r_ref[q]
        for k, prod in enumerate((res * field, field * image, res * res, res * image, image * image)):
            acc[k] = acc[k] + jnp.sum(prod, axis=0, keepdims=True)
    lane8 = lax.broadcasted_iota(jnp.int32, (8, 128), 1)
    row8 = lax.broadcasted_iota(jnp.int32, (8, 128), 0)
    packed = jnp.zeros((8, 128), jnp.float32)
    for k, a in enumerate(acc):
        packed = jnp.where((row8 == 0) & (lane8 == k), jnp.sum(a), packed)
    return packed


def _finish(total, cell_total):
    lane = lax.broadcasted_iota(jnp.int32, total.shape, 1)
    row = lax.broadcasted_iota(jnp.int32, total.shape, 0)

    def pick(k):
        return jnp.sum(jnp.where((row == 0) & (lane == k), total, 0.0), keepdims=True)

    inner_rz = pick(0) / cell_total
    inner_zq = pick(1) / cell_total
    alpha = inner_rz / inner_zq
    square_new = (pick(2) - alpha * (2.0 * pick(3) - alpha * pick(4))) / cell_total
    out = jnp.zeros(total.shape, jnp.float32)
    for k, v in enumerate((inner_rz, inner_zq, square_new, alpha)):
        out = jnp.where((row == 0) & (lane == k), v, out)
    return out


def _ar_kernel(cell_total, r_ref, p_ref, s_ref, m_ref, br_ref, ar_ref, hc_ref, o_ref, img_ref, recv_a, recv_b, own, send_sems, recv_sems):
    recvs = (recv_a, recv_b)
    groups = _groups()
    for r in recvs:
        r[...] = jnp.zeros_like(r)
    barrier = pltpu.get_barrier_semaphore()
    count = 0
    for n, mine, dev in groups:
        for d in range(1, n):
            pl.semaphore_signal(barrier, inc=1, device_id=dev((mine + d) % n), device_id_type=MESH)
            count += 1
    own[0] = _image_and_sums(r_ref, p_ref, s_ref, m_ref, br_ref, ar_ref, hc_ref, img_ref)
    pl.semaphore_wait(barrier, count)
    base = 0
    for g, (n, mine, dev) in enumerate(groups):
        src = own.at[g]
        copies = []
        for d in range(1, n):
            cp = pltpu.make_async_remote_copy(
                src_ref=src,
                dst_ref=recvs[g].at[mine],
                send_sem=send_sems.at[base + d],
                recv_sem=recv_sems.at[base + d],
                device_id=dev((mine + d) % n),
                device_id_type=MESH,
            )
            cp.start()
            copies.append(cp)
        mine_val = src[...]
        for cp in copies:
            cp.wait_recv()
        total = None
        for c in range(n):
            v = jnp.where(mine == c, mine_val, recvs[g][c])
            total = v if total is None else total + v
        for cp in copies:
            cp.wait_send()
        base += n
        if g + 1 < len(groups):
            own[g + 1] = total
        else:
            finished = _finish(total, cell_total)
            o_ref[...] = finished


def image_and_totals(residual, prec, stiffness, solid, before_rows, after_rows, halo_cols, cell_total, cid):
    return pl.pallas_call(
        functools.partial(_ar_kernel, float(cell_total)),
        out_shape=[
            jax.ShapeDtypeStruct((8, 128), jnp.float32),
            jax.ShapeDtypeStruct(prec.shape, jnp.float32),
        ],
        in_specs=[pl.BlockSpec(memory_space=pltpu.VMEM)] * 7,
        out_specs=[pl.BlockSpec(memory_space=pltpu.VMEM)] * 2,
        scratch_shapes=[
            pltpu.VMEM((32, 8, 128), jnp.float32),
            pltpu.VMEM((8, 8, 128), jnp.float32),
            pltpu.VMEM((2, 8, 128), jnp.float32),
            pltpu.SemaphoreType.DMA((40,)),
            pltpu.SemaphoreType.DMA((40,)),
        ],
        compiler_params=pltpu.CompilerParams(collective_id=cid, has_side_effects=True),
    )(residual, prec, stiffness, solid, before_rows, after_rows, halo_cols)


def _update_kernel(f_ref, d_ref, p_ref, r_ref, i_ref, dn_ref, rn_ref):
    alpha = f_ref[0:1, 3:4]
    for q in range(d_ref.shape[0]):
        dn_ref[q] = d_ref[q] + alpha * p_ref[q]
        rn_ref[q] = r_ref[q] - alpha * i_ref[q]


def apply_step(finished, disp, prec, residual, image):
    comps, rows, width = prec.shape
    steps = 2 if comps % 2 == 0 else 1
    plane = pl.BlockSpec((comps // steps, rows, width), lambda q: (q, 0, 0))
    return pl.pallas_call(
        _update_kernel,
        grid=(steps,),
        out_shape=[jax.ShapeDtypeStruct(prec.shape, jnp.float32)] * 2,
        in_specs=[pl.BlockSpec((8, 128), lambda q: (0, 0))] + [plane] * 4,
        out_specs=[plane] * 2,
    )(finished, disp, prec, residual, image)


def _to_lines_kernel(n, count, *refs):
    x_refs, o_refs = refs[:count], refs[count : 2 * count]
    send_sems, recv_sems, local_sems = refs[2 * count :]
    me = lax.axis_index("sec")
    ax = lax.axis_index("ax")
    barrier = pltpu.get_barrier_semaphore()
    for d in range(1, n):
        pl.semaphore_signal(barrier, inc=1, device_id=(ax, (me + d) % n), device_id_type=MESH)
    pl.semaphore_wait(barrier, n - 1)
    copies, local = [], []
    for i, (x_ref, o_ref) in enumerate(zip(x_refs, o_refs)):
        rows, width = o_ref.shape[1], x_ref.shape[2]
        dst = o_ref.at[:, :, pl.ds(pl.multiple_of(me * width, width), width)]
        for d in range(1, n):
            peer = (me + d) % n
            cp = pltpu.make_async_remote_copy(
                src_ref=x_ref.at[:, pl.ds(pl.multiple_of(peer * rows, rows), rows), :],
                dst_ref=dst,
                send_sem=send_sems.at[i * n + d],
                recv_sem=recv_sems.at[i * n + d],
                device_id=(ax, peer),
                device_id_type=MESH,
            )
            cp.start()
            copies.append(cp)
        local.append(
            pltpu.make_async_copy(
                x_ref.at[:, pl.ds(pl.multiple_of(me * rows, rows), rows), :], dst, local_sems.at[i]
            )
        )
        local[-1].start()
    for cp in local:
        cp.wait()
    for cp in copies:
        cp.wait()


def to_lines(arrays, n):
    count = len(arrays)
    shapes = [(x.shape[0], x.shape[1] // n, x.shape[2] * n) for x in arrays]
    return pl.pallas_call(
        functools.partial(_to_lines_kernel, n, count),
        out_shape=[jax.ShapeDtypeStruct(s, x.dtype) for s, x in zip(shapes, arrays)],
        in_specs=[pl.BlockSpec(memory_space=pltpu.VMEM)] * count,
        out_specs=[pl.BlockSpec(memory_space=pltpu.VMEM)] * count,
        scratch_shapes=[
            pltpu.SemaphoreType.DMA((count * n,)),
            pltpu.SemaphoreType.DMA((count * n,)),
            pltpu.SemaphoreType.DMA((count,)),
        ],
        compiler_params=pltpu.CompilerParams(collective_id=1, has_side_effects=True),
    )(*arrays)


def _from_lines_kernel(sizes, x_ref, cpk_ref, last_ref, first_ref, o_ref, cols_ref, before_ref,
                       after_ref, send_sems, recv_sems, local_sems):
    n_ax, n = sizes
    me = lax.axis_index("sec")
    ax = lax.axis_index("ax")
    rows, width = x_ref.shape[1], o_ref.shape[2]
    up_ax, down_ax = (ax + 1) % n_ax, (ax + n_ax - 1) % n_ax
    peers = [(ax, (me + d) % n) for d in range(1, n)]
    peers += [(up_ax, s) for s in range(n)] + [(down_ax, s) for s in range(n)]
    barrier = pltpu.get_barrier_semaphore()
    for peer in peers:
        pl.semaphore_signal(barrier, inc=1, device_id=peer, device_id_type=MESH)
    pl.semaphore_wait(barrier, len(peers))
    dst = o_ref.at[:, pl.ds(pl.multiple_of(me * rows, rows), rows), :]
    sends, recvs = [], []
    for d in range(1, n):
        peer = (me + d) % n
        for k, (src, out) in enumerate(
            (
                (x_ref.at[:, :, pl.ds(pl.multiple_of(peer * width, width), width)], dst),
                (cpk_ref.at[peer], cols_ref.at[me]),
            )
        ):
            cp = pltpu.make_async_remote_copy(
                src_ref=src,
                dst_ref=out,
                send_sem=send_sems.at[k * n + d],
                recv_sem=recv_sems.at[k * n + d],
                device_id=(ax, peer),
                device_id_type=MESH,
            )
            cp.start()
            sends.append(cp)
        origin = (me + n - d) % n
        for k, (src, out) in enumerate(
            (
                (x_ref.at[:, :, pl.ds(0, width)], o_ref.at[:, pl.ds(pl.multiple_of(origin * rows, rows), rows), :]),
                (cpk_ref.at[0], cols_ref.at[origin]),
            )
        ):
            recvs.append(
                pltpu.make_async_remote_copy(
                    src_ref=src,
                    dst_ref=out,
                    send_sem=send_sems.at[k * n + d],
                    recv_sem=recv_sems.at[k * n + d],
                    device_id=(ax, origin),
                    device_id_type=MESH,
                )
            )
    for s in range(n):
        for k, (src, out, target) in enumerate(
            ((last_ref.at[s], before_ref.at[me], up_ax), (first_ref.at[s], after_ref.at[me], down_ax))
        ):
            base = (2 + k) * n
            cp = pltpu.make_async_remote_copy(
                src_ref=src,
                dst_ref=out,
                send_sem=send_sems.at[base + s],
                recv_sem=recv_sems.at[base + me],
                device_id=(target, s),
                device_id_type=MESH,
            )
            cp.start()
            sends.append(cp)
            recvs.append(
                pltpu.make_async_remote_copy(
                    src_ref=src,
                    dst_ref=(before_ref, after_ref)[k].at[s],
                    send_sem=send_sems.at[base + s],
                    recv_sem=recv_sems.at[base + s],
                    device_id=(target, s),
                    device_id_type=MESH,
                )
            )
    local = [
        pltpu.make_async_copy(
            x_ref.at[:, :, pl.ds(pl.multiple_of(me * width, width), width)], dst, local_sems.at[0]
        ),
        pltpu.make_async_copy(cpk_ref.at[me], cols_ref.at[me], local_sems.at[1]),
    ]
    for cp in local:
        cp.start()
    for cp in local:
        cp.wait()
    for cp in recvs:
        cp.wait_recv()
    for cp in sends:
        cp.wait_send()


def from_lines_with_halo(x, cpk, last, first, n):
    comps, rows, around = x.shape
    n_ax = lax.axis_size("ax")
    shapes = [
        (comps, rows * n, around // n),
        cpk.shape,
        (n,) + last.shape[1:],
        (n,) + first.shape[1:],
    ]
    return pl.pallas_call(
        functools.partial(_from_lines_kernel, (n_ax, n)),
        out_shape=[jax.ShapeDtypeStruct(s, x.dtype) for s in shapes],
        in_specs=[pl.BlockSpec(memory_space=pltpu.VMEM)] * 4,
        out_specs=[pl.BlockSpec(memory_space=pltpu.VMEM)] * 4,
        scratch_shapes=[
            pltpu.SemaphoreType.DMA((4 * n,)),
            pltpu.SemaphoreType.DMA((4 * n,)),
            pltpu.SemaphoreType.DMA((2,)),
        ],
        compiler_params=pltpu.CompilerParams(collective_id=2, has_side_effects=True),
    )(x, cpk, last, first)


def dft_table(length):
    half = length // 2
    root = int(round(math.sqrt(length)))
    cols = jnp.concatenate([jnp.arange(half + 1), jnp.arange(1, half)])
    phase = jnp.where(jnp.arange(length) > half, 0.5 * math.pi, 0.0).astype(jnp.float32)
    step = 2.0 * math.pi / length
    coarse = step * ((root * jnp.arange(length // root)[:, None] * cols[None, :]) % length).astype(jnp.float32)
    fine = step * ((jnp.arange(root)[:, None] * cols[None, :]) % length).astype(jnp.float32) - phase
    table = jnp.cos(coarse)[:, None] * jnp.cos(fine)[None] - jnp.sin(coarse)[:, None] * jnp.sin(fine)[None]
    return table.reshape(length, length)


def paired_inverse(precond):
    length = precond.shape[2]
    half = length // 2
    low = precond[:, :, : half + 1]
    mirror = jnp.flip(precond[:, :, half + 1 :], axis=2)
    inner = jnp.concatenate([jnp.zeros_like(low[:, :, :1]), mirror, jnp.zeros_like(low[:, :, :1])], axis=2)
    paired = low + inner
    return jnp.concatenate([paired, paired[:, :, 1:half]], axis=2)


def with_halo(x, sides, width, wrap):
    for axis, dim in sides:
        size, length = (lax.axis_size(axis), x.shape[dim])
        up = [(i, (i + 1) % size) for i in range(size if wrap else size - 1)]
        down = [(j, i) for i, j in up]
        last = lax.slice_in_dim(x, length - width, length, axis=dim)
        first = lax.slice_in_dim(x, 0, width, axis=dim)
        before = lax.ppermute(last, axis, up)
        after = lax.ppermute(first, axis, down)
        x = jnp.concatenate([before, x, after], axis=dim)
    return x


def swap_channels(field):
    extent = field.shape
    folded = field.reshape((extent[0] // 2, 2) + extent[1:])
    return jnp.flip(folded, axis=1).reshape(extent)


def swap_radial(field):
    extent = field.shape
    folded = field.reshape(extent[0], extent[1] // 2, 2, extent[2])
    return jnp.flip(folded, axis=2).reshape(extent)


def apply_operator(field, stiffness):
    axial_pad = with_halo(field, (("ax", 0),), 1, False)
    sector_pad = with_halo(field, (("sec", 2),), 1, True)
    beside = axial_pad[2:] + axial_pad[:-2]
    beside = beside + sector_pad[:, :, 2:] + sector_pad[:, :, :-2]
    return (stiffness + 4.5) * field - beside - 0.5 * swap_radial(field)


def shards(load, disp, stiff, hole, section_class, class_table, precond):
    slab_count, comp_count, sector_width = disp.shape
    sector_count = lax.axis_size("sec")
    around_cells = sector_width * sector_count
    total_axial = slab_count * lax.axis_size("ax")
    position = lax.axis_index("ax") * slab_count + jnp.arange(slab_count)
    taper = 1.0 + 2.0 * position.astype(jnp.float32) / (total_axial - 1)
    one_hot = (section_class[:, None] == jnp.arange(class_table.shape[0])[None, :]).astype(
        jnp.float32
    )
    factors = jnp.dot(one_hot, class_table, precision=lax.Precision.HIGHEST)
    stiffness = stiff * (factors * taper[:, None])[:, :, None]
    solid = (1 - hole).astype(jnp.float32)[:, None, :]
    residual = solid * (load - apply_operator(disp, stiffness))
    residual_t = jnp.transpose(residual, (1, 0, 2))
    solid_t = jnp.transpose(solid, (1, 0, 2))
    lines, solid_lines = to_lines([residual_t, solid_t], sector_count)
    spectrum = lax.optimization_barrier(
        jnp.dot(
            lax.optimization_barrier(lines.reshape(-1, around_cells)),
            dft_table(around_cells),
            precision=lax.Precision.HIGH,
        )
    ).reshape(lines.shape)
    mixed = jnp.sum(paired_inverse(precond)[:, :, None] * spectrum[None], axis=1)
    smoothed_lines = lax.dot_general(
        mixed.reshape(-1, around_cells),
        dft_table(around_cells),
        (((1,), (1,)), ((), ())),
        precision=lax.Precision.HIGH,
    ) / around_cells
    prec_lines = solid_lines * smoothed_lines.reshape(lines.shape)
    group_rows = lines.shape[1]
    edge_at = [(p * sector_width - 1) % around_cells for p in range(sector_count)]
    edge_at += [((p + 1) * sector_width) % around_cells for p in range(sector_count)]
    pick = (jnp.arange(around_cells)[None, :] == jnp.array(edge_at)[:, None]).astype(jnp.float32)
    edges = lax.dot_general(
        pick,
        prec_lines.reshape(-1, around_cells),
        (((1,), (1,)), ((), ())),
        precision=lax.Precision.HIGHEST,
    ).reshape(2, sector_count, comp_count, group_rows)
    cpk = jnp.pad(
        jnp.transpose(edges, (1, 2, 0, 3)).reshape(sector_count, comp_count, 2 * group_rows),
        ((0, 0), (0, -(-comp_count // 8) * 8 - comp_count), (0, -(-2 * group_rows // 128) * 128 - 2 * group_rows)),
    )

    def row_pack(row):
        return jnp.transpose(row.reshape(comp_count, sector_count, sector_width), (1, 0, 2))

    prec_t, halo_cols, before_rows, after_rows = from_lines_with_halo(
        prec_lines, cpk, row_pack(prec_lines[:, -1]), row_pack(prec_lines[:, 0]), sector_count
    )
    stiffness_t = jnp.transpose(stiffness, (1, 0, 2))
    cell_total = slab_count * lax.axis_size("ax") * comp_count * around_cells
    finished, image_t = image_and_totals(
        residual_t, prec_t, stiffness_t, solid_t[0], before_rows, after_rows, halo_cols, cell_total, 0
    )
    disp_new_t, residual_new_t = apply_step(
        finished, jnp.transpose(disp, (1, 0, 2)), prec_t, residual_t, image_t
    )
    return (
        jnp.transpose(disp_new_t, (1, 0, 2)),
        jnp.transpose(residual_new_t, (1, 0, 2)),
        finished[0, 0:3],
    )


def solution(mesh):
    in_specs = (
        P("ax", None, "sec"),
        P("ax", None, "sec"),
        P("ax", None, "sec"),
        P("ax", "sec"),
        P("ax"),
        P(),
        P(),
    )
    out_specs = (P("ax", None, "sec"), P("ax", None, "sec"), P())
    return jax.shard_map(shards, mesh=mesh, in_specs=in_specs, out_specs=out_specs, check_vma=False)
```
